256 devices in a mesh: gx: 8 (over y, core), gy: 32 (over z, x).
Axes of the slice: x: 4, y: 4, z: 8, core: 2. Of those that a mesh axis runs over, the one named last changes fastest.
Arguments:
- reference_image: bfloat16 [64, 128, 4096], P(None, 'gx', 'gy'), may hold values from -8 to 8
- deformed_image: bfloat16 [64, 128, 4096], P(None, 'gx', 'gy'), may hold values from -8 to 8
- route: int32 [8, 32, 32, 1], P('gx', 'gy'), may hold values from 0 to 4; in each aligned block of 32 rows (0 to 31, 32 to 63, ..., all dimensions but the last counted through in order) at most 8 rows name the same one
- within: int32 [8, 32, 32], P('gx', 'gy'), may hold values from 0 to 7
- xshift: int32 [8, 32, 32], P('gx', 'gy'), may hold values from 0 to 2
- fractions: int32 [8, 32, 32, 3], P('gx', 'gy'), may hold values from 0 to 15
Outputs:
- increment: float32 [3, 5, 8, 256], P(None, None, 'gx', 'gy')
- mismatch: float32 [64, 128, 4096], P(None, 'gx', 'gy')
The draws below stay inside these ranges and needn't reach their ends.
Inputs may be any that keep to these rules, and one draw needn't show every extreme that they name: `route`: among the 32 rows of one device (aligned blocks of rows along the first three dimensions taken together) no value occurs more than 8 times, and some value occurs exactly 8 times.
All inputs are finite; a program needn't handle non-finite values.
Results may differ from the reference program's by a relative error of at most 0.0006.
Values may be sent and summed in bfloat16 or wider, within the bound.
A program may use at most 64 MiB of HBM per device.

```python
import math
import jax
import jax.numpy as jnp
import numpy as np
from jax import lax

EDGE = 16
EZ = 4
EXD = 1
EYD = 8
SPAN = 2
ITERS = 3
NEL = 32
CAP = 8
VOL = 4096
EX = 8
EY = 256
NZV = 64
NXV = 128
NYV = 4096
N_GX = 8
N_GY = 32


def wave_sum(key, amplitudes, periods):
    phases = jax.random.uniform(key, (3,), jnp.float32, 0.0, 2.0 * math.pi)
    depth_axis = jnp.arange(NZV, dtype=jnp.float32)[:, None, None]
    across = jnp.arange(NXV, dtype=jnp.float32)[None, :, None]
    height = jnp.arange(NYV, dtype=jnp.float32)[None, None, :]
    banding = amplitudes[0] * jnp.sin(2.0 * math.pi * depth_axis / periods[0] + phases[0])
    banding = banding + amplitudes[1] * jnp.sin(2.0 * math.pi * across / periods[1] + phases[1])
    return banding + amplitudes[2] * jnp.sin(2.0 * math.pi * height / periods[2] + phases[2])


def draw_reference_image(key, part):
    texture_key, phase_key = jax.random.split(jax.random.fold_in(key, 11))
    texture = jnp.clip(jax.random.normal(texture_key, (NZV, NXV, NYV), jnp.float32), -4.0, 4.0)
    banding = wave_sum(phase_key, (0.8, 1.2, 1.2), (24.0, 40.0, 56.0))
    return (texture + banding).astype(jnp.bfloat16)


def draw_deformed_image(key, part):
    texture_key, phase_key = jax.random.split(jax.random.fold_in(key, 23))
    texture = jnp.clip(jax.random.normal(texture_key, (NZV, NXV, NYV), jnp.float32), -4.0, 4.0)
    banding = wave_sum(phase_key, (0.6, 1.0, 1.5), (30.0, 52.0, 44.0))
    return (texture + banding).astype(jnp.bfloat16)


def plant(values, key, least, largest):
    spot = [jax.random.randint(jax.random.fold_in(key, axis), (), 0, length) for axis, length in enumerate(values.shape)]
    main_axis = values.shape.index(max(values.shape))
    beside = spot[:main_axis] + [(spot[main_axis] + 1) % values.shape[main_axis]] + spot[main_axis + 1:]
    return values.at[tuple(spot)].set(least).at[tuple(beside)].set(largest)


def routed_block(stream_key, own, number, rows, amount, top, most, slope):
    sequence = jax.random.permutation(stream_key, amount)
    heavy_load, common = shares(amount, rows * top, most, slope, True), shares(amount, rows * top, most, slope, False)
    places = jnp.arange(amount)

    def named(sizes, turn):
        used = int((sizes > 0).sum())
        fixed = max(1, used // 4)
        passed = fixed + (places - fixed + turn * (used - fixed)) % max(1, amount - fixed)
        return jnp.zeros((amount,), jnp.int32).at[sequence[jnp.where(places < fixed, places, passed)]].set(jnp.asarray(sizes, jnp.int32))

    sizes = jnp.where(number % 4 == 0, named(heavy_load, number // 4), named(common, number - number // 4 - 1))
    mixed = jax.random.permutation(jax.random.fold_in(own, 3), amount)
    source_of, taker = mixed[0:amount // 2 * 2:2], mixed[1:amount // 2 * 2:2]
    room = jnp.minimum(sizes[source_of] - 1, most - sizes[taker]) // 2
    room = jnp.where((source_of == sequence[0]) | (taker == sequence[0]) | (sizes[taker] == 0), 0, jnp.maximum(room, 0))
    passed = jax.random.randint(jax.random.fold_in(own, 4), (amount // 2,), 0, 1 << 20) % (room + 1)
    sizes = sizes.at[source_of].add(-passed).at[taker].add(passed)
    members = jnp.searchsorted(jnp.cumsum(sizes), jnp.arange(rows * top), side="right").astype(jnp.int32)
    grid = members.reshape(top, rows).T
    grid = grid[jax.random.permutation(jax.random.fold_in(own, 1), rows)]
    turn = jax.random.randint(jax.random.fold_in(own, 2), (rows, 1), 0, top)
    return jnp.take_along_axis(grid, (jnp.arange(top)[None, :] + turn) % top, axis=1)


def shares(count, total, most, skew, full):
    weights = [(1 << 20) // math.isqrt(standing ** skew) + 1 for standing in range(1, count + 1)]
    largest = most if full else min(most, max(-(-total // count), total * weights[0] // sum(weights)))
    least = 1 if total - largest >= count - 1 else 0
    given, surplus = [largest] + [least] * (count - 1), total - largest - least * (count - 1)
    while surplus > 0:
        candidates = [i for i in range(1, count) if given[i] < largest] or [i for i in range(1, count) if given[i] < most]
        whole, left = sum([weights[i] for i in candidates]), surplus
        for i in candidates:
            more = min(most - given[i], max(1, left * weights[i] // whole), surplus)
            given[i] = given[i] + more
            surplus = surplus - more
    return np.array(given)


def setup_inputs(seed: int = 0) -> dict:
    key_list = jax.random.split(jax.random.key(seed), 7)
    reference_image = draw_reference_image(jax.random.fold_in(key_list[6], 71), 0)
    deformed_image = draw_deformed_image(jax.random.fold_in(key_list[6], 71), 0)
    route_keys = jax.random.split(jax.random.fold_in(key_list[2], 1), N_GX * N_GY * NEL // NEL)
    route_turns = jax.random.permutation(jax.random.fold_in(key_list[2], 3), N_GX * N_GY * NEL // NEL)
    route = jax.vmap(lambda own, number: routed_block(jax.random.fold_in(key_list[2], 2), own, number, NEL, 2 * SPAN + 1, 1, CAP, 2))(route_keys, route_turns).reshape((N_GX, N_GY, NEL, 1))
    within = plant(jax.random.randint(key_list[3], (N_GX, N_GY, NEL), 0, EYD), jax.random.fold_in(key_list[3], 1), 0, EYD - 1).astype(jnp.int32)
    xshift = plant(jax.random.randint(key_list[4], (N_GX, N_GY, NEL), 0, 3), jax.random.fold_in(key_list[4], 1), 0, 2).astype(jnp.int32)
    fractions = plant(jax.random.randint(key_list[5], (N_GX, N_GY, NEL, 3), 0, EDGE), jax.random.fold_in(key_list[5], 1), 0, EDGE - 1).astype(jnp.int32)
    return dict(reference_image=reference_image, deformed_image=deformed_image, route=route, within=within, xshift=xshift, fractions=fractions)


LAMBDA = 0.05


def hat_positions(brick_edge, trailing):
    positions = (jnp.arange(brick_edge, dtype=jnp.float32) + 0.5) / brick_edge
    return positions.reshape((brick_edge,) + (1,) * trailing)


def spread_along(node_values, which_axis, brick_edge):
    node_count = node_values.shape[which_axis] - 1
    positions = hat_positions(brick_edge, node_values.ndim - which_axis - 1)
    lower_part = jnp.expand_dims(lax.slice_in_dim(node_values, 0, node_count, axis=which_axis), which_axis + 1)
    upper_part = jnp.expand_dims(lax.slice_in_dim(node_values, 1, node_count + 1, axis=which_axis), which_axis + 1)
    blended = lower_part * (1.0 - positions) + upper_part * positions
    new_shape = node_values.shape[:which_axis] + (node_count * brick_edge,) + node_values.shape[which_axis + 1:]
    return blended.reshape(new_shape)


def collect_along(voxel_values, which_axis, brick_edge):
    node_count = voxel_values.shape[which_axis] // brick_edge
    positions = hat_positions(brick_edge, voxel_values.ndim - which_axis - 1)
    blocks = voxel_values.reshape(voxel_values.shape[:which_axis] + (node_count, brick_edge) + voxel_values.shape[which_axis + 1:])
    lower_part = jnp.sum(blocks * (1.0 - positions), axis=which_axis + 1)
    upper_part = jnp.sum(blocks * positions, axis=which_axis + 1)
    zero_cap = jnp.zeros_like(lax.slice_in_dim(lower_part, 0, 1, axis=which_axis))
    return jnp.concatenate([lower_part, zero_cap], which_axis) + jnp.concatenate([zero_cap, upper_part], which_axis)


def clamp_shift(bricks, stride):
    advanced = jnp.concatenate([bricks[:, stride:], bricks[:, -stride:]], axis=1)
    places = jnp.arange(bricks.shape[1], dtype=jnp.int32)
    at_rim = (places // stride) % EDGE == EDGE - 1
    return jnp.where(at_rim[None, :], bricks, advanced)


def warp_bricks(bricks, fractions):
    weights = fractions.astype(jnp.float32) / EDGE
    blended = bricks
    for column, stride in ((2, 1), (1, EDGE), (0, EDGE * EDGE)):
        portion = weights[:, column:column + 1]
        blended = (1.0 - portion) * blended + portion * clamp_shift(blended, stride)
    return blended


def element_grid(values):
    trailing = values.shape[3:]
    shaped = values.reshape((N_GX, N_GY, EZ, EXD, EYD) + trailing)
    permuted_axes = (2, 0, 3, 1, 4) + tuple(range(5, 5 + len(trailing)))
    return shaped.transpose(permuted_axes).reshape((EZ, EX, EY) + trailing)


def brick_rows(image):
    shaped = image.reshape(EZ, EDGE, EX, EDGE, EY, EDGE)
    return shaped.transpose(0, 2, 4, 1, 3, 5).reshape(EZ, EX * EY, VOL)


def voxel_field(rows):
    shaped = rows.reshape(EZ, EX, EY, EDGE, EDGE, EDGE)
    return shaped.transpose(0, 3, 1, 4, 2, 5).reshape(NZV, NXV, NYV)


def compute_mismatch(reference_image, deformed_image, route, within, xshift, fractions):
    route_grid = element_grid(route)[..., 0]
    within_grid = element_grid(within)
    xshift_grid = element_grid(xshift)
    fraction_grid = element_grid(fractions).reshape(EZ, EX * EY, 3)
    column_x = jnp.arange(EX, dtype=jnp.int32)[:, None]
    column_y = jnp.arange(EY, dtype=jnp.int32)[None, :]
    source_x = jnp.clip(column_x + xshift_grid - 1, 0, EX - 1)
    source_y = ((column_y // EYD + route_grid - SPAN) % N_GY) * EYD + within_grid
    source_row = (source_x * EY + source_y).reshape(EZ, EX * EY).astype(jnp.int32)
    deformed_rows = brick_rows(deformed_image)
    reference_rows = brick_rows(reference_image)

    def slab_rows(inputs):
        rows_deformed, rows_reference, wanted, weights = inputs
        fetched = jnp.take(rows_deformed, wanted, axis=0)
        warped = warp_bricks(fetched.astype(jnp.float32), weights)
        return rows_reference.astype(jnp.float32) - warped

    mismatch_rows = lax.map(slab_rows, (deformed_rows, reference_rows, source_row, fraction_grid))
    return voxel_field(mismatch_rows)


def plane_gradient(padded, depth_index):
    slab = lax.dynamic_slice_in_dim(padded, depth_index, 3, 0).astype(jnp.float32)
    middle = slab[1]
    along_z = (slab[2] - slab[0])[1:-1, 1:-1] * 0.5
    along_x = (middle[2:, 1:-1] - middle[:-2, 1:-1]) * 0.5
    along_y = (middle[1:-1, 2:] - middle[1:-1, :-2]) * 0.5
    rounded = lax.optimization_barrier(jnp.stack([along_z, along_x, along_y]).astype(jnp.bfloat16))
    return rounded.astype(jnp.float32)


def layer_weights(depth_index):
    layer_index = depth_index // EDGE
    height = ((depth_index % EDGE).astype(jnp.float32) + 0.5) / EDGE
    levels = jnp.arange(EZ + 1, dtype=jnp.int32)
    return jnp.where(levels == layer_index, 1.0 - height, 0.0) + jnp.where(levels == layer_index + 1, height, 0.0)


def restrict_planes(padded, plane_terms):
    def visit_plane(running_total, depth_index):
        gradient = plane_gradient(padded, depth_index)
        voxel_terms = plane_terms(depth_index, gradient)
        plane_nodes = collect_along(collect_along(voxel_terms, 2, EDGE), 1, EDGE)
        weights = layer_weights(depth_index)
        return running_total + weights[None, :, None, None] * plane_nodes[:, None], None

    zero_nodes = jnp.zeros((3, EZ + 1, EX + 1, EY + 1), jnp.float32)
    running_total = lax.scan(visit_plane, zero_nodes, jnp.arange(NZV, dtype=jnp.int32))[0]
    return running_total[:, :, :EX, :EY] / VOL


def apply_hessian(unknown, padded):
    node_values = jnp.pad(unknown, ((0, 0), (0, 0), (0, 1), (0, 1)))

    def plane_terms(depth_index, gradient):
        weights = layer_weights(depth_index)
        plane_nodes = jnp.sum(weights[None, :, None, None] * node_values, axis=1)
        displaced = spread_along(spread_along(plane_nodes, 2, EDGE), 1, EDGE)
        normal_part = jnp.sum(gradient * displaced, axis=0)
        return gradient * normal_part

    return restrict_planes(padded, plane_terms) + LAMBDA * unknown


def reference(reference_image, deformed_image, route, within, xshift, fractions):
    mismatch = compute_mismatch(reference_image, deformed_image, route, within, xshift, fractions)
    padded = jnp.pad(reference_image, 1)

    def source_terms(depth_index, gradient):
        plane = lax.dynamic_index_in_dim(mismatch, depth_index, 0, keepdims=False)
        return gradient * plane[None]

    residual = restrict_planes(padded, source_terms)
    increment = jnp.zeros_like(residual)
    direction = residual
    norm_now = jnp.sum(residual * residual)
    for iteration in range(ITERS):
        curved = apply_hessian(direction, padded)
        step_size = norm_now / jnp.sum(direction * curved)
        increment = increment + step_size * direction
        residual = residual - step_size * curved
        norm_next = jnp.sum(residual * residual)
        direction = residual + (norm_next / norm_now) * direction
        norm_now = norm_next
    return increment, mismatch
```

```python
import jax
import jax.numpy as jnp
from jax import lax
from jax.experimental import pallas as pl
from jax.experimental.pallas import tpu as pltpu
from jax.sharding import PartitionSpec as P

EDGE = 16
EZ = 4
EYD = 8
SPAN = 2
ROUTES = 2 * SPAN + 1
NEL = 32
CAP = 8
VOL = 4096
NZ = 64
NY = 128
LAMBDA = 0.05
MESH = pl.DeviceIdType.MESH
F32 = jnp.float32
BF16 = jnp.bfloat16
EXACT = lax.Precision.HIGHEST

N_TABLE, N_BLOCK, N_FACE_X, N_FACE_Y, N_PACK, N_STENCIL, N_RHS, N_VEC = 4, 2, 2, 2, 4, 3, 11, 8
A_TABLE = 0
A_BLOCK = A_TABLE + N_TABLE
A_FACE_X = A_BLOCK + N_BLOCK
A_FACE_Y = A_FACE_X + N_FACE_X
A_PACK = A_FACE_Y + N_FACE_Y
A_STENCIL = A_PACK + N_PACK
A_RHS = A_STENCIL + N_STENCIL
A_VEC = A_RHS + N_RHS
A_END = A_VEC + 2 * N_VEC

OTHER_ROUTES = (1, 3, 0, 4)
RHS_OFFSETS = [(dp, dq) for dp in (-1, 0, 1, 2) for dq in (-1, 0, 1) if (dp, dq) != (0, 0)]
VEC_OFFSETS = [(dp, dq) for dp in (-1, 0, 1) for dq in (-1, 0, 1) if (dp, dq) != (0, 0)]
PAIRS = ((0, 0), (1, 1), (2, 2), (0, 1), (0, 2), (1, 2))


def iota(shape, dim):
    return lax.broadcasted_iota(jnp.int32, shape, dim)


def flag(condition):
    return jnp.where(condition, jnp.float32(1.0), jnp.float32(0.0))


def rolled(value, shift, axis):
    size = value.shape[axis]
    shift = shift % size
    return value if shift == 0 else pltpu.roll(value, shift, axis)


def hats(position):
    upper = (position.astype(F32) + 0.5) / EDGE
    return 1.0 - upper, upper


def kernel(
    nx, ny, route, within, xshift, fractions, ref, dfm, inc, mis,
    xb, tsend, trecv, fxs, fxr, fys, fyr, pmat, pacc, psend, precv, qmat, grad, refp, xrow, ss, sx, sy, sxy,
    kk, rrow, rs, rr, vs, vr, gs, gr, hs, hr, ssem, rsem, gssem, grsem, hssem, hrsem,
):
    p, q = lax.axis_index("gx"), lax.axis_index("gy")

    def at(dp, dq):
        return (lax.rem(p + dp + 2 * nx, nx), lax.rem(q + dq + 2 * ny, ny))

    def copy(src, dst, send_sem, recv_sem, dp, dq):
        c = pltpu.make_async_remote_copy(
            src_ref=src, dst_ref=dst, send_sem=send_sem, recv_sem=recv_sem,
            device_id=at(dp, dq), device_id_type=MESH,
        )
        c.start()
        return c

    started = []

    def send(number, src, dst, dp, dq):
        c = copy(src, dst, ssem.at[number], rsem.at[number], dp, dq)
        started.append(c)
        return c

    barrier = pltpu.get_barrier_semaphore()
    signals = 0
    for k in range(1, nx):
        pl.semaphore_signal(barrier, inc=1, device_id=at(k, 0), device_id_type=MESH)
        signals += 1
    for k in range(1, ny):
        pl.semaphore_signal(barrier, inc=1, device_id=at(0, k), device_id_type=MESH)
        signals += 1
    for dp in (-2, -1, 1, 2):
        for dq in (-1, 1):
            pl.semaphore_signal(barrier, inc=1, device_id=at(dp, dq), device_id_type=MESH)
            signals += 1

    lane, sub = iota((8, NY), 1), iota((8, NY), 0)
    block, inner = lane >> 4, lane & 15

    routes = [route[0, 0, e, 0] for e in range(NEL)]
    wanted = jnp.full((8, NY), -1, jnp.int32)
    count = jnp.zeros((8, NY), jnp.int32)
    for e in range(NEL):
        source = jnp.clip(p + xshift[0, 0, e] - 1, 0, nx - 1) - p + 1
        code = ((source * EZ + e // EYD) * EYD + within[0, 0, e]) * EDGE
        hit = sub == routes[e]
        wanted = jnp.where(hit & (count == block), inner + code, wanted)
        count = count + jnp.where(hit, 1, 0)
    tsend[...] = wanted
    pl.semaphore_wait(barrier, signals)
    tables = [
        send(A_TABLE + k, tsend, trecv.at[k], 0, r - SPAN) for k, r in enumerate(OTHER_ROUTES)
    ]
    blocks = [send(A_BLOCK, dfm, xb.at[1], -1, 0), send(A_BLOCK + 1, dfm, xb.at[0], 1, 0)]

    refp[0] = jnp.zeros((32, NY), F32)
    refp[NZ + 1] = jnp.zeros((32, NY), F32)
    refp[1 : NZ + 1, 8:24, :] = ref[...].astype(F32)
    fxs[0] = refp[1 : NZ + 1, 8, :].astype(BF16)
    fxs[1] = refp[1 : NZ + 1, 23, :].astype(BF16)
    faces_x = [
        send(A_FACE_X, fxs.at[0], fxr.at[1], -1, 0),
        send(A_FACE_X + 1, fxs.at[1], fxr.at[0], 1, 0),
    ]
    rows16, lanes16 = iota((16, NY), 0), iota((16, NY), 1)
    pick = ((rows16 == 0) & (lanes16 == 0)) | ((rows16 == 1) & (lanes16 == NY - 1))
    fys[...] = lax.dot_general(
        jnp.where(pick, 1.0, 0.0).astype(BF16), ref[...].reshape(NZ * EDGE, NY),
        (((1,), (1,)), ((), ())), preferred_element_type=F32,
    ).astype(BF16)
    faces_y = [
        send(A_FACE_Y, fys, fyr.at[1], 0, -1),
        send(A_FACE_Y + 1, fys, fyr.at[0], 0, 1),
    ]

    element = sub * EYD + block
    own_route = jnp.zeros((8, NY), jnp.int32)
    parts = [jnp.zeros((8, NY), jnp.int32) for _ in range(3)]
    for e in range(NEL):
        here = element == e
        own_route = jnp.where(here, routes[e], own_route)
        parts = [jnp.where(here, fractions[0, 0, e, c], parts[c]) for c in range(3)]
    slot = jnp.zeros((8, NY), jnp.int32)
    for e in range(NEL):
        slot = slot + jnp.where((element > e) & (own_route == routes[e]), 1, 0)
    first = (own_route * CAP + slot) * EDGE
    portion = [part.astype(F32) / EDGE for part in parts]
    target0 = first + inner
    target1 = first + jnp.minimum(inner + 1, EDGE - 1)

    for c in tables:
        c.wait_recv()
    asked = []
    for r in range(ROUTES):
        if r == SPAN:
            asked.append(wanted[r : r + 1])
        else:
            k = OTHER_ROUTES.index(r)
            asked.append(trecv[k, r : r + 1, :])
    asked = jnp.concatenate(asked, axis=1)

    def fill_pack(b, _):
        row = b * NY + iota((NY, ROUTES * NY), 0)
        pmat[pl.ds(pl.multiple_of(b * NY, NY), NY), :] = jnp.where(row == asked, 1.0, 0.0).astype(BF16)
        return 0

    lax.fori_loop(0, 3 * EZ, fill_pack, 0)

    def brick_rows(source):
        return jnp.concatenate(
            [source[z * EDGE : (z + 1) * EDGE].reshape(EDGE * EDGE, NY) for z in range(EZ)], axis=1
        )

    width = EZ * NY
    pacc[...] = jnp.dot(brick_rows(dfm), pmat[width : 2 * width, :], preferred_element_type=F32)
    blocks[1].wait_recv()
    pacc[...] += jnp.dot(brick_rows(xb[0]), pmat[0:width, :], preferred_element_type=F32)
    blocks[0].wait_recv()
    pacc[...] += jnp.dot(brick_rows(xb[1]), pmat[2 * width : 3 * width, :], preferred_element_type=F32)
    packs = []
    for k, r in enumerate(OTHER_ROUTES):
        psend[k] = pacc[:, r * NY : (r + 1) * NY].astype(BF16)
        packs.append(send(A_PACK + k, psend.at[k], precv.at[r], 0, SPAN - r))
    precv[SPAN] = pacc[:, SPAN * NY : (SPAN + 1) * NY].astype(BF16)

    for c in faces_x + faces_y:
        c.wait_recv()
    refp[1 : NZ + 1, 7, :] = fxr[0].astype(F32) * flag(p > 0)
    refp[1 : NZ + 1, 24, :] = fxr[1].astype(F32) * flag(p < nx - 1)
    here, there = iota((NY, NY), 1), iota((NY, NY), 0)
    differ = jnp.where(there == here + 1, 0.5, jnp.where(there == here - 1, -0.5, 0.0)).astype(BF16)
    rows32, lanes32 = iota((32, NY), 0), iota((32, NY), 1)
    ends = jnp.where(
        (rows32 == 1) & (lanes32 == 0), flag(q > 0) * -0.5,
        jnp.where((rows32 == 16) & (lanes32 == NY - 1), flag(q < ny - 1) * 0.5, 0.0),
    ).astype(BF16)
    sides = jnp.concatenate([fyr[0], fyr[1]], axis=0)
    along_y = jnp.dot(ref[...].reshape(NZ * EDGE, NY), differ, preferred_element_type=F32)
    along_y = along_y + lax.dot_general(sides, ends, (((0,), (0,)), ((), ())), preferred_element_type=F32)
    grad[2] = along_y.astype(BF16).reshape(NZ, EDGE, NY)

    def slope(b, _):
        base = b * 4
        below, above = refp[pl.ds(base, 4), 8:24, :], refp[pl.ds(base + 2, 4), 8:24, :]
        grad[0, pl.ds(base, 4)] = ((above - below) * 0.5).astype(BF16)
        left, right = refp[pl.ds(base + 1, 4), 7:23, :], refp[pl.ds(base + 1, 4), 9:25, :]
        grad[1, pl.ds(base, 4)] = ((right - left) * 0.5).astype(BF16)
        return 0

    lax.fori_loop(0, NZ // 4, slope, 0)

    rowm, colm = iota((24, 96), 0), iota((24, 96), 1)
    low_x, high_x = hats(colm & 15)
    order = rowm >> 3
    weight_x = jnp.where(order == 0, low_x * low_x, jnp.where(order == 1, low_x * high_x, high_x * high_x))
    weight_x = jnp.where((rowm & 7) == (colm >> 4), weight_x, 0.0)

    def moments(z, _):
        total = [[None] * 6 for _ in range(3)]
        for i in range(EDGE):
            g = [grad[c, z * EDGE + i].astype(F32) for c in range(3)]
            high = (i + 0.5) / EDGE
            low = 1.0 - high
            for k, (a, b) in enumerate(PAIRS):
                product = g[a] * g[b]
                for m, weight in enumerate((low * low, low * high, high * high)):
                    term = product * weight
                    total[m][k] = term if i == 0 else total[m][k] + term
        for m in range(3):
            rows = jnp.dot(weight_x, jnp.concatenate(total[m], axis=0), precision=EXACT, preferred_element_type=F32)
            xrow[pl.ds(pl.multiple_of((z * 3 + m) * 24, 24), 24), :] = rows
        return 0

    lax.fori_loop(0, EZ, moments, 0)
    fine, coarse = iota((NY, 3 * NY), 0), iota((NY, 3 * NY), 1)
    low_y, high_y = hats(fine & 15)
    row_y, node_y, step_y = fine >> 4, (coarse & 15) - 4, (coarse >> 7) - 1
    starts, closes = row_y == node_y, row_y + 1 == node_y
    mixed = low_y * high_y
    weight_y = jnp.where(
        step_y == 1, jnp.where(starts, mixed, 0.0),
        jnp.where(
            step_y == -1, jnp.where(closes, mixed, 0.0),
            jnp.where(starts, low_y * low_y, 0.0) + jnp.where(closes, high_y * high_y, 0.0),
        ),
    ) * (1.0 / VOL)
    yrow = jnp.dot(xrow[...], weight_y, precision=EXACT, preferred_element_type=F32)
    on = [block == z for z in range(EZ + 1)]
    for m in range(3):
        for dy in range(3):
            def term(z, depth):
                start = (z * 3 + depth) * 24 + m * 8
                return yrow[start : start + 8, dy * NY : (dy + 1) * NY]

            zero = jnp.zeros((8, NY), F32)
            down, same, up = zero, zero, zero
            for z in range(EZ):
                cross = term(z, 1)
                up = jnp.where(on[z], cross, up)
                down = jnp.where(on[z + 1], cross, down)
                same = same + jnp.where(on[z], term(z, 0), 0.0) + jnp.where(on[z + 1], term(z, 2), 0.0)
            ss[m, dy], ss[m, 3 + dy], ss[m, 6 + dy] = down, same, up
    stencils = [
        send(A_STENCIL, ss.at[1:3], sx, 1, 0),
        send(A_STENCIL + 1, ss, sy, 0, 1),
        send(A_STENCIL + 2, ss.at[1:3], sxy, 1, 1),
    ]

    for z in range(EZ):
        def fill_place(b, _):
            row = b * NY + iota((NY, NY), 0)
            high = portion[2][z : z + 1]
            place = jnp.where(row == target0[z : z + 1], 1.0 - high, 0.0)
            place = place + jnp.where(row == target1[z : z + 1], high, 0.0)
            qmat[pl.ds(pl.multiple_of(b * NY, NY), NY), z * NY : (z + 1) * NY] = place.astype(BF16)
            return 0

        lax.fori_loop(0, ROUTES, fill_place, 0)

    column = inner - 4
    own = (column >= 0) & (column < EYD) & (block <= EZ)
    has_x, has_y = flag(p > 0), flag(q > 0)
    for c in stencils:
        c.wait_recv()

    def fold(from_y):
        return jnp.where(inner < 8, rolled(from_y, -8, 1), 0.0) * has_y

    for t in range(9):
        here0 = ss[0, t] + fold(sy[0, t])
        here1 = ss[1, t] + fold(sy[1, t])
        back1 = (sx[0, t] + fold(sxy[0, t])) * has_x
        back2 = (sx[1, t] + fold(sxy[1, t])) * has_x
        kk[0, t] = jnp.where(own, back1, 0.0)
        kk[1, t] = jnp.where(own, here0 + back2, 0.0)
        kk[2, t] = jnp.where(own, here1, 0.0)

    for c in packs:
        c.wait_recv()
    taken = jnp.concatenate([precv[r] for r in range(ROUTES)], axis=1)
    fetched = jnp.dot(taken, qmat[...], preferred_element_type=F32)
    row8, col16 = iota((8, EDGE), 0), iota((8, EDGE), 1)
    low_j, high_j = hats(iota((EDGE, 1), 0))
    for z in range(EZ):
        voxels = fetched[:, z * NY : (z + 1) * NY].reshape(EDGE, EDGE, NY)
        high = portion[1][z : z + 1].reshape(1, 1, NY)
        ahead = jnp.concatenate([voxels[:, 1:], voxels[:, EDGE - 1 :]], axis=1)
        voxels = (1.0 - high) * voxels + high * ahead
        high = portion[0][z : z + 1].reshape(1, 1, NY)
        ahead = jnp.concatenate([voxels[1:], voxels[EDGE - 1 :]], axis=0)
        voxels = (1.0 - high) * voxels + high * ahead
        left = refp[1 + z * EDGE : 1 + (z + 1) * EDGE, 8:24, :] - voxels
        mis[z * EDGE : (z + 1) * EDGE] = left
        sums = [[None] * 3 for _ in range(2)]
        for i in range(EDGE):
            high = (i + 0.5) / EDGE
            for c in range(3):
                value = grad[c, z * EDGE + i].astype(F32) * left[i]
                for m, weight in enumerate((1.0 - high, high)):
                    sums[m][c] = value * weight if i == 0 else sums[m][c] + value * weight
        for m in range(2):
            rows = [jnp.sum(sums[m][c] * w, axis=0, keepdims=True) for w in (low_j, high_j) for c in range(3)]
            blank = jnp.zeros((1, NY), F32)
            start = (z * 2 + m) * 8
            rrow[start : start + 8, :] = jnp.concatenate(rows[:3] + [blank] + rows[3:] + [blank], axis=0)
    fine, coarse = iota((NY, NY), 0), iota((NY, NY), 1)
    low_y, high_y = hats(fine & 15)
    row_y, node_y = fine >> 4, (coarse & 15) - 4
    weight_y = (
        jnp.where(row_y == node_y, low_y, 0.0) + jnp.where(row_y + 1 == node_y, high_y, 0.0)
    ) * (1.0 / VOL)
    nodes = jnp.dot(rrow[...], weight_y, precision=EXACT, preferred_element_type=F32)
    tile = jnp.zeros((8, NY), F32)
    for z in range(EZ):
        for m in range(2):
            start = (z * 2 + m) * 8
            tile = tile + jnp.where(on[z + m], nodes[start : start + 8], 0.0)
    rs[...] = tile

    def gathered(mine, arrived, dp):
        total = mine
        for dq, shift, keep in ((1, 8, inner >= 8), (-1, -8, inner < 8)):
            inside = flag((q + dq >= 0) & (q + dq < ny))
            total = total + jnp.where(keep, rolled(arrived(dp, dq), shift, 1), 0.0) * inside
        return total * flag((p + dp >= 0) & (p + dp < nx))

    sent = [send(A_RHS + k, rs, rr.at[k], -dp, -dq) for k, (dp, dq) in enumerate(
        [(-dp, -dq) for dp, dq in RHS_OFFSETS])]
    for c in sent:
        c.wait_recv()

    def rhs_from(dp, dq):
        return rs[...] if (dp, dq) == (0, 0) else rr[RHS_OFFSETS.index((-dp, -dq))]

    around = {dp: gathered(rhs_from(dp, 0), rhs_from, dp) for dp in (-2, -1, 0, 1)}
    first3 = sub < 3
    inside_y = q * EYD + column < ny * EYD
    vector = []
    for dp in (-1, 0, 1):
        whole = around[dp] + rolled(around[dp - 1], 4, 0)
        vector.append(jnp.where(first3 & inside_y, whole, 0.0) * flag((p + dp >= 0) & (p + dp < nx)))

    def apply(vector):
        straight, crossed = jnp.zeros((8, NY), F32), jnp.zeros((8, NY), F32)
        for dx in range(3):
            u = [vector[dx][c : c + 1] for c in range(3)]
            second = jnp.where(sub == 0, u[0], jnp.where((sub == 1) | (sub == 3), u[1], u[2]))
            third = jnp.where(sub == 5, u[1], u[0])
            for t in range(9):
                shift = -((t // 3 - 1) * 16 + t % 3 - 1)
                weight = kk[dx, t]
                straight = straight + weight * rolled(second, shift, 1)
                crossed = crossed + weight * rolled(third, shift, 1)
        s = [straight[k : k + 1] for k in range(6)]
        out = [
            s[0] + s[3] + s[4],
            s[1] + s[5] + crossed[3:4],
            s[2] + crossed[4:5] + crossed[5:6],
        ]
        image = jnp.where(sub == 0, out[0], jnp.where(sub == 1, out[1], out[2]))
        return jnp.where(own & first3, image + LAMBDA * vector[1], 0.0)

    powers = [jnp.where(own, vector[1], 0.0)]
    for step in range(3):
        image = apply(vector)
        powers.append(image)
        if step < 2:
            vs[step] = image
            sent = [
                send(A_VEC + step * N_VEC + k, vs.at[step], vr.at[step, k], dp, dq)
                for k, (dp, dq) in enumerate(VEC_OFFSETS)
            ]
            for c in sent:
                c.wait_recv()

            def arrived(dp, dq):
                return vr[step, VEC_OFFSETS.index((-dp, -dq))]

            vector = [gathered(image if dp == 0 else arrived(dp, 0), arrived, dp) for dp in (-1, 0, 1)]

    tile = jnp.zeros((8, NY), F32)
    for k in range(6):
        product = jnp.sum(powers[k // 2] * powers[(k + 1) // 2], axis=0, keepdims=True)
        tile = jnp.where(sub == k, product, tile)
    gs[...] = tile

    def to_x(k, _):
        copy(gs, gr.at[k - 1], gssem.at[k - 1], grsem.at[k - 1], k, 0)
        return 0

    def from_x(k, total):
        pltpu.make_async_remote_copy(
            src_ref=gs, dst_ref=gr.at[k - 1], send_sem=gssem.at[k - 1], recv_sem=grsem.at[k - 1],
            device_id=at(k, 0), device_id_type=MESH,
        ).wait()
        return total + gr[k - 1]

    lax.fori_loop(1, nx, to_x, 0)
    tile = lax.fori_loop(1, nx, from_x, tile)
    hs[...] = tile

    def to_y(k, _):
        copy(hs, hr.at[k - 1], hssem.at[k - 1], hrsem.at[k - 1], 0, k)
        return 0

    def from_y(k, total):
        pltpu.make_async_remote_copy(
            src_ref=hs, dst_ref=hr.at[k - 1], send_sem=hssem.at[k - 1], recv_sem=hrsem.at[k - 1],
            device_id=at(0, k), device_id_type=MESH,
        ).wait()
        return total + hr[k - 1]

    lax.fori_loop(1, ny, to_y, 0)
    tile = lax.fori_loop(1, ny, from_y, tile)
    total = jnp.broadcast_to(jnp.sum(tile, axis=1, keepdims=True), (8, NY))
    moment = [total[k : k + 1] for k in range(6)]

    def product(a, b, more):
        value = 0.0
        for i, left in enumerate(a):
            for j, right in enumerate(b):
                value = value + left * right * moment[i + j + more]
        return value

    blank, unit = jnp.zeros((1, NY), F32), jnp.ones((1, NY), F32)
    answer, residual, direction = [blank] * 3, [unit], [unit]
    norm = moment[0]
    for step in range(3):
        bend = product(direction, direction, 1)
        alpha = norm / bend
        answer = [answer[i] + alpha * direction[i] if i < len(direction) else answer[i] for i in range(3)]
        if step < 2:
            grown = residual + [blank]
            residual = [
                grown[i] - alpha * direction[i - 1] if i > 0 else grown[i] for i in range(step + 2)
            ]
            after = product(residual, residual, 0)
            beta = after / norm
            norm = after
            widened = direction + [blank]
            direction = [residual[i] + beta * widened[i] for i in range(step + 2)]
    inc[...] = answer[0] * powers[0] + answer[1] * powers[1] + answer[2] * powers[2]
    for c in started:
        c.wait_send()


def body(nx, ny, reference_image, deformed_image, route, within, xshift, fractions):
    vmem = pl.BlockSpec(memory_space=pltpu.VMEM)
    smem = pl.BlockSpec(memory_space=pltpu.SMEM)
    half = (NZ, EDGE, NY)
    tile = (8, NY)
    inc, mis = pl.pallas_call(
        lambda *refs: kernel(nx, ny, *refs),
        name="correlate",
        out_shape=(jax.ShapeDtypeStruct(tile, F32), jax.ShapeDtypeStruct(half, F32)),
        in_specs=[smem] * 4 + [vmem] * 2,
        out_specs=(vmem, vmem),
        scratch_shapes=[
            pltpu.VMEM((2,) + half, BF16),
            pltpu.VMEM(tile, jnp.int32),
            pltpu.VMEM((4,) + tile, jnp.int32),
            pltpu.VMEM((2, NZ, NY), BF16),
            pltpu.VMEM((2, NZ, NY), BF16),
            pltpu.VMEM((16, NZ * EDGE), BF16),
            pltpu.VMEM((2, 16, NZ * EDGE), BF16),
            pltpu.VMEM((3 * EZ * NY, ROUTES * NY), BF16),
            pltpu.VMEM((EDGE * EDGE, ROUTES * NY), F32),
            pltpu.VMEM((4, EDGE * EDGE, NY), BF16),
            pltpu.VMEM((ROUTES, EDGE * EDGE, NY), BF16),
            pltpu.VMEM((ROUTES * NY, EZ * NY), BF16),
            pltpu.VMEM((3,) + half, BF16),
            pltpu.VMEM((NZ + 2, 32, NY), F32),
            pltpu.VMEM((12 * 24, NY), F32),
            pltpu.VMEM((3, 9) + tile, F32),
            pltpu.VMEM((2, 9) + tile, F32),
            pltpu.VMEM((3, 9) + tile, F32),
            pltpu.VMEM((2, 9) + tile, F32),
            pltpu.VMEM((3, 9) + tile, F32),
            pltpu.VMEM((64, NY), F32),
            pltpu.VMEM(tile, F32),
            pltpu.VMEM((N_RHS,) + tile, F32),
            pltpu.VMEM((2,) + tile, F32),
            pltpu.VMEM((2, N_VEC) + tile, F32),
            pltpu.VMEM(tile, F32),
            pltpu.VMEM((nx - 1,) + tile, F32),
            pltpu.VMEM(tile, F32),
            pltpu.VMEM((ny - 1,) + tile, F32),
            pltpu.SemaphoreType.DMA((A_END,)),
            pltpu.SemaphoreType.DMA((A_END,)),
            pltpu.SemaphoreType.DMA((nx - 1,)),
            pltpu.SemaphoreType.DMA((nx - 1,)),
            pltpu.SemaphoreType.DMA((ny - 1,)),
            pltpu.SemaphoreType.DMA((ny - 1,)),
        ],
        compiler_params=pltpu.CompilerParams(
            collective_id=0, has_side_effects=True, vmem_limit_bytes=48 << 20
        ),
    )(route, within, xshift, fractions, reference_image, deformed_image)
    grid = inc[:3].reshape(3, 8, 16)
    return grid[:, : EZ + 1, None, 4 : 4 + EYD], mis


def solution(mesh):
    nx, ny = mesh.shape["gx"], mesh.shape["gy"]
    placed = (
        P(None, "gx", "gy"),
        P(None, "gx", "gy"),
        P("gx", "gy", None, None),
        P("gx", "gy", None),
        P("gx", "gy", None),
        P("gx", "gy", None, None),
    )
    return jax.shard_map(
        lambda *blocks: body(nx, ny, *blocks),
        mesh=mesh,
        in_specs=placed,
        out_specs=(P(None, None, "gx", "gy"), P(None, "gx", "gy")),
        check_vma=False,
    )
```

```python
import jax
import jax.numpy as jnp
from jax import lax
from jax.experimental import pallas as pl
from jax.experimental.pallas import tpu as pltpu
from jax.sharding import PartitionSpec as P

EDGE = 16
EZ = 4
EYD = 8
SPAN = 2
ROUTES = 2 * SPAN + 1
NEL = 32
CAP = 8
VOL = 4096
NZ = 64
NY = 128
LAMBDA = 0.05
MESH = pl.DeviceIdType.MESH
F32 = jnp.float32
BF16 = jnp.bfloat16
EXACT = lax.Precision.HIGHEST

N_TABLE, N_BLOCK, N_FACE_X, N_FACE_Y, N_PACK, N_STENCIL, N_RHS, N_VEC = 4, 2, 2, 2, 4, 3, 11, 8
A_TABLE = 0
A_BLOCK = A_TABLE + N_TABLE
A_FACE_X = A_BLOCK + N_BLOCK
A_FACE_Y = A_FACE_X + N_FACE_X
A_PACK = A_FACE_Y + N_FACE_Y
A_STENCIL = A_PACK + N_PACK
A_RHS = A_STENCIL + N_STENCIL
A_VEC = A_RHS + N_RHS
A_END = A_VEC + 2 * N_VEC

OTHER_ROUTES = (1, 3, 0, 4)
RHS_OFFSETS = [(dp, dq) for dp in (-1, 0, 1, 2) for dq in (-1, 0, 1) if (dp, dq) != (0, 0)]
VEC_OFFSETS = [(dp, dq) for dp in (-1, 0, 1) for dq in (-1, 0, 1) if (dp, dq) != (0, 0)]
PAIRS = ((0, 0), (1, 1), (2, 2), (0, 1), (0, 2), (1, 2))


def iota(shape, dim):
    return lax.broadcasted_iota(jnp.int32, shape, dim)


def flag(condition):
    return jnp.where(condition, jnp.float32(1.0), jnp.float32(0.0))


def rolled(value, shift, axis):
    size = value.shape[axis]
    shift = shift % size
    return value if shift == 0 else pltpu.roll(value, shift, axis)


def halves(value):
    high = value.astype(BF16)
    return high, (value - high.astype(F32)).astype(BF16)


def near_exact(left, right):
    a, b = halves(left), halves(right)
    total = jnp.dot(a[0], b[1], preferred_element_type=F32) + jnp.dot(a[1], b[0], preferred_element_type=F32)
    return total + jnp.dot(a[0], b[0], preferred_element_type=F32)


def hats(position):
    upper = (position.astype(F32) + 0.5) / EDGE
    return 1.0 - upper, upper


def kernel(
    nx, ny, route_hbm, within_hbm, xshift_hbm, fractions_hbm, ref_hbm, dfm_hbm, inc, mis,
    route, within, xshift, fractions, ref, dfm, lsem, gossip,
    xb, tsend, trecv, fxs, fxr, fys, fyr, pmat, pacc, psend, precv, qmat, grad, refp, xrow, ss, sx, sy, sxy,
    kk, rrow, rs, rr, vs, vr, gs, gr, hs, hr, ssem, rsem, gssem, grsem, hssem, hrsem,
):
    p, q = lax.axis_index("gx"), lax.axis_index("gy")

    def at(dp, dq):
        return (lax.rem(p + dp + 2 * nx, nx), lax.rem(q + dq + 2 * ny, ny))

    def copy(src, dst, send_sem, recv_sem, dp, dq):
        c = pltpu.make_async_remote_copy(
            src_ref=src, dst_ref=dst, send_sem=send_sem, recv_sem=recv_sem,
            device_id=at(dp, dq), device_id_type=MESH,
        )
        c.start()
        return c

    started = []

    def send(number, src, dst, dp, dq):
        c = copy(src, dst, ssem.at[number], rsem.at[number], dp, dq)
        started.append(c)
        return c

    near = ((1, 0), (-1, 0), (0, 1), (0, -1), (0, 2), (0, -2))
    barrier = pltpu.get_barrier_semaphore()
    for dp, dq in near:
        pl.semaphore_signal(barrier, inc=1, device_id=at(dp, dq), device_id_type=MESH)
    loads = []
    for k, (src, dst) in enumerate((
        (route_hbm, route), (within_hbm, within), (xshift_hbm, xshift), (fractions_hbm, fractions),
        (ref_hbm, ref), (dfm_hbm, dfm),
    )):
        loads.append(pltpu.make_async_copy(src, dst, lsem.at[k]))
        loads[k].start()

    def tell(number, *places):
        for dp, dq in places:
            pl.semaphore_signal(gossip.at[number], inc=1, device_id=at(dp, dq), device_id_type=MESH)

    def hear(number, count):
        pl.semaphore_wait(gossip.at[number], count)

    pl.semaphore_wait(barrier, len(near))
    blocks = [send(A_BLOCK, dfm_hbm, xb.at[1], -1, 0), send(A_BLOCK + 1, dfm_hbm, xb.at[0], 1, 0)]

    lane, sub = iota((8, NY), 1), iota((8, NY), 0)
    block, inner = lane >> 4, lane & 15

    for c in loads[:3]:
        c.wait()
    routes = [route[0, 0, e] for e in range(NEL)]
    wanted = jnp.full((8, NY), -1, jnp.int32)
    count = jnp.zeros((8, NY), jnp.int32)
    for e in range(NEL):
        source = jnp.clip(p + xshift[0, 0, e] - 1, 0, nx - 1) - p + 1
        code = ((source * EZ + e // EYD) * EYD + within[0, 0, e]) * EDGE
        hit = sub == routes[e]
        wanted = jnp.where(hit & (count == block), inner + code, wanted)
        count = count + jnp.where(hit, 1, 0)
    tsend[...] = wanted
    tables = [
        send(A_TABLE + k, tsend, trecv.at[k], 0, r - SPAN) for k, r in enumerate(OTHER_ROUTES)
    ]

    loads[4].wait()
    refp[0] = jnp.zeros((32, NY), F32)
    refp[NZ + 1] = jnp.zeros((32, NY), F32)
    refp[1 : NZ + 1, 8:24, :] = ref[...].astype(F32)
    fxs[0] = refp[1 : NZ + 1, 8, :].astype(BF16)
    fxs[1] = refp[1 : NZ + 1, 23, :].astype(BF16)
    faces_x = [
        send(A_FACE_X, fxs.at[0], fxr.at[1], -1, 0),
        send(A_FACE_X + 1, fxs.at[1], fxr.at[0], 1, 0),
    ]
    rows16, lanes16 = iota((16, NY), 0), iota((16, NY), 1)
    pick = ((rows16 == 0) & (lanes16 == 0)) | ((rows16 == 1) & (lanes16 == NY - 1))
    fys[...] = lax.dot_general(
        jnp.where(pick, 1.0, 0.0).astype(BF16), ref[...].reshape(NZ * EDGE, NY),
        (((1,), (1,)), ((), ())), preferred_element_type=F32,
    ).astype(BF16)
    faces_y = [
        send(A_FACE_Y, fys, fyr.at[1], 0, -1),
        send(A_FACE_Y + 1, fys, fyr.at[0], 0, 1),
    ]

    loads[3].wait()
    element = sub * EYD + block
    own_route = jnp.zeros((8, NY), jnp.int32)
    parts = [jnp.zeros((8, NY), jnp.int32) for _ in range(3)]
    for e in range(NEL):
        here = element == e
        own_route = jnp.where(here, routes[e], own_route)
        parts = [jnp.where(here, fractions[0, c, 0, e], parts[c]) for c in range(3)]
    slot = jnp.zeros((8, NY), jnp.int32)
    for e in range(NEL):
        slot = slot + jnp.where((element > e) & (own_route == routes[e]), 1, 0)
    first = (own_route * CAP + slot) * EDGE
    portion = [part.astype(F32) / EDGE for part in parts]
    target0 = first + inner
    target1 = first + jnp.minimum(inner + 1, EDGE - 1)

    for c in faces_x + faces_y:
        c.wait_recv()
    refp[1 : NZ + 1, 7, :] = fxr[0].astype(F32) * flag(p > 0)
    refp[1 : NZ + 1, 24, :] = fxr[1].astype(F32) * flag(p < nx - 1)
    here, there = iota((NY, NY), 1), iota((NY, NY), 0)
    differ = jnp.where(there == here + 1, 0.5, jnp.where(there == here - 1, -0.5, 0.0)).astype(BF16)
    rows32, lanes32 = iota((32, NY), 0), iota((32, NY), 1)
    ends = jnp.where(
        (rows32 == 1) & (lanes32 == 0), flag(q > 0) * -0.5,
        jnp.where((rows32 == 16) & (lanes32 == NY - 1), flag(q < ny - 1) * 0.5, 0.0),
    ).astype(BF16)
    sides = jnp.concatenate([fyr[0], fyr[1]], axis=0)
    along_y = jnp.dot(ref[...].reshape(NZ * EDGE, NY), differ, preferred_element_type=F32)
    along_y = along_y + lax.dot_general(sides, ends, (((0,), (0,)), ((), ())), preferred_element_type=F32)
    grad[2] = along_y.astype(BF16).reshape(NZ, EDGE, NY)

    def slope(b, _):
        base = b * 4
        below, above = refp[pl.ds(base, 4), 8:24, :], refp[pl.ds(base + 2, 4), 8:24, :]
        grad[0, pl.ds(base, 4)] = ((above - below) * 0.5).astype(BF16)
        left, right = refp[pl.ds(base + 1, 4), 7:23, :], refp[pl.ds(base + 1, 4), 9:25, :]
        grad[1, pl.ds(base, 4)] = ((right - left) * 0.5).astype(BF16)
        return 0

    lax.fori_loop(0, NZ // 4, slope, 0)
    tell(0, (1, 0), (-1, 0))

    for z in range(EZ):
        def fill_place(b, _):
            row = b * NY + iota((NY, NY), 0)
            high = portion[2][z : z + 1]
            place = jnp.where(row == target0[z : z + 1], 1.0 - high, 0.0)
            place = place + jnp.where(row == target1[z : z + 1], high, 0.0)
            qmat[pl.ds(pl.multiple_of(b * NY, NY), NY), z * NY : (z + 1) * NY] = place.astype(BF16)
            return 0

        lax.fori_loop(0, ROUTES, fill_place, 0)

    for c in tables:
        c.wait_recv()
    tell(2, (0, 4), (0, -4))
    asked = []
    for r in range(ROUTES):
        if r == SPAN:
            asked.append(wanted[r : r + 1])
        else:
            k = OTHER_ROUTES.index(r)
            asked.append(trecv[k, r : r + 1, :])
    asked = jnp.concatenate(asked, axis=1)

    def fill_pack(b, _):
        row = b * NY + iota((NY, ROUTES * NY), 0)
        pmat[pl.ds(pl.multiple_of(b * NY, NY), NY), :] = jnp.where(row == asked, 1.0, 0.0).astype(BF16)
        return 0

    lax.fori_loop(0, 3 * EZ, fill_pack, 0)

    def brick_rows(source):
        return jnp.concatenate(
            [source[z * EDGE : (z + 1) * EDGE].reshape(EDGE * EDGE, NY) for z in range(EZ)], axis=1
        )

    width = EZ * NY
    loads[5].wait()
    pacc[...] = jnp.dot(brick_rows(dfm), pmat[width : 2 * width, :], preferred_element_type=F32)
    blocks[1].wait_recv()
    pacc[...] += jnp.dot(brick_rows(xb[0]), pmat[0:width, :], preferred_element_type=F32)
    blocks[0].wait_recv()
    pacc[...] += jnp.dot(brick_rows(xb[1]), pmat[2 * width : 3 * width, :], preferred_element_type=F32)
    packs = []
    for k, r in enumerate(OTHER_ROUTES):
        psend[k] = pacc[:, r * NY : (r + 1) * NY].astype(BF16)
        packs.append(send(A_PACK + k, psend.at[k], precv.at[r], 0, SPAN - r))
    hear(0, 2)
    tell(1, (1, 0), (-1, 0))
    hear(2, 2)
    tell(3, (0, 8), (0, -8))
    precv[SPAN] = pacc[:, SPAN * NY : (SPAN + 1) * NY].astype(BF16)

    rowm, colm = iota((24, 96), 0), iota((24, 96), 1)
    low_x, high_x = hats(colm & 15)
    order = rowm >> 3
    weight_x = jnp.where(order == 0, low_x * low_x, jnp.where(order == 1, low_x * high_x, high_x * high_x))
    weight_x = jnp.where((rowm & 7) == (colm >> 4), weight_x, 0.0)
    weights_x = jnp.concatenate(halves(weight_x), axis=0)

    def moments(z, _):
        total = [[None] * 6 for _ in range(3)]
        for i in range(EDGE):
            g = [grad[c, z * EDGE + i].astype(F32) for c in range(3)]
            high = (i + 0.5) / EDGE
            low = 1.0 - high
            for k, (a, b) in enumerate(PAIRS):
                product = g[a] * g[b]
                for m, weight in enumerate((low * low, low * high, high * high)):
                    term = product * weight
                    total[m][k] = term if i == 0 else total[m][k] + term
        for m in range(3):
            parts = [
                jnp.dot(weights_x, part, preferred_element_type=F32)
                for part in halves(jnp.concatenate(total[m], axis=0))
            ]
            rows = (parts[1][:24] + parts[0][24:]) + parts[0][:24]
            xrow[pl.ds(pl.multiple_of((z * 3 + m) * 24, 24), 24), :] = rows
        return 0

    lax.fori_loop(0, EZ, moments, 0)
    fine, coarse = iota((NY, 3 * NY), 0), iota((NY, 3 * NY), 1)
    low_y, high_y = hats(fine & 15)
    row_y, node_y, step_y = fine >> 4, (coarse & 15) - 4, (coarse >> 7) - 1
    starts, closes = row_y == node_y, row_y + 1 == node_y
    mixed = low_y * high_y
    weight_y = jnp.where(
        step_y == 1, jnp.where(starts, mixed, 0.0),
        jnp.where(
            step_y == -1, jnp.where(closes, mixed, 0.0),
            jnp.where(starts, low_y * low_y, 0.0) + jnp.where(closes, high_y * high_y, 0.0),
        ),
    ) * (1.0 / VOL)
    yrow = near_exact(xrow[...], weight_y)
    on = [block == z for z in range(EZ + 1)]
    for m in range(3):
        for dy in range(3):
            def term(z, depth):
                start = (z * 3 + depth) * 24 + m * 8
                return yrow[start : start + 8, dy * NY : (dy + 1) * NY]

            zero = jnp.zeros((8, NY), F32)
            down, same, up = zero, zero, zero
            for z in range(EZ):
                cross = term(z, 1)
                up = jnp.where(on[z], cross, up)
                down = jnp.where(on[z + 1], cross, down)
                same = same + jnp.where(on[z], term(z, 0), 0.0) + jnp.where(on[z + 1], term(z, 2), 0.0)
            ss[m, dy], ss[m, 3 + dy], ss[m, 6 + dy] = down, same, up
    stencils = [
        send(A_STENCIL, ss.at[1:3], sx, 1, 0),
        send(A_STENCIL + 1, ss, sy, 0, 1),
        send(A_STENCIL + 2, ss.at[1:3], sxy, 1, 1),
    ]

    column = inner - 4
    own = (column >= 0) & (column < EYD) & (block <= EZ)
    has_x, has_y = flag(p > 0), flag(q > 0)
    for c in stencils:
        c.wait_recv()

    def fold(from_y):
        return jnp.where(inner < 8, rolled(from_y, -8, 1), 0.0) * has_y

    for t in range(9):
        here0 = ss[0, t] + fold(sy[0, t])
        here1 = ss[1, t] + fold(sy[1, t])
        back1 = (sx[0, t] + fold(sxy[0, t])) * has_x
        back2 = (sx[1, t] + fold(sxy[1, t])) * has_x
        kk[0, t] = jnp.where(own, back1, 0.0)
        kk[1, t] = jnp.where(own, here0 + back2, 0.0)
        kk[2, t] = jnp.where(own, here1, 0.0)

    for c in packs:
        c.wait_recv()
    taken = jnp.concatenate([precv[r] for r in range(ROUTES)], axis=1)
    fetched = jnp.dot(taken, qmat[...], preferred_element_type=F32)
    row8, col16 = iota((8, EDGE), 0), iota((8, EDGE), 1)
    low_j, high_j = hats(iota((EDGE, 1), 0))
    for z in range(EZ):
        voxels = fetched[:, z * NY : (z + 1) * NY].reshape(EDGE, EDGE, NY)
        high = portion[1][z : z + 1].reshape(1, 1, NY)
        ahead = jnp.concatenate([voxels[:, 1:], voxels[:, EDGE - 1 :]], axis=1)
        voxels = (1.0 - high) * voxels + high * ahead
        high = portion[0][z : z + 1].reshape(1, 1, NY)
        ahead = jnp.concatenate([voxels[1:], voxels[EDGE - 1 :]], axis=0)
        voxels = (1.0 - high) * voxels + high * ahead
        left = refp[1 + z * EDGE : 1 + (z + 1) * EDGE, 8:24, :] - voxels
        mis[z * EDGE : (z + 1) * EDGE] = left
        sums = [[None] * 3 for _ in range(2)]
        for i in range(EDGE):
            high = (i + 0.5) / EDGE
            for c in range(3):
                value = grad[c, z * EDGE + i].astype(F32) * left[i]
                for m, weight in enumerate((1.0 - high, high)):
                    sums[m][c] = value * weight if i == 0 else sums[m][c] + value * weight
        for m in range(2):
            rows = [jnp.sum(sums[m][c] * w, axis=0, keepdims=True) for w in (low_j, high_j) for c in range(3)]
            blank = jnp.zeros((1, NY), F32)
            start = (z * 2 + m) * 8
            rrow[start : start + 8, :] = jnp.concatenate(rows[:3] + [blank] + rows[3:] + [blank], axis=0)
    fine, coarse = iota((NY, NY), 0), iota((NY, NY), 1)
    low_y, high_y = hats(fine & 15)
    row_y, node_y = fine >> 4, (coarse & 15) - 4
    weight_y = (
        jnp.where(row_y == node_y, low_y, 0.0) + jnp.where(row_y + 1 == node_y, high_y, 0.0)
    ) * (1.0 / VOL)
    nodes = jnp.dot(rrow[...], weight_y, precision=EXACT, preferred_element_type=F32)
    tile = jnp.zeros((8, NY), F32)
    for z in range(EZ):
        for m in range(2):
            start = (z * 2 + m) * 8
            tile = tile + jnp.where(on[z + m], nodes[start : start + 8], 0.0)
    rs[...] = tile

    def gathered(mine, arrived, dp):
        total = mine
        for dq, shift, keep in ((1, 8, inner >= 8), (-1, -8, inner < 8)):
            inside = flag((q + dq >= 0) & (q + dq < ny))
            total = total + jnp.where(keep, rolled(arrived(dp, dq), shift, 1), 0.0) * inside
        return total * flag((p + dp >= 0) & (p + dp < nx))

    sent = [send(A_RHS + k, rs, rr.at[k], -dp, -dq) for k, (dp, dq) in enumerate(
        [(-dp, -dq) for dp, dq in RHS_OFFSETS])]
    for c in sent:
        c.wait_recv()

    def rhs_from(dp, dq):
        return rs[...] if (dp, dq) == (0, 0) else rr[RHS_OFFSETS.index((-dp, -dq))]

    around = {dp: gathered(rhs_from(dp, 0), rhs_from, dp) for dp in (-2, -1, 0, 1)}
    first3 = sub < 3
    inside_y = q * EYD + column < ny * EYD
    vector = []
    for dp in (-1, 0, 1):
        whole = around[dp] + rolled(around[dp - 1], 4, 0)
        vector.append(jnp.where(first3 & inside_y, whole, 0.0) * flag((p + dp >= 0) & (p + dp < nx)))

    def apply(vector):
        straight, crossed = jnp.zeros((8, NY), F32), jnp.zeros((8, NY), F32)
        for dx in range(3):
            u = [vector[dx][c : c + 1] for c in range(3)]
            second = jnp.where(sub == 0, u[0], jnp.where((sub == 1) | (sub == 3), u[1], u[2]))
            third = jnp.where(sub == 5, u[1], u[0])
            for t in range(9):
                shift = -((t // 3 - 1) * 16 + t % 3 - 1)
                weight = kk[dx, t]
                straight = straight + weight * rolled(second, shift, 1)
                crossed = crossed + weight * rolled(third, shift, 1)
        s = [straight[k : k + 1] for k in range(6)]
        out = [
            s[0] + s[3] + s[4],
            s[1] + s[5] + crossed[3:4],
            s[2] + crossed[4:5] + crossed[5:6],
        ]
        image = jnp.where(sub == 0, out[0], jnp.where(sub == 1, out[1], out[2]))
        return jnp.where(own & first3, image + LAMBDA * vector[1], 0.0)

    powers = [jnp.where(own, vector[1], 0.0)]
    for step in range(3):
        image = apply(vector)
        powers.append(image)
        if step < 2:
            vs[step] = image
            sent = [
                send(A_VEC + step * N_VEC + k, vs.at[step], vr.at[step, k], dp, dq)
                for k, (dp, dq) in enumerate(VEC_OFFSETS)
            ]
            for c in sent:
                c.wait_recv()

            def arrived(dp, dq):
                return vr[step, VEC_OFFSETS.index((-dp, -dq))]

            vector = [gathered(image if dp == 0 else arrived(dp, 0), arrived, dp) for dp in (-1, 0, 1)]

    tile = jnp.zeros((8, NY), F32)
    for k in range(6):
        product = jnp.sum(powers[k // 2] * powers[(k + 1) // 2], axis=0, keepdims=True)
        tile = jnp.where(sub == k, product, tile)
    gs[...] = tile
    hear(1, 2)
    hear(3, 2)

    def to_x(k, _):
        copy(gs, gr.at[k - 1], gssem.at[k - 1], grsem.at[k - 1], k, 0)
        return 0

    def from_x(k, total):
        pltpu.make_async_remote_copy(
            src_ref=gs, dst_ref=gr.at[k - 1], send_sem=gssem.at[k - 1], recv_sem=grsem.at[k - 1],
            device_id=at(k, 0), device_id_type=MESH,
        ).wait()
        return total + gr[k - 1]

    for k in sorted(range(1, nx), key=lambda k: (-min(k, nx - k), k)):
        to_x(k, 0)
    for k in range(1, nx):
        tile = from_x(k, tile)
    hs[...] = tile

    def to_y(k, _):
        copy(hs, hr.at[k - 1], hssem.at[k - 1], hrsem.at[k - 1], 0, k)
        return 0

    def from_y(k, total):
        pltpu.make_async_remote_copy(
            src_ref=hs, dst_ref=hr.at[k - 1], send_sem=hssem.at[k - 1], recv_sem=hrsem.at[k - 1],
            device_id=at(0, k), device_id_type=MESH,
        ).wait()
        return total + hr[k - 1]

    for k in sorted(range(1, ny), key=lambda k: (-min(k, ny - k), k)):
        to_y(k, 0)
    for k in range(1, ny):
        tile = from_y(k, tile)
    total = jnp.broadcast_to(jnp.sum(tile, axis=1, keepdims=True), (8, NY))
    moment = [total[k : k + 1] for k in range(6)]

    def product(a, b, more):
        value = 0.0
        for i, left in enumerate(a):
            for j, right in enumerate(b):
                value = value + left * right * moment[i + j + more]
        return value

    blank, unit = jnp.zeros((1, NY), F32), jnp.ones((1, NY), F32)
    answer, residual, direction = [blank] * 3, [unit], [unit]
    norm = moment[0]
    for step in range(3):
        bend = product(direction, direction, 1)
        alpha = norm / bend
        answer = [answer[i] + alpha * direction[i] if i < len(direction) else answer[i] for i in range(3)]
        if step < 2:
            grown = residual + [blank]
            residual = [
                grown[i] - alpha * direction[i - 1] if i > 0 else grown[i] for i in range(step + 2)
            ]
            after = product(residual, residual, 0)
            beta = after / norm
            norm = after
            widened = direction + [blank]
            direction = [residual[i] + beta * widened[i] for i in range(step + 2)]
    inc[...] = answer[0] * powers[0] + answer[1] * powers[1] + answer[2] * powers[2]
    for c in started:
        c.wait_send()


def body(nx, ny, reference_image, deformed_image, route, within, xshift, fractions):
    vmem = pl.BlockSpec(memory_space=pltpu.VMEM)
    half = (NZ, EDGE, NY)
    tile = (8, NY)
    inc, mis = pl.pallas_call(
        lambda *refs: kernel(nx, ny, *refs),
        name="correlate",
        out_shape=(jax.ShapeDtypeStruct(tile, F32), jax.ShapeDtypeStruct(half, F32)),
        in_specs=[pl.BlockSpec(memory_space=pltpu.HBM)] * 6,
        out_specs=(vmem, vmem),
        scratch_shapes=[
            pltpu.SMEM((1, 1, NEL), jnp.int32),
            pltpu.SMEM((1, 1, NEL), jnp.int32),
            pltpu.SMEM((1, 1, NEL), jnp.int32),
            pltpu.SMEM((1, 3, 1, NEL), jnp.int32),
            pltpu.VMEM(half, BF16),
            pltpu.VMEM(half, BF16),
            pltpu.SemaphoreType.DMA((6,)),
            pltpu.SemaphoreType.REGULAR((4,)),
            pltpu.VMEM((2,) + half, BF16),
            pltpu.VMEM(tile, jnp.int32),
            pltpu.VMEM((4,) + tile, jnp.int32),
            pltpu.VMEM((2, NZ, NY), BF16),
            pltpu.VMEM((2, NZ, NY), BF16),
            pltpu.VMEM((16, NZ * EDGE), BF16),
            pltpu.VMEM((2, 16, NZ * EDGE), BF16),
            pltpu.VMEM((3 * EZ * NY, ROUTES * NY), BF16),
            pltpu.VMEM((EDGE * EDGE, ROUTES * NY), F32),
            pltpu.VMEM((4, EDGE * EDGE, NY), BF16),
            pltpu.VMEM((ROUTES, EDGE * EDGE, NY), BF16),
            pltpu.VMEM((ROUTES * NY, EZ * NY), BF16),
            pltpu.VMEM((3,) + half, BF16),
            pltpu.VMEM((NZ + 2, 32, NY), F32),
            pltpu.VMEM((12 * 24, NY), F32),
            pltpu.VMEM((3, 9) + tile, F32),
            pltpu.VMEM((2, 9) + tile, F32),
            pltpu.VMEM((3, 9) + tile, F32),
            pltpu.VMEM((2, 9) + tile, F32),
            pltpu.VMEM((3, 9) + tile, F32),
            pltpu.VMEM((64, NY), F32),
            pltpu.VMEM(tile, F32),
            pltpu.VMEM((N_RHS,) + tile, F32),
            pltpu.VMEM((2,) + tile, F32),
            pltpu.VMEM((2, N_VEC) + tile, F32),
            pltpu.VMEM(tile, F32),
            pltpu.VMEM((nx - 1,) + tile, F32),
            pltpu.VMEM(tile, F32),
            pltpu.VMEM((ny - 1,) + tile, F32),
            pltpu.SemaphoreType.DMA((A_END,)),
            pltpu.SemaphoreType.DMA((A_END,)),
            pltpu.SemaphoreType.DMA((nx - 1,)),
            pltpu.SemaphoreType.DMA((nx - 1,)),
            pltpu.SemaphoreType.DMA((ny - 1,)),
            pltpu.SemaphoreType.DMA((ny - 1,)),
        ],
        compiler_params=pltpu.CompilerParams(
            collective_id=0, has_side_effects=True, vmem_limit_bytes=63 << 20
        ),
    )(route.reshape(1, 1, NEL), within, xshift, fractions.transpose(0, 3, 1, 2), reference_image, deformed_image)
    grid = inc[:3].reshape(3, 8, 16)
    return grid[:, : EZ + 1, None, 4 : 4 + EYD], mis


def solution(mesh):
    nx, ny = mesh.shape["gx"], mesh.shape["gy"]
    placed = (
        P(None, "gx", "gy"),
        P(None, "gx", "gy"),
        P("gx", "gy", None, None),
        P("gx", "gy", None),
        P("gx", "gy", None),
        P("gx", "gy", None, None),
    )
    return jax.shard_map(
        lambda *blocks: body(nx, ny, *blocks),
        mesh=mesh,
        in_specs=placed,
        out_specs=(P(None, None, "gx", "gy"), P(None, "gx", "gy")),
        check_vma=False,
    )
```

```python
import jax
import jax.numpy as jnp
from jax import lax
from jax.experimental import pallas as pl
from jax.experimental.pallas import tpu as pltpu
from jax.sharding import PartitionSpec as P

EDGE = 16
EZ = 4
EYD = 8
SPAN = 2
ROUTES = 2 * SPAN + 1
NEL = 32
CAP = 8
VOL = 4096
NZ = 64
NY = 128
LAMBDA = 0.05
MESH = pl.DeviceIdType.MESH
F32 = jnp.float32
BF16 = jnp.bfloat16
EXACT = lax.Precision.HIGHEST

N_TABLE, N_BLOCK, N_FACE_X, N_FACE_Y, N_PACK, N_EDGE = 4, 2, 2, 2, 4, 2
A_TABLE = 0
A_BLOCK = A_TABLE + N_TABLE
A_FACE_X = A_BLOCK + N_BLOCK
A_FACE_Y = A_FACE_X + N_FACE_X
A_PACK = A_FACE_Y + N_FACE_Y
A_EDGE = A_PACK + N_PACK
A_END = A_EDGE + N_EDGE

OTHER_ROUTES = (1, 3, 0, 4)
STEPS = ((0, 0), (0, 1), (1, -1), (1, 0), (1, 1))
HALF = len(STEPS)
PAIRS = ((0, 0), (1, 1), (2, 2), (0, 1), (0, 2), (1, 2))


def iota(shape, dim):
    return lax.broadcasted_iota(jnp.int32, shape, dim)


def flag(condition):
    return jnp.where(condition, jnp.float32(1.0), jnp.float32(0.0))


def rolled(value, shift, axis):
    size = value.shape[axis]
    shift = shift % size
    return value if shift == 0 else pltpu.roll(value, shift, axis)


def halves(value):
    high = value.astype(BF16)
    return high, (value - high.astype(F32)).astype(BF16)


def near_exact(left, right):
    a, b = halves(left), halves(right)
    total = jnp.dot(a[0], b[1], preferred_element_type=F32) + jnp.dot(a[1], b[0], preferred_element_type=F32)
    return total + jnp.dot(a[0], b[0], preferred_element_type=F32)


def hats(position):
    upper = (position.astype(F32) + 0.5) / EDGE
    return 1.0 - upper, upper


def kernel(
    nx, ny, route_hbm, within_hbm, xshift_hbm, fractions_hbm, ref_hbm, dfm_hbm, inc, mis,
    route, within, xshift, fractions, ref, dfm, lsem, gossip,
    xb, tsend, trecv, fxs, fxr, fys, fyr, pmat, pacc, psend, precv, qmat, grad, refp, xrow, es, er, sg,
    kd, k1, rrow, rr, vv, hs, hr, ssem, rsem, gssem, grsem, rssem, rrsem, hssem, hrsem,
):
    p, q = lax.axis_index("gx"), lax.axis_index("gy")

    def at(dp, dq):
        return (lax.rem(p + dp + 2 * nx, nx), lax.rem(q + dq + 2 * ny, ny))

    def copy(src, dst, send_sem, recv_sem, dp, dq):
        c = pltpu.make_async_remote_copy(
            src_ref=src, dst_ref=dst, send_sem=send_sem, recv_sem=recv_sem,
            device_id=at(dp, dq), device_id_type=MESH,
        )
        c.start()
        return c

    started = []

    def send(number, src, dst, dp, dq):
        c = copy(src, dst, ssem.at[number], rsem.at[number], dp, dq)
        started.append(c)
        return c

    near = ((1, 0), (-1, 0), (0, 1), (0, -1), (0, 2), (0, -2))
    barrier = pltpu.get_barrier_semaphore()
    for dp, dq in near:
        pl.semaphore_signal(barrier, inc=1, device_id=at(dp, dq), device_id_type=MESH)
    loads = []
    for k, (src, dst) in enumerate((
        (route_hbm, route), (within_hbm, within), (xshift_hbm, xshift), (fractions_hbm, fractions),
        (ref_hbm, ref), (dfm_hbm, dfm),
    )):
        loads.append(pltpu.make_async_copy(src, dst, lsem.at[k]))
        loads[k].start()

    def tell(number, *places):
        for dp, dq in places:
            pl.semaphore_signal(gossip.at[number], inc=1, device_id=at(dp, dq), device_id_type=MESH)

    def hear(number, count):
        pl.semaphore_wait(gossip.at[number], count)

    pl.semaphore_wait(barrier, len(near))
    blocks = [send(A_BLOCK, dfm_hbm, xb.at[1], -1, 0), send(A_BLOCK + 1, dfm_hbm, xb.at[0], 1, 0)]

    lane, sub = iota((8, NY), 1), iota((8, NY), 0)
    block, inner = lane >> 4, lane & 15

    for c in loads[:3]:
        c.wait()
    routes = [route[0, 0, e] for e in range(NEL)]
    wanted = jnp.full((8, NY), -1, jnp.int32)
    count = jnp.zeros((8, NY), jnp.int32)
    for e in range(NEL):
        source = jnp.clip(p + xshift[0, 0, e] - 1, 0, nx - 1) - p + 1
        code = ((source * EZ + e // EYD) * EYD + within[0, 0, e]) * EDGE
        hit = sub == routes[e]
        wanted = jnp.where(hit & (count == block), inner + code, wanted)
        count = count + jnp.where(hit, 1, 0)
    tsend[...] = wanted
    tables = [
        send(A_TABLE + k, tsend, trecv.at[k], 0, r - SPAN) for k, r in enumerate(OTHER_ROUTES)
    ]

    loads[4].wait()
    refp[0] = jnp.zeros((32, NY), F32)
    refp[NZ + 1] = jnp.zeros((32, NY), F32)
    refp[1 : NZ + 1, 8:24, :] = ref[...].astype(F32)
    fxs[0] = refp[1 : NZ + 1, 8, :].astype(BF16)
    fxs[1] = refp[1 : NZ + 1, 23, :].astype(BF16)
    faces_x = [
        send(A_FACE_X, fxs.at[0], fxr.at[1], -1, 0),
        send(A_FACE_X + 1, fxs.at[1], fxr.at[0], 1, 0),
    ]
    rows16, lanes16 = iota((16, NY), 0), iota((16, NY), 1)
    pick = ((rows16 == 0) & (lanes16 == 0)) | ((rows16 == 1) & (lanes16 == NY - 1))
    fys[...] = lax.dot_general(
        jnp.where(pick, 1.0, 0.0).astype(BF16), ref[...].reshape(NZ * EDGE, NY),
        (((1,), (1,)), ((), ())), preferred_element_type=F32,
    ).astype(BF16)
    faces_y = [
        send(A_FACE_Y, fys, fyr.at[1], 0, -1),
        send(A_FACE_Y + 1, fys, fyr.at[0], 0, 1),
    ]

    loads[3].wait()
    element = sub * EYD + block
    own_route = jnp.zeros((8, NY), jnp.int32)
    parts = [jnp.zeros((8, NY), jnp.int32) for _ in range(3)]
    for e in range(NEL):
        here = element == e
        own_route = jnp.where(here, routes[e], own_route)
        parts = [jnp.where(here, fractions[0, c, 0, e], parts[c]) for c in range(3)]
    slot = jnp.zeros((8, NY), jnp.int32)
    for e in range(NEL):
        slot = slot + jnp.where((element > e) & (own_route == routes[e]), 1, 0)
    first = (own_route * CAP + slot) * EDGE
    portion = [part.astype(F32) / EDGE for part in parts]
    target0 = first + inner
    target1 = first + jnp.minimum(inner + 1, EDGE - 1)

    for c in faces_x:
        c.wait_recv()
    tell(0, (1, 0), (-1, 0))
    for c in faces_y:
        c.wait_recv()
    refp[1 : NZ + 1, 7, :] = fxr[0].astype(F32) * flag(p > 0)
    refp[1 : NZ + 1, 24, :] = fxr[1].astype(F32) * flag(p < nx - 1)
    here, there = iota((NY, NY), 1), iota((NY, NY), 0)
    differ = jnp.where(there == here + 1, 0.5, jnp.where(there == here - 1, -0.5, 0.0)).astype(BF16)
    rows32, lanes32 = iota((32, NY), 0), iota((32, NY), 1)
    ends = jnp.where(
        (rows32 == 1) & (lanes32 == 0), flag(q > 0) * -0.5,
        jnp.where((rows32 == 16) & (lanes32 == NY - 1), flag(q < ny - 1) * 0.5, 0.0),
    ).astype(BF16)
    sides = jnp.concatenate([fyr[0], fyr[1]], axis=0)
    along_y = jnp.dot(ref[...].reshape(NZ * EDGE, NY), differ, preferred_element_type=F32)
    along_y = along_y + lax.dot_general(sides, ends, (((0,), (0,)), ((), ())), preferred_element_type=F32)
    grad[2] = along_y.astype(BF16).reshape(NZ, EDGE, NY)

    def slope(b, _):
        base = b * 4
        below, above = refp[pl.ds(base, 4), 8:24, :], refp[pl.ds(base + 2, 4), 8:24, :]
        grad[0, pl.ds(base, 4)] = ((above - below) * 0.5).astype(BF16)
        left, right = refp[pl.ds(base + 1, 4), 7:23, :], refp[pl.ds(base + 1, 4), 9:25, :]
        grad[1, pl.ds(base, 4)] = ((right - left) * 0.5).astype(BF16)
        return 0

    lax.fori_loop(0, NZ // 4, slope, 0)

    for z in range(EZ):
        def fill_place(b, _):
            row = b * NY + iota((NY, NY), 0)
            high = portion[2][z : z + 1]
            place = jnp.where(row == target0[z : z + 1], 1.0 - high, 0.0)
            place = place + jnp.where(row == target1[z : z + 1], high, 0.0)
            qmat[pl.ds(pl.multiple_of(b * NY, NY), NY), z * NY : (z + 1) * NY] = place.astype(BF16)
            return 0

        lax.fori_loop(0, ROUTES, fill_place, 0)

    for c in tables:
        c.wait_recv()
    tell(3, (0, 4), (0, -4))
    asked = []
    for r in range(ROUTES):
        if r == SPAN:
            asked.append(wanted[r : r + 1])
        else:
            k = OTHER_ROUTES.index(r)
            asked.append(trecv[k, r : r + 1, :])
    asked = jnp.concatenate(asked, axis=1)

    def fill_pack(b, _):
        row = b * NY + iota((NY, ROUTES * NY), 0)
        pmat[pl.ds(pl.multiple_of(b * NY, NY), NY), :] = jnp.where(row == asked, 1.0, 0.0).astype(BF16)
        return 0

    lax.fori_loop(0, 3 * EZ, fill_pack, 0)

    def brick_rows(source):
        return jnp.concatenate(
            [source[z * EDGE : (z + 1) * EDGE].reshape(EDGE * EDGE, NY) for z in range(EZ)], axis=1
        )

    width = EZ * NY
    hear(0, 2)
    tell(1, (1, 0), (-1, 0))
    loads[5].wait()
    pacc[...] = jnp.dot(brick_rows(dfm), pmat[width : 2 * width, :], preferred_element_type=F32)
    blocks[1].wait_recv()
    pacc[...] += jnp.dot(brick_rows(xb[0]), pmat[0:width, :], preferred_element_type=F32)
    blocks[0].wait_recv()
    pacc[...] += jnp.dot(brick_rows(xb[1]), pmat[2 * width : 3 * width, :], preferred_element_type=F32)
    packs = []
    for k, r in enumerate(OTHER_ROUTES):
        psend[k] = pacc[:, r * NY : (r + 1) * NY].astype(BF16)
        packs.append(send(A_PACK + k, psend.at[k], precv.at[r], 0, SPAN - r))
    precv[SPAN] = pacc[:, SPAN * NY : (SPAN + 1) * NY].astype(BF16)

    hear(1, 2)
    tell(2, (1, 0), (-1, 0))
    hear(3, 2)
    tell(4, (0, 8), (0, -8))

    rowm, colm = iota((24, 96), 0), iota((24, 96), 1)
    low_x, high_x = hats(colm & 15)
    order = rowm >> 3
    weight_x = jnp.where(order == 0, low_x * low_x, jnp.where(order == 1, low_x * high_x, high_x * high_x))
    weight_x = jnp.where((rowm & 7) == (colm >> 4), weight_x, 0.0)
    weights_x = jnp.concatenate(halves(weight_x), axis=0)

    def moments(z, _):
        total = [[None] * 6 for _ in range(3)]
        for i in range(EDGE):
            g = [grad[c, z * EDGE + i].astype(F32) for c in range(3)]
            high = (i + 0.5) / EDGE
            low = 1.0 - high
            for k, (a, b) in enumerate(PAIRS):
                product = g[a] * g[b]
                for m, weight in enumerate((low * low, low * high, high * high)):
                    term = product * weight
                    total[m][k] = term if i == 0 else total[m][k] + term
        for m in range(3):
            parts = [
                jnp.dot(weights_x, part, preferred_element_type=F32)
                for part in halves(jnp.concatenate(total[m], axis=0))
            ]
            rows = (parts[1][:24] + parts[0][24:]) + parts[0][:24]
            xrow[pl.ds(pl.multiple_of((z * 3 + m) * 24, 24), 24), :] = rows
        return 0

    lax.fori_loop(0, EZ, moments, 0)
    fine, coarse = iota((NY, 3 * NY), 0), iota((NY, 3 * NY), 1)
    low_y, high_y = hats(fine & 15)
    row_y, node_y, step_y = fine >> 4, (coarse & 15) - 4, (coarse >> 7) - 1
    starts, closes = row_y == node_y, row_y + 1 == node_y
    mixed = low_y * high_y
    weight_y = jnp.where(
        step_y == 1, jnp.where(starts, mixed, 0.0),
        jnp.where(
            step_y == -1, jnp.where(closes, mixed, 0.0),
            jnp.where(starts, low_y * low_y, 0.0) + jnp.where(closes, high_y * high_y, 0.0),
        ),
    ) * (1.0 / VOL)
    yrow = near_exact(xrow[...], weight_y)
    on = [block == z for z in range(EZ + 1)]
    mine = [[None] * HALF for _ in range(3)]
    for m in range(3):
        for k, (dz, dy) in enumerate(STEPS):
            def term(z, depth):
                start = (z * 3 + depth) * 24 + m * 8
                return yrow[start : start + 8, (dy + 1) * NY : (dy + 2) * NY]

            total = jnp.zeros((8, NY), F32)
            for z in range(EZ):
                if dz == 1:
                    total = jnp.where(on[z], term(z, 1), total)
                else:
                    total = total + jnp.where(on[z], term(z, 0), 0.0) + jnp.where(on[z + 1], term(z, 2), 0.0)
            mine[m][k] = total
    for m in range(3):
        for part, ks in enumerate(((0, 1, 2), (3, 4))):
            upper, lower = jnp.zeros((8, NY), F32), jnp.zeros((8, NY), F32)
            for k in ks:
                offset = 5 * (k % 3)
                spot = (inner >= offset) & (inner < offset + 5)
                upper = jnp.where(spot, rolled(mine[m][k], offset - 8, 1), upper)
                lower = jnp.where(spot, rolled(mine[m][k], offset - 4, 1), lower)
            es[0, m * 2 + part], es[1, m * 2 + part] = upper, lower
    edges = [send(A_EDGE, es.at[0], er.at[0], 0, 1), send(A_EDGE + 1, es.at[1], er.at[1], 0, -1)]
    for c in edges:
        c.wait_recv()
    for m in range(3):
        for k in range(HALF):
            offset, part = 5 * (k % 3), k // 3
            below = jnp.where(inner < 5, rolled(er[0, m * 2 + part], -offset, 1), 0.0) * flag(q > 0)
            above = jnp.where(inner >= 12, rolled(er[1, m * 2 + part], 12 - offset, 1), 0.0) * flag(q < ny - 1)
            sg[p, m * HALF + k] = mine[m][k] + below + above
    spread = []
    for k in sorted(range(1, nx), key=lambda k: (-min(k, nx - k), k)):
        spread.append(copy(sg.at[p], sg.at[p], gssem.at[k - 1], grsem.at[k - 1], k, 0))
    started.extend(spread)

    for c in packs:
        c.wait_recv()
    taken = jnp.concatenate([precv[r] for r in range(ROUTES)], axis=1)
    column = inner - 4
    own = (column >= 0) & (column < EYD) & (block <= EZ) & (sub < 3)
    inside = (q * EYD + column < ny * EYD) & (sub < 3)
    fetched = jnp.dot(taken, qmat[...], preferred_element_type=F32)
    row8, col16 = iota((8, EDGE), 0), iota((8, EDGE), 1)
    low_j, high_j = hats(iota((EDGE, 1), 0))
    for z in range(EZ):
        voxels = fetched[:, z * NY : (z + 1) * NY].reshape(EDGE, EDGE, NY)
        high = portion[1][z : z + 1].reshape(1, 1, NY)
        ahead = jnp.concatenate([voxels[:, 1:], voxels[:, EDGE - 1 :]], axis=1)
        voxels = (1.0 - high) * voxels + high * ahead
        high = portion[0][z : z + 1].reshape(1, 1, NY)
        ahead = jnp.concatenate([voxels[1:], voxels[EDGE - 1 :]], axis=0)
        voxels = (1.0 - high) * voxels + high * ahead
        left = refp[1 + z * EDGE : 1 + (z + 1) * EDGE, 8:24, :] - voxels
        mis[z * EDGE : (z + 1) * EDGE] = left
        sums = [[None] * 3 for _ in range(2)]
        for i in range(EDGE):
            high = (i + 0.5) / EDGE
            for c in range(3):
                value = grad[c, z * EDGE + i].astype(F32) * left[i]
                for m, weight in enumerate((1.0 - high, high)):
                    sums[m][c] = value * weight if i == 0 else sums[m][c] + value * weight
        for m in range(2):
            rows = [jnp.sum(sums[m][c] * w, axis=0, keepdims=True) for w in (low_j, high_j) for c in range(3)]
            blank = jnp.zeros((1, NY), F32)
            start = (z * 2 + m) * 8
            rrow[start : start + 8, :] = jnp.concatenate(rows[:3] + [blank] + rows[3:] + [blank], axis=0)
    fine, coarse = iota((NY, NY), 0), iota((NY, NY), 1)
    low_y, high_y = hats(fine & 15)
    row_y, node_y = fine >> 4, (coarse & 15) - 4
    weight_y = (
        jnp.where(row_y == node_y, low_y, 0.0) + jnp.where(row_y + 1 == node_y, high_y, 0.0)
    ) * (1.0 / VOL)
    nodes = jnp.dot(rrow[...], weight_y, precision=EXACT, preferred_element_type=F32)
    tile = jnp.zeros((8, NY), F32)
    for z in range(EZ):
        for m in range(2):
            start = (z * 2 + m) * 8
            tile = tile + jnp.where(on[z + m], nodes[start : start + 8], 0.0)
    rr[1, p] = tile
    hear(2, 2)
    sent = []
    for k in sorted(range(nx), key=lambda k: (-min(k, nx - k), k)):
        for dq in (1, -1, 0):
            if k or dq:
                number = k * 3 + 1 - dq
                sent.append(copy(rr.at[1, p], rr.at[1 - dq, p], rssem.at[number], rrsem.at[number], k, dq))
    started.extend(sent)

    for c in spread:
        c.wait_recv()
    for x in range(nx):
        for k, (dz, dy) in enumerate(STEPS):
            level, cross = sg[x, k], sg[x, HALF + k]
            if x > 0:
                level = level + sg[x - 1, 2 * HALF + k]
            kd[x, 4 + k], k1[x, 4 + k] = level, cross
            if k:
                shift = dz * 16 + dy
                kd[x, 4 - k], k1[x, 4 - k] = rolled(level, shift, 1), rolled(cross, shift, 1)

    for c in sent:
        c.wait_recv()
    below, above = flag(q > 0), flag(q < ny - 1)
    tiles = []
    for x in range(nx):
        from_below = jnp.where(inner < 8, rolled(rr[0, x], -8, 1), 0.0) * below
        from_above = jnp.where(inner >= 8, rolled(rr[2, x], 8, 1), 0.0) * above
        tiles.append(rr[1, x] + from_below + from_above)
    for x in range(nx):
        whole = tiles[x] + rolled(tiles[x - 1], 4, 0) if x else tiles[x]
        vv[0, x] = jnp.where(inside, whole, 0.0)

    for step in range(3):
        straight = [jnp.zeros((8, NY), F32) for _ in range(nx)]
        crossed = [jnp.zeros((8, NY), F32) for _ in range(nx)]
        for x in range(nx):
            u = [vv[step, x, c : c + 1, :] for c in range(3)]
            second = jnp.where(sub == 0, u[0], jnp.where((sub == 1) | (sub == 3), u[1], u[2]))
            third = jnp.where(sub == 5, u[1], u[0])
            for t in range(9):
                shift = -((t // 3 - 1) * 16 + t % 3 - 1)
                moved, other = rolled(second, shift, 1), rolled(third, shift, 1)
                level, cross = kd[x, t], k1[x, t]
                straight[x] = straight[x] + level * moved
                crossed[x] = crossed[x] + level * other
                if x + 1 < nx:
                    straight[x + 1] = straight[x + 1] + cross * moved
                    crossed[x + 1] = crossed[x + 1] + cross * other
                if x > 0:
                    before = k1[x - 1, t]
                    straight[x - 1] = straight[x - 1] + before * moved
                    crossed[x - 1] = crossed[x - 1] + before * other
        for x in range(nx):
            a, b = straight[x], crossed[x]
            out = [
                a[0:1] + a[3:4] + a[4:5],
                a[1:2] + a[5:6] + b[3:4],
                a[2:3] + b[4:5] + b[5:6],
            ]
            image = jnp.where(sub == 0, out[0], jnp.where(sub == 1, out[1], out[2]))
            vv[step + 1, x] = jnp.where(inside, image + LAMBDA * vv[step, x], 0.0)

    tile = jnp.zeros((8, NY), F32)
    for k in range(6):
        product = jnp.zeros((8, NY), F32)
        for x in range(nx):
            product = product + vv[k // 2, x] * vv[(k + 1) // 2, x]
        product = jnp.sum(jnp.where(own, product, 0.0), axis=0, keepdims=True)
        tile = jnp.where(sub == k, product, tile)
    hear(4, 2)

    hs[...] = tile

    def to_y(k, _):
        copy(hs, hr.at[k - 1], hssem.at[k - 1], hrsem.at[k - 1], 0, k)
        return 0

    def from_y(k, total):
        pltpu.make_async_remote_copy(
            src_ref=hs, dst_ref=hr.at[k - 1], send_sem=hssem.at[k - 1], recv_sem=hrsem.at[k - 1],
            device_id=at(0, k), device_id_type=MESH,
        ).wait()
        return total + hr[k - 1]

    for k in sorted(range(1, ny), key=lambda k: (-min(k, ny - k), k)):
        to_y(k, 0)
    for k in range(1, ny):
        tile = from_y(k, tile)
    total = jnp.broadcast_to(jnp.sum(tile, axis=1, keepdims=True), (8, NY))
    moment = [total[k : k + 1] for k in range(6)]

    def product(a, b, more):
        value = 0.0
        for i, left in enumerate(a):
            for j, right in enumerate(b):
                value = value + left * right * moment[i + j + more]
        return value

    blank, unit = jnp.zeros((1, NY), F32), jnp.ones((1, NY), F32)
    answer, residual, direction = [blank] * 3, [unit], [unit]
    norm = moment[0]
    for step in range(3):
        bend = product(direction, direction, 1)
        alpha = norm / bend
        answer = [answer[i] + alpha * direction[i] if i < len(direction) else answer[i] for i in range(3)]
        if step < 2:
            grown = residual + [blank]
            residual = [
                grown[i] - alpha * direction[i - 1] if i > 0 else grown[i] for i in range(step + 2)
            ]
            after = product(residual, residual, 0)
            beta = after / norm
            norm = after
            widened = direction + [blank]
            direction = [residual[i] + beta * widened[i] for i in range(step + 2)]
    inc[...] = answer[0] * vv[0, p] + answer[1] * vv[1, p] + answer[2] * vv[2, p]
    for c in started:
        c.wait_send()


def body(nx, ny, reference_image, deformed_image, route, within, xshift, fractions):
    vmem = pl.BlockSpec(memory_space=pltpu.VMEM)
    half = (NZ, EDGE, NY)
    tile = (8, NY)
    inc, mis = pl.pallas_call(
        lambda *refs: kernel(nx, ny, *refs),
        name="correlate",
        out_shape=(jax.ShapeDtypeStruct(tile, F32), jax.ShapeDtypeStruct(half, F32)),
        in_specs=[pl.BlockSpec(memory_space=pltpu.HBM)] * 6,
        out_specs=(vmem, vmem),
        scratch_shapes=[
            pltpu.SMEM((1, 1, NEL), jnp.int32),
            pltpu.SMEM((1, 1, NEL), jnp.int32),
            pltpu.SMEM((1, 1, NEL), jnp.int32),
            pltpu.SMEM((1, 3, 1, NEL), jnp.int32),
            pltpu.VMEM(half, BF16),
            pltpu.VMEM(half, BF16),
            pltpu.SemaphoreType.DMA((6,)),
            pltpu.SemaphoreType.REGULAR((5,)),
            pltpu.VMEM((2,) + half, BF16),
            pltpu.VMEM(tile, jnp.int32),
            pltpu.VMEM((4,) + tile, jnp.int32),
            pltpu.VMEM((2, NZ, NY), BF16),
            pltpu.VMEM((2, NZ, NY), BF16),
            pltpu.VMEM((16, NZ * EDGE), BF16),
            pltpu.VMEM((2, 16, NZ * EDGE), BF16),
            pltpu.VMEM((3 * EZ * NY, ROUTES * NY), BF16),
            pltpu.VMEM((EDGE * EDGE, ROUTES * NY), F32),
            pltpu.VMEM((4, EDGE * EDGE, NY), BF16),
            pltpu.VMEM((ROUTES, EDGE * EDGE, NY), BF16),
            pltpu.VMEM((ROUTES * NY, EZ * NY), BF16),
            pltpu.VMEM((3,) + half, BF16),
            pltpu.VMEM((NZ + 2, 32, NY), F32),
            pltpu.VMEM((12 * 24, NY), F32),
            pltpu.VMEM((2, 6) + tile, F32),
            pltpu.VMEM((2, 6) + tile, F32),
            pltpu.VMEM((nx, 3 * HALF) + tile, F32),
            pltpu.VMEM((nx, 9) + tile, F32),
            pltpu.VMEM((nx, 9) + tile, F32),
            pltpu.VMEM((64, NY), F32),
            pltpu.VMEM((3, nx) + tile, F32),
            pltpu.VMEM((4, nx) + tile, F32),
            pltpu.VMEM(tile, F32),
            pltpu.VMEM((ny - 1,) + tile, F32),
            pltpu.SemaphoreType.DMA((A_END,)),
            pltpu.SemaphoreType.DMA((A_END,)),
            pltpu.SemaphoreType.DMA((nx - 1,)),
            pltpu.SemaphoreType.DMA((nx - 1,)),
            pltpu.SemaphoreType.DMA((3 * nx,)),
            pltpu.SemaphoreType.DMA((3 * nx,)),
            pltpu.SemaphoreType.DMA((ny - 1,)),
            pltpu.SemaphoreType.DMA((ny - 1,)),
        ],
        compiler_params=pltpu.CompilerParams(
            collective_id=0, has_side_effects=True, vmem_limit_bytes=63 << 20
        ),
    )(route.reshape(1, 1, NEL), within, xshift, fractions.transpose(0, 3, 1, 2), reference_image, deformed_image)
    grid = inc[:3].reshape(3, 8, 16)
    return grid[:, : EZ + 1, None, 4 : 4 + EYD], mis


def solution(mesh):
    nx, ny = mesh.shape["gx"], mesh.shape["gy"]
    placed = (
        P(None, "gx", "gy"),
        P(None, "gx", "gy"),
        P("gx", "gy", None, None),
        P("gx", "gy", None),
        P("gx", "gy", None),
        P("gx", "gy", None, None),
    )
    return jax.shard_map(
        lambda *blocks: body(nx, ny, *blocks),
        mesh=mesh,
        in_specs=placed,
        out_specs=(P(None, None, "gx", "gy"), P(None, "gx", "gy")),
        check_vma=False,
    )
```

```python
import jax
import jax.numpy as jnp
from jax import lax
from jax.experimental import pallas as pl
from jax.experimental.pallas import tpu as pltpu
from jax.sharding import PartitionSpec as P

EDGE = 16
EZ = 4
EYD = 8
SPAN = 2
ROUTES = 2 * SPAN + 1
NEL = 32
CAP = 8
VOL = 4096
NZ = 64
NY = 128
LAMBDA = 0.05
MESH = pl.DeviceIdType.MESH
F32 = jnp.float32
BF16 = jnp.bfloat16
EXACT = lax.Precision.HIGHEST

N_TABLE, N_BLOCK, N_FACE_X, N_FACE_Y, N_PACK, N_EDGE = 4, 2, 2, 2, 4, 2
A_TABLE = 0
A_BLOCK = A_TABLE + N_TABLE
A_FACE_X = A_BLOCK + N_BLOCK
A_FACE_Y = A_FACE_X + N_FACE_X
A_PACK = A_FACE_Y + N_FACE_Y
A_EDGE = A_PACK + N_PACK
A_END = A_EDGE + N_EDGE

OTHER_ROUTES = (0, 4, 1, 3)
STEPS = ((0, 0), (0, 1), (1, -1), (1, 0), (1, 1))
HALF = len(STEPS)
PAIRS = ((0, 0), (1, 1), (2, 2), (0, 1), (0, 2), (1, 2))


def iota(shape, dim):
    return lax.broadcasted_iota(jnp.int32, shape, dim)


def flag(condition):
    return jnp.where(condition, jnp.float32(1.0), jnp.float32(0.0))


def rolled(value, shift, axis):
    size = value.shape[axis]
    shift = shift % size
    return value if shift == 0 else pltpu.roll(value, shift, axis)


def halves(value):
    high = value.astype(BF16)
    return high, (value - high.astype(F32)).astype(BF16)


def near_exact(left, right):
    a, b = halves(left), halves(right)
    total = jnp.dot(a[0], b[1], preferred_element_type=F32) + jnp.dot(a[1], b[0], preferred_element_type=F32)
    return total + jnp.dot(a[0], b[0], preferred_element_type=F32)


def hats(position):
    upper = (position.astype(F32) + 0.5) / EDGE
    return 1.0 - upper, upper


def kernel(
    nx, ny, route_hbm, within_hbm, xshift_hbm, fractions_hbm, ref_hbm, dfm_hbm, inc, mis,
    route, within, xshift, fractions, ref, dfm, lsem, gossip,
    xb, tsend, trecv, fxs, fxr, fys, fyr, pmat, pacc, psend, precv, qmat, grad, refp, xrow, es, er, sg,
    kd, k1, rrow, rr, vv, hs, hr, ssem, rsem, gssem, grsem, rssem, rrsem, hssem, hrsem,
):
    p, q = lax.axis_index("gx"), lax.axis_index("gy")

    def at(dp, dq):
        return (lax.rem(p + dp + 2 * nx, nx), lax.rem(q + dq + 2 * ny, ny))

    def copy(src, dst, send_sem, recv_sem, dp, dq):
        c = pltpu.make_async_remote_copy(
            src_ref=src, dst_ref=dst, send_sem=send_sem, recv_sem=recv_sem,
            device_id=at(dp, dq), device_id_type=MESH,
        )
        c.start()
        return c

    started = []

    def send(number, src, dst, dp, dq):
        c = copy(src, dst, ssem.at[number], rsem.at[number], dp, dq)
        started.append(c)
        return c

    near = ((1, 0), (-1, 0), (0, 1), (0, -1), (0, 2), (0, -2))
    barrier = pltpu.get_barrier_semaphore()
    for dp, dq in near:
        pl.semaphore_signal(barrier, inc=1, device_id=at(dp, dq), device_id_type=MESH)
    loads = []
    for k, (src, dst) in enumerate((
        (route_hbm, route), (within_hbm, within), (xshift_hbm, xshift), (fractions_hbm, fractions),
        (ref_hbm, ref), (dfm_hbm, dfm),
    )):
        loads.append(pltpu.make_async_copy(src, dst, lsem.at[k]))
        loads[k].start()

    def tell(number, *places):
        for dp, dq in places:
            pl.semaphore_signal(gossip.at[number], inc=1, device_id=at(dp, dq), device_id_type=MESH)

    def hear(number, count):
        pl.semaphore_wait(gossip.at[number], count)

    lane, sub = iota((8, NY), 1), iota((8, NY), 0)
    block, inner = lane >> 4, lane & 15

    for c in loads[:3]:
        c.wait()
    routes = [route[0, 0, e] for e in range(NEL)]
    wanted = jnp.full((8, NY), -1, jnp.int32)
    count = jnp.zeros((8, NY), jnp.int32)
    for e in range(NEL):
        source = jnp.clip(p + xshift[0, 0, e] - 1, 0, nx - 1) - p + 1
        code = ((source * EZ + e // EYD) * EYD + within[0, 0, e]) * EDGE
        hit = sub == routes[e]
        wanted = jnp.where(hit & (count == block), inner + code, wanted)
        count = count + jnp.where(hit, 1, 0)
    tsend[...] = wanted

    loads[4].wait()
    refp[0] = jnp.zeros((32, NY), F32)
    refp[NZ + 1] = jnp.zeros((32, NY), F32)
    refp[1 : NZ + 1, 8:24, :] = ref[...].astype(F32)
    fxs[0] = refp[1 : NZ + 1, 8, :].astype(BF16)
    fxs[1] = refp[1 : NZ + 1, 23, :].astype(BF16)
    rows16, lanes16 = iota((16, NY), 0), iota((16, NY), 1)
    pick = ((rows16 == 0) & (lanes16 == 0)) | ((rows16 == 1) & (lanes16 == NY - 1))
    fys[...] = lax.dot_general(
        jnp.where(pick, 1.0, 0.0).astype(BF16), ref[...].reshape(NZ * EDGE, NY),
        (((1,), (1,)), ((), ())), preferred_element_type=F32,
    ).astype(BF16)

    pl.semaphore_wait(barrier, len(near))
    faces_y = [
        send(A_FACE_Y, fys, fyr.at[1], 0, -1),
        send(A_FACE_Y + 1, fys, fyr.at[0], 0, 1),
    ]
    tables = [
        send(A_TABLE + k, tsend, trecv.at[k], 0, r - SPAN) for k, r in enumerate(OTHER_ROUTES)
    ]
    faces_x = [
        send(A_FACE_X, fxs.at[0], fxr.at[1], -1, 0),
        send(A_FACE_X + 1, fxs.at[1], fxr.at[0], 1, 0),
    ]
    blocks = [send(A_BLOCK, dfm_hbm, xb.at[1], -1, 0), send(A_BLOCK + 1, dfm_hbm, xb.at[0], 1, 0)]

    loads[3].wait()
    element = sub * EYD + block
    own_route = jnp.zeros((8, NY), jnp.int32)
    parts = [jnp.zeros((8, NY), jnp.int32) for _ in range(3)]
    for e in range(NEL):
        here = element == e
        own_route = jnp.where(here, routes[e], own_route)
        parts = [jnp.where(here, fractions[0, c, 0, e], parts[c]) for c in range(3)]
    slot = jnp.zeros((8, NY), jnp.int32)
    for e in range(NEL):
        slot = slot + jnp.where((element > e) & (own_route == routes[e]), 1, 0)
    first = (own_route * CAP + slot) * EDGE
    portion = [part.astype(F32) / EDGE for part in parts]
    target0 = first + inner
    target1 = first + jnp.minimum(inner + 1, EDGE - 1)

    for z in range(EZ):
        def fill_place(b, _):
            row = b * NY + iota((NY, NY), 0)
            high = portion[2][z : z + 1]
            place = jnp.where(row == target0[z : z + 1], 1.0 - high, 0.0)
            place = place + jnp.where(row == target1[z : z + 1], high, 0.0)
            qmat[pl.ds(pl.multiple_of(b * NY, NY), NY), z * NY : (z + 1) * NY] = place.astype(BF16)
            return 0

        lax.fori_loop(0, ROUTES, fill_place, 0)

    for c in tables:
        c.wait_recv()
    tell(3, (0, 4), (0, -4))
    asked = []
    for r in range(ROUTES):
        if r == SPAN:
            asked.append(wanted[r : r + 1])
        else:
            k = OTHER_ROUTES.index(r)
            asked.append(trecv[k, r : r + 1, :])
    asked = jnp.concatenate(asked, axis=1)

    def fill_pack(b, _):
        row = b * NY + iota((NY, ROUTES * NY), 0)
        pmat[pl.ds(pl.multiple_of(b * NY, NY), NY), :] = jnp.where(row == asked, 1.0, 0.0).astype(BF16)
        return 0

    lax.fori_loop(0, 3 * EZ, fill_pack, 0)

    def brick_rows(source):
        return jnp.concatenate(
            [source[z * EDGE : (z + 1) * EDGE].reshape(EDGE * EDGE, NY) for z in range(EZ)], axis=1
        )

    width = EZ * NY
    loads[5].wait()
    pacc[...] = jnp.dot(brick_rows(dfm), pmat[width : 2 * width, :], preferred_element_type=F32)

    for c in faces_x:
        c.wait_recv()
    tell(0, (1, 0), (-1, 0))
    for c in faces_y:
        c.wait_recv()
    refp[1 : NZ + 1, 7, :] = fxr[0].astype(F32) * flag(p > 0)
    refp[1 : NZ + 1, 24, :] = fxr[1].astype(F32) * flag(p < nx - 1)
    here, there = iota((NY, NY), 1), iota((NY, NY), 0)
    differ = jnp.where(there == here + 1, 0.5, jnp.where(there == here - 1, -0.5, 0.0)).astype(BF16)
    rows32, lanes32 = iota((32, NY), 0), iota((32, NY), 1)
    ends = jnp.where(
        (rows32 == 1) & (lanes32 == 0), flag(q > 0) * -0.5,
        jnp.where((rows32 == 16) & (lanes32 == NY - 1), flag(q < ny - 1) * 0.5, 0.0),
    ).astype(BF16)
    sides = jnp.concatenate([fyr[0], fyr[1]], axis=0)
    along_y = jnp.dot(ref[...].reshape(NZ * EDGE, NY), differ, preferred_element_type=F32)
    along_y = along_y + lax.dot_general(sides, ends, (((0,), (0,)), ((), ())), preferred_element_type=F32)
    grad[2] = along_y.astype(BF16).reshape(NZ, EDGE, NY)

    def slope(b, _):
        base = b * 4
        below, above = refp[pl.ds(base, 4), 8:24, :], refp[pl.ds(base + 2, 4), 8:24, :]
        grad[0, pl.ds(base, 4)] = ((above - below) * 0.5).astype(BF16)
        left, right = refp[pl.ds(base + 1, 4), 7:23, :], refp[pl.ds(base + 1, 4), 9:25, :]
        grad[1, pl.ds(base, 4)] = ((right - left) * 0.5).astype(BF16)
        return 0

    lax.fori_loop(0, NZ // 4, slope, 0)

    rowm, colm = iota((24, 96), 0), iota((24, 96), 1)
    low_x, high_x = hats(colm & 15)
    order = rowm >> 3
    weight_x = jnp.where(order == 0, low_x * low_x, jnp.where(order == 1, low_x * high_x, high_x * high_x))
    weight_x = jnp.where((rowm & 7) == (colm >> 4), weight_x, 0.0)
    weights_x = jnp.concatenate(halves(weight_x), axis=0)

    def moments(z, _):
        total = [[None] * 6 for _ in range(3)]
        for i in range(EDGE):
            g = [grad[c, z * EDGE + i].astype(F32) for c in range(3)]
            high = (i + 0.5) / EDGE
            low = 1.0 - high
            for k, (a, b) in enumerate(PAIRS):
                product = g[a] * g[b]
                for m, weight in enumerate((low * low, low * high, high * high)):
                    term = product * weight
                    total[m][k] = term if i == 0 else total[m][k] + term
        for m in range(3):
            parts = [
                jnp.dot(weights_x, part, preferred_element_type=F32)
                for part in halves(jnp.concatenate(total[m], axis=0))
            ]
            rows = (parts[1][:24] + parts[0][24:]) + parts[0][:24]
            xrow[pl.ds(pl.multiple_of((z * 3 + m) * 24, 24), 24), :] = rows
        return 0

    lax.fori_loop(0, EZ, moments, 0)
    fine, coarse = iota((NY, 3 * NY), 0), iota((NY, 3 * NY), 1)
    low_y, high_y = hats(fine & 15)
    row_y, node_y, step_y = fine >> 4, (coarse & 15) - 4, (coarse >> 7) - 1
    starts, closes = row_y == node_y, row_y + 1 == node_y
    mixed = low_y * high_y
    weight_y = jnp.where(
        step_y == 1, jnp.where(starts, mixed, 0.0),
        jnp.where(
            step_y == -1, jnp.where(closes, mixed, 0.0),
            jnp.where(starts, low_y * low_y, 0.0) + jnp.where(closes, high_y * high_y, 0.0),
        ),
    ) * (1.0 / VOL)
    yrow = near_exact(xrow[...], weight_y)
    on = [block == z for z in range(EZ + 1)]
    mine = [[None] * HALF for _ in range(3)]
    for m in range(3):
        for k, (dz, dy) in enumerate(STEPS):
            def term(z, depth):
                start = (z * 3 + depth) * 24 + m * 8
                return yrow[start : start + 8, (dy + 1) * NY : (dy + 2) * NY]

            total = jnp.zeros((8, NY), F32)
            for z in range(EZ):
                if dz == 1:
                    total = jnp.where(on[z], term(z, 1), total)
                else:
                    total = total + jnp.where(on[z], term(z, 0), 0.0) + jnp.where(on[z + 1], term(z, 2), 0.0)
            mine[m][k] = total
    for m in range(3):
        for part, ks in enumerate(((0, 1, 2), (3, 4))):
            upper, lower = jnp.zeros((8, NY), F32), jnp.zeros((8, NY), F32)
            for k in ks:
                offset = 5 * (k % 3)
                spot = (inner >= offset) & (inner < offset + 5)
                upper = jnp.where(spot, rolled(mine[m][k], offset - 8, 1), upper)
                lower = jnp.where(spot, rolled(mine[m][k], offset - 4, 1), lower)
            es[0, m * 2 + part], es[1, m * 2 + part] = upper, lower
    edges = [send(A_EDGE, es.at[0], er.at[0], 0, 1), send(A_EDGE + 1, es.at[1], er.at[1], 0, -1)]
    hear(0, 2)
    tell(1, (1, 0), (-1, 0))
    blocks[1].wait_recv()
    pacc[...] += jnp.dot(brick_rows(xb[0]), pmat[0:width, :], preferred_element_type=F32)
    blocks[0].wait_recv()
    pacc[...] += jnp.dot(brick_rows(xb[1]), pmat[2 * width : 3 * width, :], preferred_element_type=F32)
    packs = []
    for k, r in enumerate(OTHER_ROUTES):
        psend[k] = pacc[:, r * NY : (r + 1) * NY].astype(BF16)
        packs.append(send(A_PACK + k, psend.at[k], precv.at[r], 0, SPAN - r))
    precv[SPAN] = pacc[:, SPAN * NY : (SPAN + 1) * NY].astype(BF16)
    hear(1, 2)
    tell(2, (1, 0), (-1, 0))
    hear(3, 2)
    tell(4, (0, 8), (0, -8))

    for c in edges:
        c.wait_recv()
    for m in range(3):
        for k in range(HALF):
            offset, part = 5 * (k % 3), k // 3
            below = jnp.where(inner < 5, rolled(er[0, m * 2 + part], -offset, 1), 0.0) * flag(q > 0)
            above = jnp.where(inner >= 12, rolled(er[1, m * 2 + part], 12 - offset, 1), 0.0) * flag(q < ny - 1)
            sg[p, m * HALF + k] = mine[m][k] + below + above
    spread = []
    for k in sorted(range(1, nx), key=lambda k: (-min(k, nx - k), k)):
        spread.append(copy(sg.at[p], sg.at[p], gssem.at[k - 1], grsem.at[k - 1], k, 0))
    started.extend(spread)

    for c in packs:
        c.wait_recv()
    taken = jnp.concatenate([precv[r] for r in range(ROUTES)], axis=1)
    column = inner - 4
    own = (column >= 0) & (column < EYD) & (block <= EZ) & (sub < 3)
    inside = (q * EYD + column < ny * EYD) & (sub < 3)
    fetched = jnp.dot(taken, qmat[...], preferred_element_type=F32)
    row8, col16 = iota((8, EDGE), 0), iota((8, EDGE), 1)
    low_j, high_j = hats(iota((EDGE, 1), 0))
    for z in range(EZ):
        voxels = fetched[:, z * NY : (z + 1) * NY].reshape(EDGE, EDGE, NY)
        high = portion[1][z : z + 1].reshape(1, 1, NY)
        ahead = jnp.concatenate([voxels[:, 1:], voxels[:, EDGE - 1 :]], axis=1)
        voxels = (1.0 - high) * voxels + high * ahead
        high = portion[0][z : z + 1].reshape(1, 1, NY)
        ahead = jnp.concatenate([voxels[1:], voxels[EDGE - 1 :]], axis=0)
        voxels = (1.0 - high) * voxels + high * ahead
        left = refp[1 + z * EDGE : 1 + (z + 1) * EDGE, 8:24, :] - voxels
        mis[z * EDGE : (z + 1) * EDGE] = left
        sums = [[None] * 3 for _ in range(2)]
        for i in range(EDGE):
            high = (i + 0.5) / EDGE
            for c in range(3):
                value = grad[c, z * EDGE + i].astype(F32) * left[i]
                for m, weight in enumerate((1.0 - high, high)):
                    sums[m][c] = value * weight if i == 0 else sums[m][c] + value * weight
        for m in range(2):
            rows = [jnp.sum(sums[m][c] * w, axis=0, keepdims=True) for w in (low_j, high_j) for c in range(3)]
            blank = jnp.zeros((1, NY), F32)
            start = (z * 2 + m) * 8
            rrow[start : start + 8, :] = jnp.concatenate(rows[:3] + [blank] + rows[3:] + [blank], axis=0)
    fine, coarse = iota((NY, NY), 0), iota((NY, NY), 1)
    low_y, high_y = hats(fine & 15)
    row_y, node_y = fine >> 4, (coarse & 15) - 4
    weight_y = (
        jnp.where(row_y == node_y, low_y, 0.0) + jnp.where(row_y + 1 == node_y, high_y, 0.0)
    ) * (1.0 / VOL)
    nodes = jnp.dot(rrow[...], weight_y, precision=EXACT, preferred_element_type=F32)
    tile = jnp.zeros((8, NY), F32)
    for z in range(EZ):
        for m in range(2):
            start = (z * 2 + m) * 8
            tile = tile + jnp.where(on[z + m], nodes[start : start + 8], 0.0)
    rr[1, p] = tile
    hear(2, 2)
    sent = []
    for k in sorted(range(nx), key=lambda k: (-min(k, nx - k), k)):
        for dq in (1, -1, 0):
            if k or dq:
                number = k * 3 + 1 - dq
                sent.append(copy(rr.at[1, p], rr.at[1 - dq, p], rssem.at[number], rrsem.at[number], k, dq))
    started.extend(sent)

    for c in spread:
        c.wait_recv()
    for x in range(nx):
        for k, (dz, dy) in enumerate(STEPS):
            level, cross = sg[x, k], sg[x, HALF + k]
            if x > 0:
                level = level + sg[x - 1, 2 * HALF + k]
            kd[x, 4 + k], k1[x, 4 + k] = level, cross
            if k:
                shift = dz * 16 + dy
                kd[x, 4 - k], k1[x, 4 - k] = rolled(level, shift, 1), rolled(cross, shift, 1)

    for c in sent:
        c.wait_recv()
    below, above = flag(q > 0), flag(q < ny - 1)
    tiles = []
    for x in range(nx):
        from_below = jnp.where(inner < 8, rolled(rr[0, x], -8, 1), 0.0) * below
        from_above = jnp.where(inner >= 8, rolled(rr[2, x], 8, 1), 0.0) * above
        tiles.append(rr[1, x] + from_below + from_above)
    for x in range(nx):
        whole = tiles[x] + rolled(tiles[x - 1], 4, 0) if x else tiles[x]
        vv[0, x] = jnp.where(inside, whole, 0.0)

    for step in range(3):
        straight = [jnp.zeros((8, NY), F32) for _ in range(nx)]
        crossed = [jnp.zeros((8, NY), F32) for _ in range(nx)]
        for x in range(nx):
            u = [vv[step, x, c : c + 1, :] for c in range(3)]
            second = jnp.where(sub == 0, u[0], jnp.where((sub == 1) | (sub == 3), u[1], u[2]))
            third = jnp.where(sub == 5, u[1], u[0])
            for t in range(9):
                shift = -((t // 3 - 1) * 16 + t % 3 - 1)
                moved, other = rolled(second, shift, 1), rolled(third, shift, 1)
                level, cross = kd[x, t], k1[x, t]
                straight[x] = straight[x] + level * moved
                crossed[x] = crossed[x] + level * other
                if x + 1 < nx:
                    straight[x + 1] = straight[x + 1] + cross * moved
                    crossed[x + 1] = crossed[x + 1] + cross * other
                if x > 0:
                    before = k1[x - 1, t]
                    straight[x - 1] = straight[x - 1] + before * moved
                    crossed[x - 1] = crossed[x - 1] + before * other
        for x in range(nx):
            a, b = straight[x], crossed[x]
            out = [
                a[0:1] + a[3:4] + a[4:5],
                a[1:2] + a[5:6] + b[3:4],
                a[2:3] + b[4:5] + b[5:6],
            ]
            image = jnp.where(sub == 0, out[0], jnp.where(sub == 1, out[1], out[2]))
            vv[step + 1, x] = jnp.where(inside, image + LAMBDA * vv[step, x], 0.0)

    tile = jnp.zeros((8, NY), F32)
    for k in range(6):
        product = jnp.zeros((8, NY), F32)
        for x in range(nx):
            product = product + vv[k // 2, x] * vv[(k + 1) // 2, x]
        product = jnp.sum(jnp.where(own, product, 0.0), axis=0, keepdims=True)
        tile = jnp.where(sub == k, product, tile)
    hear(4, 2)

    hs[...] = tile

    def to_y(k, _):
        copy(hs, hr.at[k - 1], hssem.at[k - 1], hrsem.at[k - 1], 0, k)
        return 0

    def from_y(k, total):
        pltpu.make_async_remote_copy(
            src_ref=hs, dst_ref=hr.at[k - 1], send_sem=hssem.at[k - 1], recv_sem=hrsem.at[k - 1],
            device_id=at(0, k), device_id_type=MESH,
        ).wait()
        return total + hr[k - 1]

    for k in sorted(range(1, ny), key=lambda k: (-min(k, ny - k), k)):
        to_y(k, 0)
    for k in range(1, ny):
        tile = from_y(k, tile)
    total = jnp.broadcast_to(jnp.sum(tile, axis=1, keepdims=True), (8, NY))
    moment = [total[k : k + 1] for k in range(6)]

    def product(a, b, more):
        value = 0.0
        for i, left in enumerate(a):
            for j, right in enumerate(b):
                value = value + left * right * moment[i + j + more]
        return value

    blank, unit = jnp.zeros((1, NY), F32), jnp.ones((1, NY), F32)
    answer, residual, direction = [blank] * 3, [unit], [unit]
    norm = moment[0]
    for step in range(3):
        bend = product(direction, direction, 1)
        alpha = norm / bend
        answer = [answer[i] + alpha * direction[i] if i < len(direction) else answer[i] for i in range(3)]
        if step < 2:
            grown = residual + [blank]
            residual = [
                grown[i] - alpha * direction[i - 1] if i > 0 else grown[i] for i in range(step + 2)
            ]
            after = product(residual, residual, 0)
            beta = after / norm
            norm = after
            widened = direction + [blank]
            direction = [residual[i] + beta * widened[i] for i in range(step + 2)]
    inc[...] = answer[0] * vv[0, p] + answer[1] * vv[1, p] + answer[2] * vv[2, p]
    for c in started:
        c.wait_send()


def body(nx, ny, reference_image, deformed_image, route, within, xshift, fractions):
    vmem = pl.BlockSpec(memory_space=pltpu.VMEM)
    half = (NZ, EDGE, NY)
    tile = (8, NY)
    inc, mis = pl.pallas_call(
        lambda *refs: kernel(nx, ny, *refs),
        name="correlate",
        out_shape=(jax.ShapeDtypeStruct(tile, F32), jax.ShapeDtypeStruct(half, F32)),
        in_specs=[pl.BlockSpec(memory_space=pltpu.HBM)] * 6,
        out_specs=(vmem, vmem),
        scratch_shapes=[
            pltpu.SMEM((1, 1, NEL), jnp.int32),
            pltpu.SMEM((1, 1, NEL), jnp.int32),
            pltpu.SMEM((1, 1, NEL), jnp.int32),
            pltpu.SMEM((1, 3, 1, NEL), jnp.int32),
            pltpu.VMEM(half, BF16),
            pltpu.VMEM(half, BF16),
            pltpu.SemaphoreType.DMA((6,)),
            pltpu.SemaphoreType.REGULAR((5,)),
            pltpu.VMEM((2,) + half, BF16),
            pltpu.VMEM(tile, jnp.int32),
            pltpu.VMEM((4,) + tile, jnp.int32),
            pltpu.VMEM((2, NZ, NY), BF16),
            pltpu.VMEM((2, NZ, NY), BF16),
            pltpu.VMEM((16, NZ * EDGE), BF16),
            pltpu.VMEM((2, 16, NZ * EDGE), BF16),
            pltpu.VMEM((3 * EZ * NY, ROUTES * NY), BF16),
            pltpu.VMEM((EDGE * EDGE, ROUTES * NY), F32),
            pltpu.VMEM((4, EDGE * EDGE, NY), BF16),
            pltpu.VMEM((ROUTES, EDGE * EDGE, NY), BF16),
            pltpu.VMEM((ROUTES * NY, EZ * NY), BF16),
            pltpu.VMEM((3,) + half, BF16),
            pltpu.VMEM((NZ + 2, 32, NY), F32),
            pltpu.VMEM((12 * 24, NY), F32),
            pltpu.VMEM((2, 6) + tile, F32),
            pltpu.VMEM((2, 6) + tile, F32),
            pltpu.VMEM((nx, 3 * HALF) + tile, F32),
            pltpu.VMEM((nx, 9) + tile, F32),
            pltpu.VMEM((nx, 9) + tile, F32),
            pltpu.VMEM((64, NY), F32),
            pltpu.VMEM((3, nx) + tile, F32),
            pltpu.VMEM((4, nx) + tile, F32),
            pltpu.VMEM(tile, F32),
            pltpu.VMEM((ny - 1,) + tile, F32),
            pltpu.SemaphoreType.DMA((A_END,)),
            pltpu.SemaphoreType.DMA((A_END,)),
            pltpu.SemaphoreType.DMA((nx - 1,)),
            pltpu.SemaphoreType.DMA((nx - 1,)),
            pltpu.SemaphoreType.DMA((3 * nx,)),
            pltpu.SemaphoreType.DMA((3 * nx,)),
            pltpu.SemaphoreType.DMA((ny - 1,)),
            pltpu.SemaphoreType.DMA((ny - 1,)),
        ],
        compiler_params=pltpu.CompilerParams(
            collective_id=0, has_side_effects=True, vmem_limit_bytes=63 << 20
        ),
    )(route.reshape(1, 1, NEL), within, xshift, fractions.transpose(0, 3, 1, 2), reference_image, deformed_image)
    grid = inc[:3].reshape(3, 8, 16)
    return grid[:, : EZ + 1, None, 4 : 4 + EYD], mis


def solution(mesh):
    nx, ny = mesh.shape["gx"], mesh.shape["gy"]
    placed = (
        P(None, "gx", "gy"),
        P(None, "gx", "gy"),
        P("gx", "gy", None, None),
        P("gx", "gy", None),
        P("gx", "gy", None),
        P("gx", "gy", None, None),
    )
    return jax.shard_map(
        lambda *blocks: body(nx, ny, *blocks),
        mesh=mesh,
        in_specs=placed,
        out_specs=(P(None, None, "gx", "gy"), P(None, "gx", "gy")),
        check_vma=False,
    )
```

```python
import jax
import jax.numpy as jnp
import numpy as np
from jax import lax
from jax.experimental import pallas as pl
from jax.experimental.pallas import tpu as pltpu
from jax.sharding import PartitionSpec as P

EDGE = 16
EZ = 4
EYD = 8
SPAN = 2
ROUTES = 2 * SPAN + 1
NEL = 32
CAP = 8
VOL = 4096
NZ = 64
NY = 128
LAMBDA = 0.05
LAMBDA_PARTS = (float(np.float32(LAMBDA)), 0.0)
MESH = pl.DeviceIdType.MESH
F32 = jnp.float32
BF16 = jnp.bfloat16
EXACT = lax.Precision.HIGHEST

N_TABLE, N_BLOCK, N_FACE_X, N_FACE_Y, N_PACK, N_EDGE = 4, 2, 2, 2, 4, 2
A_TABLE = 0
A_BLOCK = A_TABLE + N_TABLE
A_FACE_X = A_BLOCK + N_BLOCK
A_FACE_Y = A_FACE_X + N_FACE_X
A_PACK = A_FACE_Y + N_FACE_Y
A_EDGE = A_PACK + N_PACK
A_END = A_EDGE + N_EDGE

OTHER_ROUTES = (0, 4, 1, 3)
STEPS = ((0, 0), (0, 1), (1, -1), (1, 0), (1, 1))
HALF = len(STEPS)
PAIRS = ((0, 0), (1, 1), (2, 2), (0, 1), (0, 2), (1, 2))


def iota(shape, dim):
    return lax.broadcasted_iota(jnp.int32, shape, dim)


def flag(condition):
    return jnp.where(condition, jnp.float32(1.0), jnp.float32(0.0))


def rolled(value, shift, axis):
    size = value.shape[axis]
    shift = shift % size
    return value if shift == 0 else pltpu.roll(value, shift, axis)


def halves(value):
    high = value.astype(BF16)
    return high, (value - high.astype(F32)).astype(BF16)


def near_exact(left, right):
    a, b = halves(left), halves(right)
    total = jnp.dot(a[0], b[1], preferred_element_type=F32) + jnp.dot(a[1], b[0], preferred_element_type=F32)
    return total + jnp.dot(a[0], b[0], preferred_element_type=F32)


def two_sum(a, b):
    total = a + b
    part = total - a
    return total, (a - (total - part)) + (b - part)


def quick_sum(a, b):
    total = a + b
    return total, b - (total - a)


def cut_in_two(a):
    wide = a * 4097.0
    high = wide - (wide - a)
    return high, a - high


def two_product(a, b):
    value = a * b
    (ah, al), (bh, bl) = cut_in_two(a), cut_in_two(b)
    return value, ((ah * bh - value) + ah * bl + al * bh) + al * bl


def plus(a, b):
    high, low = two_sum(a[0], b[0])
    return quick_sum(high, low + a[1] + b[1])


def minus(a, b):
    return plus(a, (-b[0], -b[1]))


def times(a, b):
    high, low = two_product(a[0], b[0])
    return quick_sum(high, low + (a[0] * b[1] + a[1] * b[0]))


def inverse(pivot, scale):
    sound = pivot[0] > scale[0] * 1e-12
    safe = (jnp.where(sound, pivot[0], 1.0), jnp.where(sound, pivot[1], 0.0))
    guess = 1.0 / safe[0]
    zero = jnp.zeros_like(guess)
    left = minus((zero + 1.0, zero), times(safe, (guess, zero)))
    result = quick_sum(guess, guess * left[0])
    return jnp.where(sound, result[0], 0.0), jnp.where(sound, result[1], 0.0)


def best_coefficients(moment, weight):
    count = 3
    level = (jnp.full_like(moment[0][0], weight[0]), jnp.full_like(moment[0][0], weight[1]))
    shifted = [plus(moment[k + 1], times(level, moment[k])) for k in range(2 * count - 1)]
    matrix = [[shifted[i + j] for j in range(count)] for i in range(count)]
    right = moment[:count]
    scale = [matrix[i][i] for i in range(count)]
    pivots = []
    for i in range(count):
        pivots.append(inverse(matrix[i][i], scale[i]))
        for j in range(i + 1, count):
            ratio = times(matrix[i][j], pivots[i])
            for k in range(j, count):
                matrix[j][k] = minus(matrix[j][k], times(ratio, matrix[i][k]))
            right[j] = minus(right[j], times(ratio, right[i]))
    answer = [None] * count
    for i in reversed(range(count)):
        value = right[i]
        for j in range(i + 1, count):
            value = minus(value, times(matrix[i][j], answer[j]))
        answer[i] = times(value, pivots[i])
    return answer


def hats(position):
    upper = (position.astype(F32) + 0.5) / EDGE
    return 1.0 - upper, upper


def kernel(
    nx, ny, route_hbm, within_hbm, xshift_hbm, fractions_hbm, ref_hbm, dfm_hbm, inc, mis,
    route, within, xshift, fractions, ref, dfm, lsem, gossip,
    xb, tsend, trecv, fxs, fxr, fys, fyr, pmat, pacc, psend, precv, qmat, grad, refp, xrow, es, er, sg,
    kd, k1, rrow, rr, vv, hs, hr, ssem, rsem, gssem, grsem, rssem, rrsem, hssem, hrsem,
):
    p, q = lax.axis_index("gx"), lax.axis_index("gy")

    def at(dp, dq):
        return (lax.rem(p + dp + 2 * nx, nx), lax.rem(q + dq + 2 * ny, ny))

    def copy(src, dst, send_sem, recv_sem, dp, dq):
        c = pltpu.make_async_remote_copy(
            src_ref=src, dst_ref=dst, send_sem=send_sem, recv_sem=recv_sem,
            device_id=at(dp, dq), device_id_type=MESH,
        )
        c.start()
        return c

    started = []

    def send(number, src, dst, dp, dq):
        c = copy(src, dst, ssem.at[number], rsem.at[number], dp, dq)
        started.append(c)
        return c

    near = ((1, 0), (-1, 0), (0, 1), (0, -1), (0, 2), (0, -2))
    barrier = pltpu.get_barrier_semaphore()
    for dp, dq in near:
        pl.semaphore_signal(barrier, inc=1, device_id=at(dp, dq), device_id_type=MESH)
    loads = []
    for k, (src, dst) in enumerate((
        (route_hbm, route), (within_hbm, within), (xshift_hbm, xshift), (fractions_hbm, fractions),
        (ref_hbm, ref), (dfm_hbm, dfm),
    )):
        loads.append(pltpu.make_async_copy(src, dst, lsem.at[k]))
        loads[k].start()

    def tell(number, *places):
        for dp, dq in places:
            pl.semaphore_signal(gossip.at[number], inc=1, device_id=at(dp, dq), device_id_type=MESH)

    def hear(number, count):
        pl.semaphore_wait(gossip.at[number], count)

    lane, sub = iota((8, NY), 1), iota((8, NY), 0)
    block, inner = lane >> 4, lane & 15

    for c in loads[:3]:
        c.wait()
    routes = [route[0, 0, e] for e in range(NEL)]
    wanted = jnp.full((8, NY), -1, jnp.int32)
    count = jnp.zeros((8, NY), jnp.int32)
    for e in range(NEL):
        source = jnp.clip(p + xshift[0, 0, e] - 1, 0, nx - 1) - p + 1
        code = ((source * EZ + e // EYD) * EYD + within[0, 0, e]) * EDGE
        hit = sub == routes[e]
        wanted = jnp.where(hit & (count == block), inner + code, wanted)
        count = count + jnp.where(hit, 1, 0)
    tsend[...] = wanted

    loads[4].wait()
    refp[0] = jnp.zeros((32, NY), F32)
    refp[NZ + 1] = jnp.zeros((32, NY), F32)
    refp[1 : NZ + 1, 8:24, :] = ref[...].astype(F32)
    fxs[0] = refp[1 : NZ + 1, 8, :].astype(BF16)
    fxs[1] = refp[1 : NZ + 1, 23, :].astype(BF16)
    rows16, lanes16 = iota((16, NY), 0), iota((16, NY), 1)
    pick = ((rows16 == 0) & (lanes16 == 0)) | ((rows16 == 1) & (lanes16 == NY - 1))
    fys[...] = lax.dot_general(
        jnp.where(pick, 1.0, 0.0).astype(BF16), ref[...].reshape(NZ * EDGE, NY),
        (((1,), (1,)), ((), ())), preferred_element_type=F32,
    ).astype(BF16)

    pl.semaphore_wait(barrier, len(near))
    faces_y = [
        send(A_FACE_Y, fys, fyr.at[1], 0, -1),
        send(A_FACE_Y + 1, fys, fyr.at[0], 0, 1),
    ]
    tables = [
        send(A_TABLE + k, tsend, trecv.at[k], 0, r - SPAN) for k, r in enumerate(OTHER_ROUTES)
    ]
    faces_x = [
        send(A_FACE_X, fxs.at[0], fxr.at[1], -1, 0),
        send(A_FACE_X + 1, fxs.at[1], fxr.at[0], 1, 0),
    ]
    blocks = [send(A_BLOCK, dfm_hbm, xb.at[1], -1, 0), send(A_BLOCK + 1, dfm_hbm, xb.at[0], 1, 0)]

    loads[3].wait()
    element = sub * EYD + block
    own_route = jnp.zeros((8, NY), jnp.int32)
    parts = [jnp.zeros((8, NY), jnp.int32) for _ in range(3)]
    for e in range(NEL):
        here = element == e
        own_route = jnp.where(here, routes[e], own_route)
        parts = [jnp.where(here, fractions[0, c, 0, e], parts[c]) for c in range(3)]
    slot = jnp.zeros((8, NY), jnp.int32)
    for e in range(NEL):
        slot = slot + jnp.where((element > e) & (own_route == routes[e]), 1, 0)
    first = (own_route * CAP + slot) * EDGE
    portion = [part.astype(F32) / EDGE for part in parts]
    target0 = first + inner
    target1 = first + jnp.minimum(inner + 1, EDGE - 1)

    for z in range(EZ):
        def fill_place(b, _):
            row = b * NY + iota((NY, NY), 0)
            high = portion[2][z : z + 1]
            place = jnp.where(row == target0[z : z + 1], 1.0 - high, 0.0)
            place = place + jnp.where(row == target1[z : z + 1], high, 0.0)
            qmat[pl.ds(pl.multiple_of(b * NY, NY), NY), z * NY : (z + 1) * NY] = place.astype(BF16)
            return 0

        lax.fori_loop(0, ROUTES, fill_place, 0)

    for c in tables:
        c.wait_recv()
    tell(3, (0, 4), (0, -4))
    asked = []
    for r in range(ROUTES):
        if r == SPAN:
            asked.append(wanted[r : r + 1])
        else:
            k = OTHER_ROUTES.index(r)
            asked.append(trecv[k, r : r + 1, :])
    asked = jnp.concatenate(asked, axis=1)

    def fill_pack(b, _):
        row = b * NY + iota((NY, ROUTES * NY), 0)
        pmat[pl.ds(pl.multiple_of(b * NY, NY), NY), :] = jnp.where(row == asked, 1.0, 0.0).astype(BF16)
        return 0

    lax.fori_loop(0, 3 * EZ, fill_pack, 0)

    def brick_rows(source):
        return jnp.concatenate(
            [source[z * EDGE : (z + 1) * EDGE].reshape(EDGE * EDGE, NY) for z in range(EZ)], axis=1
        )

    width = EZ * NY
    loads[5].wait()
    pacc[...] = jnp.dot(brick_rows(dfm), pmat[width : 2 * width, :], preferred_element_type=F32)

    for c in faces_x:
        c.wait_recv()
    tell(0, (1, 0), (-1, 0))
    for c in faces_y:
        c.wait_recv()
    refp[1 : NZ + 1, 7, :] = fxr[0].astype(F32) * flag(p > 0)
    refp[1 : NZ + 1, 24, :] = fxr[1].astype(F32) * flag(p < nx - 1)
    here, there = iota((NY, NY), 1), iota((NY, NY), 0)
    differ = jnp.where(there == here + 1, 0.5, jnp.where(there == here - 1, -0.5, 0.0)).astype(BF16)
    rows32, lanes32 = iota((32, NY), 0), iota((32, NY), 1)
    ends = jnp.where(
        (rows32 == 1) & (lanes32 == 0), flag(q > 0) * -0.5,
        jnp.where((rows32 == 16) & (lanes32 == NY - 1), flag(q < ny - 1) * 0.5, 0.0),
    ).astype(BF16)
    sides = jnp.concatenate([fyr[0], fyr[1]], axis=0)
    along_y = jnp.dot(ref[...].reshape(NZ * EDGE, NY), differ, preferred_element_type=F32)
    along_y = along_y + lax.dot_general(sides, ends, (((0,), (0,)), ((), ())), preferred_element_type=F32)
    grad[2] = along_y.astype(BF16).reshape(NZ, EDGE, NY)

    def slope(b, _):
        base = b * 4
        below, above = refp[pl.ds(base, 4), 8:24, :], refp[pl.ds(base + 2, 4), 8:24, :]
        grad[0, pl.ds(base, 4)] = ((above - below) * 0.5).astype(BF16)
        left, right = refp[pl.ds(base + 1, 4), 7:23, :], refp[pl.ds(base + 1, 4), 9:25, :]
        grad[1, pl.ds(base, 4)] = ((right - left) * 0.5).astype(BF16)
        return 0

    lax.fori_loop(0, NZ // 4, slope, 0)

    rowm, colm = iota((24, 96), 0), iota((24, 96), 1)
    low_x, high_x = hats(colm & 15)
    order = rowm >> 3
    weight_x = jnp.where(order == 0, low_x * low_x, jnp.where(order == 1, low_x * high_x, high_x * high_x))
    weight_x = jnp.where((rowm & 7) == (colm >> 4), weight_x, 0.0)
    weights_x = jnp.concatenate(halves(weight_x), axis=0)

    def moments(z, _):
        total = [[None] * 6 for _ in range(3)]
        for i in range(EDGE):
            g = [grad[c, z * EDGE + i].astype(F32) for c in range(3)]
            high = (i + 0.5) / EDGE
            low = 1.0 - high
            for k, (a, b) in enumerate(PAIRS):
                product = g[a] * g[b]
                for m, weight in enumerate((low * low, low * high, high * high)):
                    term = product * weight
                    total[m][k] = term if i == 0 else total[m][k] + term
        for m in range(3):
            parts = [
                jnp.dot(weights_x, part, preferred_element_type=F32)
                for part in halves(jnp.concatenate(total[m], axis=0))
            ]
            rows = (parts[1][:24] + parts[0][24:]) + parts[0][:24]
            xrow[pl.ds(pl.multiple_of((z * 3 + m) * 24, 24), 24), :] = rows
        return 0

    lax.fori_loop(0, EZ, moments, 0)
    fine, coarse = iota((NY, 3 * NY), 0), iota((NY, 3 * NY), 1)
    low_y, high_y = hats(fine & 15)
    row_y, node_y, step_y = fine >> 4, (coarse & 15) - 4, (coarse >> 7) - 1
    starts, closes = row_y == node_y, row_y + 1 == node_y
    mixed = low_y * high_y
    weight_y = jnp.where(
        step_y == 1, jnp.where(starts, mixed, 0.0),
        jnp.where(
            step_y == -1, jnp.where(closes, mixed, 0.0),
            jnp.where(starts, low_y * low_y, 0.0) + jnp.where(closes, high_y * high_y, 0.0),
        ),
    ) * (1.0 / VOL)
    yrow = near_exact(xrow[...], weight_y)
    on = [block == z for z in range(EZ + 1)]
    mine = [[None] * HALF for _ in range(3)]
    for m in range(3):
        for k, (dz, dy) in enumerate(STEPS):
            def term(z, depth):
                start = (z * 3 + depth) * 24 + m * 8
                return yrow[start : start + 8, (dy + 1) * NY : (dy + 2) * NY]

            total = jnp.zeros((8, NY), F32)
            for z in range(EZ):
                if dz == 1:
                    total = jnp.where(on[z], term(z, 1), total)
                else:
                    total = total + jnp.where(on[z], term(z, 0), 0.0) + jnp.where(on[z + 1], term(z, 2), 0.0)
            mine[m][k] = total
    for m in range(3):
        for part, ks in enumerate(((0, 1, 2), (3, 4))):
            upper, lower = jnp.zeros((8, NY), F32), jnp.zeros((8, NY), F32)
            for k in ks:
                offset = 5 * (k % 3)
                spot = (inner >= offset) & (inner < offset + 5)
                upper = jnp.where(spot, rolled(mine[m][k], offset - 8, 1), upper)
                lower = jnp.where(spot, rolled(mine[m][k], offset - 4, 1), lower)
            es[0, m * 2 + part], es[1, m * 2 + part] = upper, lower
    edges = [send(A_EDGE, es.at[0], er.at[0], 0, 1), send(A_EDGE + 1, es.at[1], er.at[1], 0, -1)]
    hear(0, 2)
    tell(1, (1, 0), (-1, 0))
    blocks[1].wait_recv()
    pacc[...] += jnp.dot(brick_rows(xb[0]), pmat[0:width, :], preferred_element_type=F32)
    blocks[0].wait_recv()
    last = brick_rows(xb[1])

    def packed(r):
        part = jnp.dot(last, pmat[2 * width : 3 * width, r * NY : (r + 1) * NY], preferred_element_type=F32)
        return (pacc[:, r * NY : (r + 1) * NY] + part).astype(BF16)

    packs = []
    for k, r in enumerate(OTHER_ROUTES):
        psend[k] = packed(r)
        packs.append(send(A_PACK + k, psend.at[k], precv.at[r], 0, SPAN - r))
    precv[SPAN] = packed(SPAN)
    hear(1, 2)
    tell(2, (1, 0), (-1, 0))
    hear(3, 2)
    tell(4, (0, 8), (0, -8))

    for c in edges:
        c.wait_recv()
    for m in range(3):
        for k in range(HALF):
            offset, part = 5 * (k % 3), k // 3
            below = jnp.where(inner < 5, rolled(er[0, m * 2 + part], -offset, 1), 0.0) * flag(q > 0)
            above = jnp.where(inner >= 12, rolled(er[1, m * 2 + part], 12 - offset, 1), 0.0) * flag(q < ny - 1)
            sg[p, m * HALF + k] = mine[m][k] + below + above
    spread = []
    for k in sorted(range(1, nx), key=lambda k: (-min(k, nx - k), k)):
        spread.append(copy(sg.at[p], sg.at[p], gssem.at[k - 1], grsem.at[k - 1], k, 0))
    started.extend(spread)

    for c in packs:
        c.wait_recv()
    taken = jnp.concatenate([precv[r] for r in range(ROUTES)], axis=1)
    column = inner - 4
    own = (column >= 0) & (column < EYD) & (block <= EZ) & (sub < 3)
    inside = (q * EYD + column < ny * EYD) & (sub < 3)
    fetched = jnp.dot(taken, qmat[...], preferred_element_type=F32)
    row8, col16 = iota((8, EDGE), 0), iota((8, EDGE), 1)
    low_j, high_j = hats(iota((EDGE, 1), 0))
    for z in range(EZ):
        voxels = fetched[:, z * NY : (z + 1) * NY].reshape(EDGE, EDGE, NY)
        high = portion[1][z : z + 1].reshape(1, 1, NY)
        ahead = jnp.concatenate([voxels[:, 1:], voxels[:, EDGE - 1 :]], axis=1)
        voxels = (1.0 - high) * voxels + high * ahead
        high = portion[0][z : z + 1].reshape(1, 1, NY)
        ahead = jnp.concatenate([voxels[1:], voxels[EDGE - 1 :]], axis=0)
        voxels = (1.0 - high) * voxels + high * ahead
        left = refp[1 + z * EDGE : 1 + (z + 1) * EDGE, 8:24, :] - voxels
        mis[z * EDGE : (z + 1) * EDGE] = left
        sums = [[None] * 3 for _ in range(2)]
        for i in range(EDGE):
            high = (i + 0.5) / EDGE
            for c in range(3):
                value = grad[c, z * EDGE + i].astype(F32) * left[i]
                for m, weight in enumerate((1.0 - high, high)):
                    sums[m][c] = value * weight if i == 0 else sums[m][c] + value * weight
        for m in range(2):
            rows = [jnp.sum(sums[m][c] * w, axis=0, keepdims=True) for w in (low_j, high_j) for c in range(3)]
            blank = jnp.zeros((1, NY), F32)
            start = (z * 2 + m) * 8
            rrow[start : start + 8, :] = jnp.concatenate(rows[:3] + [blank] + rows[3:] + [blank], axis=0)
    fine, coarse = iota((NY, NY), 0), iota((NY, NY), 1)
    low_y, high_y = hats(fine & 15)
    row_y, node_y = fine >> 4, (coarse & 15) - 4
    weight_y = (
        jnp.where(row_y == node_y, low_y, 0.0) + jnp.where(row_y + 1 == node_y, high_y, 0.0)
    ) * (1.0 / VOL)
    nodes = jnp.dot(rrow[...], weight_y, precision=EXACT, preferred_element_type=F32)
    tile = jnp.zeros((8, NY), F32)
    for z in range(EZ):
        for m in range(2):
            start = (z * 2 + m) * 8
            tile = tile + jnp.where(on[z + m], nodes[start : start + 8], 0.0)
    rr[1, p] = tile
    hear(2, 2)
    sent = []
    for k in sorted(range(nx), key=lambda k: (-min(k, nx - k), k)):
        for dq in (1, -1, 0):
            if k or dq:
                number = k * 3 + 1 - dq
                sent.append(copy(rr.at[1, p], rr.at[1 - dq, p], rssem.at[number], rrsem.at[number], k, dq))
    started.extend(sent)

    for c in spread:
        c.wait_recv()
    for x in range(nx):
        for k, (dz, dy) in enumerate(STEPS):
            level, cross = sg[x, k], sg[x, HALF + k]
            if x > 0:
                level = level + sg[x - 1, 2 * HALF + k]
            kd[x, 4 + k], k1[x, 4 + k] = level, cross
            if k:
                shift = dz * 16 + dy
                kd[x, 4 - k], k1[x, 4 - k] = rolled(level, shift, 1), rolled(cross, shift, 1)

    for c in sent:
        c.wait_recv()
    below, above = flag(q > 0), flag(q < ny - 1)
    tiles = []
    for x in range(nx):
        from_below = jnp.where(inner < 8, rolled(rr[0, x], -8, 1), 0.0) * below
        from_above = jnp.where(inner >= 8, rolled(rr[2, x], 8, 1), 0.0) * above
        tiles.append(rr[1, x] + from_below + from_above)
    for x in range(nx):
        whole = tiles[x] + rolled(tiles[x - 1], 4, 0) if x else tiles[x]
        vv[0, x] = jnp.where(inside, whole, 0.0)

    for step in range(3):
        straight = [jnp.zeros((8, NY), F32) for _ in range(nx)]
        crossed = [jnp.zeros((8, NY), F32) for _ in range(nx)]
        for x in range(nx):
            u = [vv[step, x, c : c + 1, :] for c in range(3)]
            second = jnp.where(sub == 0, u[0], jnp.where((sub == 1) | (sub == 3), u[1], u[2]))
            third = jnp.where(sub == 5, u[1], u[0])
            for t in range(9):
                shift = -((t // 3 - 1) * 16 + t % 3 - 1)
                moved, other = rolled(second, shift, 1), rolled(third, shift, 1)
                level, cross = kd[x, t], k1[x, t]
                straight[x] = straight[x] + level * moved
                crossed[x] = crossed[x] + level * other
                if x + 1 < nx:
                    straight[x + 1] = straight[x + 1] + cross * moved
                    crossed[x + 1] = crossed[x + 1] + cross * other
                if x > 0:
                    before = k1[x - 1, t]
                    straight[x - 1] = straight[x - 1] + before * moved
                    crossed[x - 1] = crossed[x - 1] + before * other
        for x in range(nx):
            a, b = straight[x], crossed[x]
            out = [
                a[0:1] + a[3:4] + a[4:5],
                a[1:2] + a[5:6] + b[3:4],
                a[2:3] + b[4:5] + b[5:6],
            ]
            image = jnp.where(sub == 0, out[0], jnp.where(sub == 1, out[1], out[2]))
            vv[step + 1, x] = jnp.where(inside, image, 0.0)

    zero = jnp.zeros((8, NY), F32)
    tile = zero
    for k in range(6):
        high, low = zero, zero
        for x in range(nx):
            value, rest = two_product(vv[k // 2, x], vv[(k + 1) // 2, x])
            high, lost = two_sum(high, value)
            low = low + (lost + rest)
        value, lost = two_sum(high[0:1], high[1:2])
        value, more = two_sum(value, high[2:3])
        rest = (low[0:1] + low[1:2]) + (low[2:3] + (lost + more))
        owned = own[0:1]
        both = jnp.where(owned, value, 0.0) + rolled(jnp.where(owned, rest, 0.0), 8, 1)
        tile = jnp.where(sub == k, both, tile)
    hear(4, 2)
    hs[...] = tile

    sums = {}
    for k in sorted(range(1, ny), key=lambda k: (-min(k, ny - k), k)):
        sums[k] = copy(hs, hr.at[k - 1], hssem.at[k - 1], hrsem.at[k - 1], 0, k)
    for c in started:
        c.wait_send()
    rest = zero
    for k in sorted(range(1, ny), key=lambda k: (min(k, ny - k), k)):
        sums[k].wait_recv()
        tile, lost = two_sum(tile, hr[k - 1])
        rest = rest + lost
    for shift in (64, 32, 16, 8, 4, 2, 1):
        tile, lost = two_sum(tile, rolled(tile, shift, 1))
        rest = (rest + rolled(rest, shift, 1)) + lost
    tile, rest = quick_sum(tile, rest)

    moment = [(tile[k : k + 1], rest[k : k + 1]) for k in range(6)]
    answer = [high for high, low in best_coefficients(moment, LAMBDA_PARTS)]
    for k in range(1, ny):
        sums[k].wait_send()
    found = answer[0] * vv[0, p] + answer[1] * vv[1, p] + answer[2] * vv[2, p]
    for c in range(3):
        for z in range(EZ + 1):
            inc[c, z, 0:1, :] = found[c : c + 1, z * 16 + 4 : z * 16 + 4 + EYD]


def body(nx, ny, reference_image, deformed_image, route, within, xshift, fractions):
    vmem = pl.BlockSpec(memory_space=pltpu.VMEM)
    half = (NZ, EDGE, NY)
    tile = (8, NY)
    inc, mis = pl.pallas_call(
        lambda *refs: kernel(nx, ny, *refs),
        name="correlate",
        out_shape=(jax.ShapeDtypeStruct((3, EZ + 1, 1, EYD), F32), jax.ShapeDtypeStruct(half, F32)),
        in_specs=[pl.BlockSpec(memory_space=pltpu.HBM)] * 6,
        out_specs=(vmem, vmem),
        scratch_shapes=[
            pltpu.SMEM((1, 1, NEL), jnp.int32),
            pltpu.SMEM((1, 1, NEL), jnp.int32),
            pltpu.SMEM((1, 1, NEL), jnp.int32),
            pltpu.SMEM((1, 3, 1, NEL), jnp.int32),
            pltpu.VMEM(half, BF16),
            pltpu.VMEM(half, BF16),
            pltpu.SemaphoreType.DMA((6,)),
            pltpu.SemaphoreType.REGULAR((5,)),
            pltpu.VMEM((2,) + half, BF16),
            pltpu.VMEM(tile, jnp.int32),
            pltpu.VMEM((4,) + tile, jnp.int32),
            pltpu.VMEM((2, NZ, NY), BF16),
            pltpu.VMEM((2, NZ, NY), BF16),
            pltpu.VMEM((16, NZ * EDGE), BF16),
            pltpu.VMEM((2, 16, NZ * EDGE), BF16),
            pltpu.VMEM((3 * EZ * NY, ROUTES * NY), BF16),
            pltpu.VMEM((EDGE * EDGE, ROUTES * NY), F32),
            pltpu.VMEM((4, EDGE * EDGE, NY), BF16),
            pltpu.VMEM((ROUTES, EDGE * EDGE, NY), BF16),
            pltpu.VMEM((ROUTES * NY, EZ * NY), BF16),
            pltpu.VMEM((3,) + half, BF16),
            pltpu.VMEM((NZ + 2, 32, NY), F32),
            pltpu.VMEM((12 * 24, NY), F32),
            pltpu.VMEM((2, 6) + tile, F32),
            pltpu.VMEM((2, 6) + tile, F32),
            pltpu.VMEM((nx, 3 * HALF) + tile, F32),
            pltpu.VMEM((nx, 9) + tile, F32),
            pltpu.VMEM((nx, 9) + tile, F32),
            pltpu.VMEM((64, NY), F32),
            pltpu.VMEM((3, nx) + tile, F32),
            pltpu.VMEM((4, nx) + tile, F32),
            pltpu.VMEM(tile, F32),
            pltpu.VMEM((ny - 1,) + tile, F32),
            pltpu.SemaphoreType.DMA((A_END,)),
            pltpu.SemaphoreType.DMA((A_END,)),
            pltpu.SemaphoreType.DMA((nx - 1,)),
            pltpu.SemaphoreType.DMA((nx - 1,)),
            pltpu.SemaphoreType.DMA((3 * nx,)),
            pltpu.SemaphoreType.DMA((3 * nx,)),
            pltpu.SemaphoreType.DMA((ny - 1,)),
            pltpu.SemaphoreType.DMA((ny - 1,)),
        ],
        compiler_params=pltpu.CompilerParams(
            collective_id=0, has_side_effects=True, vmem_limit_bytes=63 << 20
        ),
    )(route.reshape(1, 1, NEL), within, xshift, fractions.transpose(0, 3, 1, 2), reference_image, deformed_image)
    return inc, mis


def solution(mesh):
    nx, ny = mesh.shape["gx"], mesh.shape["gy"]
    placed = (
        P(None, "gx", "gy"),
        P(None, "gx", "gy"),
        P("gx", "gy", None, None),
        P("gx", "gy", None),
        P("gx", "gy", None),
        P("gx", "gy", None, None),
    )
    return jax.shard_map(
        lambda *blocks: body(nx, ny, *blocks),
        mesh=mesh,
        in_specs=placed,
        out_specs=(P(None, None, "gx", "gy"), P(None, "gx", "gy")),
        check_vma=False,
    )
```

```python
import jax
import jax.numpy as jnp
import numpy as np
from jax import lax
from jax.experimental import pallas as pl
from jax.experimental.pallas import tpu as pltpu
from jax.sharding import PartitionSpec as P

EDGE = 16
EZ = 4
EYD = 8
SPAN = 2
ROUTES = 2 * SPAN + 1
NEL = 32
CAP = 8
VOL = 4096
NZ = 64
NY = 128
LAMBDA = 0.05
LAMBDA_PARTS = (float(np.float32(LAMBDA)), 0.0)
MESH = pl.DeviceIdType.MESH
F32 = jnp.float32
BF16 = jnp.bfloat16
EXACT = lax.Precision.HIGHEST

N_TABLE, N_BLOCK, N_FACE_X, N_FACE_Y, N_PACK, N_EDGE = 4, 2, 2, 2, 4, 2
A_TABLE = 0
A_BLOCK = A_TABLE + N_TABLE
A_FACE_X = A_BLOCK + N_BLOCK
A_FACE_Y = A_FACE_X + N_FACE_X
A_PACK = A_FACE_Y + N_FACE_Y
A_EDGE = A_PACK + N_PACK
A_END = A_EDGE + N_EDGE

OTHER_ROUTES = (0, 4, 1, 3)
STEPS = ((0, 0), (0, 1), (1, -1), (1, 0), (1, 1))
HALF = len(STEPS)
PAIRS = ((0, 0), (1, 1), (2, 2), (0, 1), (0, 2), (1, 2))


def iota(shape, dim):
    return lax.broadcasted_iota(jnp.int32, shape, dim)


def flag(condition):
    return jnp.where(condition, jnp.float32(1.0), jnp.float32(0.0))


def rolled(value, shift, axis):
    size = value.shape[axis]
    shift = shift % size
    return value if shift == 0 else pltpu.roll(value, shift, axis)


def halves(value):
    high = value.astype(BF16)
    return high, (value - high.astype(F32)).astype(BF16)


def near_exact(left, right):
    a, b = halves(left), halves(right)
    total = jnp.dot(a[0], b[1], preferred_element_type=F32) + jnp.dot(a[1], b[0], preferred_element_type=F32)
    return total + jnp.dot(a[0], b[0], preferred_element_type=F32)


def two_sum(a, b):
    total = a + b
    part = total - a
    return total, (a - (total - part)) + (b - part)


def quick_sum(a, b):
    total = a + b
    return total, b - (total - a)


def cut_in_two(a):
    wide = a * 4097.0
    high = wide - (wide - a)
    return high, a - high


def two_product(a, b):
    value = a * b
    (ah, al), (bh, bl) = cut_in_two(a), cut_in_two(b)
    return value, ((ah * bh - value) + ah * bl + al * bh) + al * bl


def plus(a, b):
    high, low = two_sum(a[0], b[0])
    return quick_sum(high, low + a[1] + b[1])


def minus(a, b):
    return plus(a, (-b[0], -b[1]))


def times(a, b):
    high, low = two_product(a[0], b[0])
    return quick_sum(high, low + (a[0] * b[1] + a[1] * b[0]))


def inverse(pivot, scale):
    sound = pivot[0] > scale[0] * 1e-12
    safe = (jnp.where(sound, pivot[0], 1.0), jnp.where(sound, pivot[1], 0.0))
    guess = 1.0 / safe[0]
    zero = jnp.zeros_like(guess)
    left = minus((zero + 1.0, zero), times(safe, (guess, zero)))
    result = quick_sum(guess, guess * left[0])
    return jnp.where(sound, result[0], 0.0), jnp.where(sound, result[1], 0.0)


def best_coefficients(moment, weight):
    count = 3
    level = (jnp.full_like(moment[0][0], weight[0]), jnp.full_like(moment[0][0], weight[1]))
    shifted = [plus(moment[k + 1], times(level, moment[k])) for k in range(2 * count - 1)]
    matrix = [[shifted[i + j] for j in range(count)] for i in range(count)]
    right = moment[:count]
    scale = [matrix[i][i] for i in range(count)]
    pivots = []
    for i in range(count):
        pivots.append(inverse(matrix[i][i], scale[i]))
        for j in range(i + 1, count):
            ratio = times(matrix[i][j], pivots[i])
            for k in range(j, count):
                matrix[j][k] = minus(matrix[j][k], times(ratio, matrix[i][k]))
            right[j] = minus(right[j], times(ratio, right[i]))
    answer = [None] * count
    for i in reversed(range(count)):
        value = right[i]
        for j in range(i + 1, count):
            value = minus(value, times(matrix[i][j], answer[j]))
        answer[i] = times(value, pivots[i])
    return answer


def hats(position):
    upper = (position.astype(F32) + 0.5) / EDGE
    return 1.0 - upper, upper


def kernel(
    nx, ny, route_hbm, within_hbm, xshift_hbm, fractions_hbm, ref_hbm, dfm_hbm, inc, mis,
    route, within, xshift, fractions, ref, dfm, lsem, gossip,
    xb, tsend, trecv, fxs, fxr, fys, fyr, pmat, pacc, psend, precv, qmat, grad, refp, xrow, es, er, sg,
    kd, k1, rrow, rr, vv, hs, hr, ssem, rsem, gssem, grsem, rssem, rrsem, hssem, hrsem,
):
    p, q = lax.axis_index("gx"), lax.axis_index("gy")

    def at(dp, dq):
        return (lax.rem(p + dp + 2 * nx, nx), lax.rem(q + dq + 2 * ny, ny))

    def copy(src, dst, send_sem, recv_sem, dp, dq):
        c = pltpu.make_async_remote_copy(
            src_ref=src, dst_ref=dst, send_sem=send_sem, recv_sem=recv_sem,
            device_id=at(dp, dq), device_id_type=MESH,
        )
        c.start()
        return c

    started = []

    def send(number, src, dst, dp, dq):
        c = copy(src, dst, ssem.at[number], rsem.at[number], dp, dq)
        started.append(c)
        return c

    near = ((1, 0), (-1, 0), (0, 1), (0, -1), (0, 2), (0, -2))
    barrier = pltpu.get_barrier_semaphore()
    for dp, dq in near:
        pl.semaphore_signal(barrier, inc=1, device_id=at(dp, dq), device_id_type=MESH)
    loads = []
    for k, (src, dst) in enumerate((
        (route_hbm, route), (within_hbm, within), (xshift_hbm, xshift), (fractions_hbm, fractions),
        (ref_hbm, ref), (dfm_hbm, dfm),
    )):
        loads.append(pltpu.make_async_copy(src, dst, lsem.at[k]))
        loads[k].start()

    def tell(number, *places):
        for dp, dq in places:
            pl.semaphore_signal(gossip.at[number], inc=1, device_id=at(dp, dq), device_id_type=MESH)

    def hear(number, count):
        pl.semaphore_wait(gossip.at[number], count)

    lane, sub = iota((8, NY), 1), iota((8, NY), 0)
    block, inner = lane >> 4, lane & 15

    for c in loads[:3]:
        c.wait()
    routes = [route[0, 0, e] for e in range(NEL)]
    wanted = jnp.full((8, NY), -1, jnp.int32)
    count = jnp.zeros((8, NY), jnp.int32)
    for e in range(NEL):
        source = jnp.clip(p + xshift[0, 0, e] - 1, 0, nx - 1) - p + 1
        code = ((source * EZ + e // EYD) * EYD + within[0, 0, e]) * EDGE
        hit = sub == routes[e]
        wanted = jnp.where(hit & (count == block), inner + code, wanted)
        count = count + jnp.where(hit, 1, 0)
    tsend[...] = wanted

    loads[4].wait()
    refp[0] = jnp.zeros((32, NY), F32)
    refp[NZ + 1] = jnp.zeros((32, NY), F32)
    refp[1 : NZ + 1, 8:24, :] = ref[...].astype(F32)
    fxs[0] = refp[1 : NZ + 1, 8, :].astype(BF16)
    fxs[1] = refp[1 : NZ + 1, 23, :].astype(BF16)
    rows16, lanes16 = iota((16, NY), 0), iota((16, NY), 1)
    pick = ((rows16 == 0) & (lanes16 == 0)) | ((rows16 == 1) & (lanes16 == NY - 1))
    fys[...] = lax.dot_general(
        jnp.where(pick, 1.0, 0.0).astype(BF16), ref[...].reshape(NZ * EDGE, NY),
        (((1,), (1,)), ((), ())), preferred_element_type=F32,
    ).astype(BF16)

    pl.semaphore_wait(barrier, len(near))
    faces_y = [
        send(A_FACE_Y, fys, fyr.at[1], 0, -1),
        send(A_FACE_Y + 1, fys, fyr.at[0], 0, 1),
    ]
    tables = [
        send(A_TABLE + k, tsend, trecv.at[k], 0, r - SPAN) for k, r in enumerate(OTHER_ROUTES)
    ]
    faces_x = [
        send(A_FACE_X, fxs.at[0], fxr.at[1], -1, 0),
        send(A_FACE_X + 1, fxs.at[1], fxr.at[0], 1, 0),
    ]
    blocks = [send(A_BLOCK, dfm_hbm, xb.at[1], -1, 0), send(A_BLOCK + 1, dfm_hbm, xb.at[0], 1, 0)]

    loads[3].wait()
    element = sub * EYD + block
    own_route = jnp.zeros((8, NY), jnp.int32)
    parts = [jnp.zeros((8, NY), jnp.int32) for _ in range(3)]
    for e in range(NEL):
        here = element == e
        own_route = jnp.where(here, routes[e], own_route)
        parts = [jnp.where(here, fractions[0, c, 0, e], parts[c]) for c in range(3)]
    slot = jnp.zeros((8, NY), jnp.int32)
    for e in range(NEL):
        slot = slot + jnp.where((element > e) & (own_route == routes[e]), 1, 0)
    first = (own_route * CAP + slot) * EDGE
    portion = [part.astype(F32) / EDGE for part in parts]
    target0 = first + inner
    target1 = first + jnp.minimum(inner + 1, EDGE - 1)

    for z in range(EZ):
        def fill_place(b, _):
            row = b * NY + iota((NY, NY), 0)
            high = portion[2][z : z + 1]
            place = jnp.where(row == target0[z : z + 1], 1.0 - high, 0.0)
            place = place + jnp.where(row == target1[z : z + 1], high, 0.0)
            qmat[pl.ds(pl.multiple_of(b * NY, NY), NY), z * NY : (z + 1) * NY] = place.astype(BF16)
            return 0

        lax.fori_loop(0, ROUTES, fill_place, 0)

    for c in tables:
        c.wait_recv()
    tell(3, (0, 4), (0, -4))
    asked = []
    for r in range(ROUTES):
        if r == SPAN:
            asked.append(wanted[r : r + 1])
        else:
            k = OTHER_ROUTES.index(r)
            asked.append(trecv[k, r : r + 1, :])
    asked = jnp.concatenate(asked, axis=1)

    def fill_pack(b, _):
        row = b * NY + iota((NY, ROUTES * NY), 0)
        pmat[pl.ds(pl.multiple_of(b * NY, NY), NY), :] = jnp.where(row == asked, 1.0, 0.0).astype(BF16)
        return 0

    lax.fori_loop(0, 3 * EZ, fill_pack, 0)

    def brick_rows(source):
        return jnp.concatenate(
            [source[z * EDGE : (z + 1) * EDGE].reshape(EDGE * EDGE, NY) for z in range(EZ)], axis=1
        )

    width = EZ * NY
    loads[5].wait()
    pacc[...] = jnp.dot(brick_rows(dfm), pmat[width : 2 * width, :], preferred_element_type=F32)

    for c in faces_x:
        c.wait_recv()
    tell(0, (1, 0), (-1, 0))
    for c in faces_y:
        c.wait_recv()
    refp[1 : NZ + 1, 7, :] = fxr[0].astype(F32) * flag(p > 0)
    refp[1 : NZ + 1, 24, :] = fxr[1].astype(F32) * flag(p < nx - 1)
    here, there = iota((NY, NY), 1), iota((NY, NY), 0)
    differ = jnp.where(there == here + 1, 0.5, jnp.where(there == here - 1, -0.5, 0.0)).astype(BF16)
    rows32, lanes32 = iota((32, NY), 0), iota((32, NY), 1)
    ends = jnp.where(
        (rows32 == 1) & (lanes32 == 0), flag(q > 0) * -0.5,
        jnp.where((rows32 == 16) & (lanes32 == NY - 1), flag(q < ny - 1) * 0.5, 0.0),
    ).astype(BF16)
    sides = jnp.concatenate([fyr[0], fyr[1]], axis=0)
    along_y = jnp.dot(ref[...].reshape(NZ * EDGE, NY), differ, preferred_element_type=F32)
    along_y = along_y + lax.dot_general(sides, ends, (((0,), (0,)), ((), ())), preferred_element_type=F32)
    grad[2] = along_y.astype(BF16).reshape(NZ, EDGE, NY)

    def slope(b, _):
        base = b * 4
        below, above = refp[pl.ds(base, 4), 8:24, :], refp[pl.ds(base + 2, 4), 8:24, :]
        grad[0, pl.ds(base, 4)] = ((above - below) * 0.5).astype(BF16)
        left, right = refp[pl.ds(base + 1, 4), 7:23, :], refp[pl.ds(base + 1, 4), 9:25, :]
        grad[1, pl.ds(base, 4)] = ((right - left) * 0.5).astype(BF16)
        return 0

    lax.fori_loop(0, NZ // 4, slope, 0)

    rowm, colm = iota((24, 96), 0), iota((24, 96), 1)
    low_x, high_x = hats(colm & 15)
    order = rowm >> 3
    weight_x = jnp.where(order == 0, low_x * low_x, jnp.where(order == 1, low_x * high_x, high_x * high_x))
    weight_x = jnp.where((rowm & 7) == (colm >> 4), weight_x, 0.0)
    weights_x = jnp.concatenate(halves(weight_x), axis=0)

    def moments(z, _):
        total = [[None] * 6 for _ in range(3)]
        for i in range(EDGE):
            g = [grad[c, z * EDGE + i].astype(F32) for c in range(3)]
            high = (i + 0.5) / EDGE
            low = 1.0 - high
            for k, (a, b) in enumerate(PAIRS):
                product = g[a] * g[b]
                for m, weight in enumerate((low * low, low * high, high * high)):
                    term = product * weight
                    total[m][k] = term if i == 0 else total[m][k] + term
        for m in range(3):
            parts = [
                jnp.dot(weights_x, part, preferred_element_type=F32)
                for part in halves(jnp.concatenate(total[m], axis=0))
            ]
            rows = (parts[1][:24] + parts[0][24:]) + parts[0][:24]
            xrow[pl.ds(pl.multiple_of((z * 3 + m) * 24, 24), 24), :] = rows
        return 0

    lax.fori_loop(0, EZ, moments, 0)
    fine, coarse = iota((NY, 3 * NY), 0), iota((NY, 3 * NY), 1)
    low_y, high_y = hats(fine & 15)
    row_y, node_y, step_y = fine >> 4, (coarse & 15) - 4, (coarse >> 7) - 1
    starts, closes = row_y == node_y, row_y + 1 == node_y
    mixed = low_y * high_y
    weight_y = jnp.where(
        step_y == 1, jnp.where(starts, mixed, 0.0),
        jnp.where(
            step_y == -1, jnp.where(closes, mixed, 0.0),
            jnp.where(starts, low_y * low_y, 0.0) + jnp.where(closes, high_y * high_y, 0.0),
        ),
    ) * (1.0 / VOL)
    yrow = near_exact(xrow[...], weight_y)
    on = [block == z for z in range(EZ + 1)]
    mine = [[None] * HALF for _ in range(3)]
    for m in range(3):
        for k, (dz, dy) in enumerate(STEPS):
            def term(z, depth):
                start = (z * 3 + depth) * 24 + m * 8
                return yrow[start : start + 8, (dy + 1) * NY : (dy + 2) * NY]

            total = jnp.zeros((8, NY), F32)
            for z in range(EZ):
                if dz == 1:
                    total = jnp.where(on[z], term(z, 1), total)
                else:
                    total = total + jnp.where(on[z], term(z, 0), 0.0) + jnp.where(on[z + 1], term(z, 2), 0.0)
            mine[m][k] = total
    for m in range(3):
        for part, ks in enumerate(((0, 1, 2), (3, 4))):
            upper, lower = jnp.zeros((8, NY), F32), jnp.zeros((8, NY), F32)
            for k in ks:
                offset = 5 * (k % 3)
                spot = (inner >= offset) & (inner < offset + 5)
                upper = jnp.where(spot, rolled(mine[m][k], offset - 8, 1), upper)
                lower = jnp.where(spot, rolled(mine[m][k], offset - 4, 1), lower)
            es[0, m * 2 + part], es[1, m * 2 + part] = upper, lower
    edges = [send(A_EDGE, es.at[0], er.at[0], 0, 1), send(A_EDGE + 1, es.at[1], er.at[1], 0, -1)]
    hear(0, 2)
    tell(1, (1, 0), (-1, 0))
    blocks[1].wait_recv()
    pacc[...] += jnp.dot(brick_rows(xb[0]), pmat[0:width, :], preferred_element_type=F32)
    blocks[0].wait_recv()
    last = brick_rows(xb[1])

    def packed(r):
        part = jnp.dot(last, pmat[2 * width : 3 * width, r * NY : (r + 1) * NY], preferred_element_type=F32)
        return (pacc[:, r * NY : (r + 1) * NY] + part).astype(BF16)

    packs = []
    for k, r in enumerate(OTHER_ROUTES):
        psend[k] = packed(r)
        packs.append(send(A_PACK + k, psend.at[k], precv.at[r], 0, SPAN - r))
    precv[SPAN] = packed(SPAN)
    hear(1, 2)
    tell(2, (1, 0), (-1, 0))
    hear(3, 2)
    tell(4, (0, 8), (0, -8))

    for c in edges:
        c.wait_recv()
    for m in range(3):
        for k in range(HALF):
            offset, part = 5 * (k % 3), k // 3
            below = jnp.where(inner < 5, rolled(er[0, m * 2 + part], -offset, 1), 0.0) * flag(q > 0)
            above = jnp.where(inner >= 12, rolled(er[1, m * 2 + part], 12 - offset, 1), 0.0) * flag(q < ny - 1)
            sg[p, m * HALF + k] = mine[m][k] + below + above
    spread = []
    for k in sorted(range(1, nx), key=lambda k: (-min(k, nx - k), k)):
        spread.append(copy(sg.at[p], sg.at[p], gssem.at[k - 1], grsem.at[k - 1], k, 0))
    started.extend(spread)

    for c in packs:
        c.wait_recv()
    taken = jnp.concatenate([precv[r] for r in range(ROUTES)], axis=1)
    column = inner - 4
    own = (column >= 0) & (column < EYD) & (block <= EZ) & (sub < 3)
    inside = (q * EYD + column < ny * EYD) & (sub < 3)
    fetched = jnp.dot(taken, qmat[...], preferred_element_type=F32)
    row8, col16 = iota((8, EDGE), 0), iota((8, EDGE), 1)
    low_j, high_j = hats(iota((EDGE, 1), 0))
    for z in range(EZ):
        voxels = fetched[:, z * NY : (z + 1) * NY].reshape(EDGE, EDGE, NY)
        high = portion[1][z : z + 1].reshape(1, 1, NY)
        ahead = jnp.concatenate([voxels[:, 1:], voxels[:, EDGE - 1 :]], axis=1)
        voxels = (1.0 - high) * voxels + high * ahead
        high = portion[0][z : z + 1].reshape(1, 1, NY)
        ahead = jnp.concatenate([voxels[1:], voxels[EDGE - 1 :]], axis=0)
        voxels = (1.0 - high) * voxels + high * ahead
        left = refp[1 + z * EDGE : 1 + (z + 1) * EDGE, 8:24, :] - voxels
        mis[z * EDGE : (z + 1) * EDGE] = left
        sums = [[None] * 3 for _ in range(2)]
        for i in range(EDGE):
            high = (i + 0.5) / EDGE
            for c in range(3):
                value = grad[c, z * EDGE + i].astype(F32) * left[i]
                for m, weight in enumerate((1.0 - high, high)):
                    sums[m][c] = value * weight if i == 0 else sums[m][c] + value * weight
        for m in range(2):
            rows = [jnp.sum(sums[m][c] * w, axis=0, keepdims=True) for w in (low_j, high_j) for c in range(3)]
            blank = jnp.zeros((1, NY), F32)
            start = (z * 2 + m) * 8
            rrow[start : start + 8, :] = jnp.concatenate(rows[:3] + [blank] + rows[3:] + [blank], axis=0)
    fine, coarse = iota((NY, NY), 0), iota((NY, NY), 1)
    low_y, high_y = hats(fine & 15)
    row_y, node_y = fine >> 4, (coarse & 15) - 4
    weight_y = (
        jnp.where(row_y == node_y, low_y, 0.0) + jnp.where(row_y + 1 == node_y, high_y, 0.0)
    ) * (1.0 / VOL)
    nodes = jnp.dot(rrow[...], weight_y, precision=EXACT, preferred_element_type=F32)
    tile = jnp.zeros((8, NY), F32)
    for z in range(EZ):
        for m in range(2):
            start = (z * 2 + m) * 8
            tile = tile + jnp.where(on[z + m], nodes[start : start + 8], 0.0)
    rr[1, p] = tile
    hear(2, 2)
    sent = []
    for k in sorted(range(nx), key=lambda k: (-min(k, nx - k), k)):
        for dq in (1, -1, 0):
            if k or dq:
                number = k * 3 + 1 - dq
                sent.append(copy(rr.at[1, p], rr.at[1 - dq, p], rssem.at[number], rrsem.at[number], k, dq))
    started.extend(sent)

    for c in spread:
        c.wait_recv()
    for x in range(nx):
        for k, (dz, dy) in enumerate(STEPS):
            level, cross = sg[x, k], sg[x, HALF + k]
            if x > 0:
                level = level + sg[x - 1, 2 * HALF + k]
            kd[x, 4 + k], k1[x, 4 + k] = level, cross
            if k:
                shift = dz * 16 + dy
                kd[x, 4 - k], k1[x, 4 - k] = rolled(level, shift, 1), rolled(cross, shift, 1)

    for c in sent:
        c.wait_recv()
    below, above = flag(q > 0), flag(q < ny - 1)
    tiles = []
    for x in range(nx):
        from_below = jnp.where(inner < 8, rolled(rr[0, x], -8, 1), 0.0) * below
        from_above = jnp.where(inner >= 8, rolled(rr[2, x], 8, 1), 0.0) * above
        tiles.append(rr[1, x] + from_below + from_above)
    for x in range(nx):
        whole = tiles[x] + rolled(tiles[x - 1], 4, 0) if x else tiles[x]
        vv[0, x] = jnp.where(inside, whole, 0.0)

    for step in range(3):
        straight = [jnp.zeros((8, NY), F32) for _ in range(nx)]
        crossed = [jnp.zeros((8, NY), F32) for _ in range(nx)]
        for x in range(nx):
            u = [vv[step, x, c : c + 1, :] for c in range(3)]
            second = jnp.where(sub == 0, u[0], jnp.where((sub == 1) | (sub == 3), u[1], u[2]))
            third = jnp.where(sub == 5, u[1], u[0])
            for t in range(9):
                shift = -((t // 3 - 1) * 16 + t % 3 - 1)
                moved, other = rolled(second, shift, 1), rolled(third, shift, 1)
                level, cross = kd[x, t], k1[x, t]
                straight[x] = straight[x] + level * moved
                crossed[x] = crossed[x] + level * other
                if x + 1 < nx:
                    straight[x + 1] = straight[x + 1] + cross * moved
                    crossed[x + 1] = crossed[x + 1] + cross * other
                if x > 0:
                    before = k1[x - 1, t]
                    straight[x - 1] = straight[x - 1] + before * moved
                    crossed[x - 1] = crossed[x - 1] + before * other
        for x in range(nx):
            a, b = straight[x], crossed[x]
            out = [
                a[0:1] + a[3:4] + a[4:5],
                a[1:2] + a[5:6] + b[3:4],
                a[2:3] + b[4:5] + b[5:6],
            ]
            image = jnp.where(sub == 0, out[0], jnp.where(sub == 1, out[1], out[2]))
            vv[step + 1, x] = jnp.where(inside, image, 0.0)

    zero = jnp.zeros((8, NY), F32)
    tile = zero
    for k in range(6):
        high, low = zero, zero
        for x in range(nx):
            value, rest = two_product(vv[k // 2, x], vv[(k + 1) // 2, x])
            high, lost = two_sum(high, value)
            low = low + (lost + rest)
        value, lost = two_sum(high[0:1], high[1:2])
        value, more = two_sum(value, high[2:3])
        rest = (low[0:1] + low[1:2]) + (low[2:3] + (lost + more))
        owned = own[0:1]
        both = jnp.where(owned, value, 0.0) + rolled(jnp.where(owned, rest, 0.0), 8, 1)
        tile = jnp.where(sub == k, both, tile)
    hear(4, 2)
    hs[...] = tile

    sums = {}
    for k in sorted(range(1, ny), key=lambda k: (-min(k, ny - k), k)):
        sums[k] = copy(hs, hr.at[k - 1], hssem.at[k - 1], hrsem.at[k - 1], 0, k)
    for c in started:
        c.wait_send()
    rest = zero
    for k in sorted(range(1, ny), key=lambda k: (min(k, ny - k), k)):
        sums[k].wait_recv()
        tile, lost = two_sum(tile, hr[k - 1])
        rest = rest + lost
    for shift in (64, 32, 16, 8, 4, 2, 1):
        tile, lost = two_sum(tile, rolled(tile, shift, 1))
        rest = (rest + rolled(rest, shift, 1)) + lost
    tile, rest = quick_sum(tile, rest)

    moment = [(tile[k : k + 1], rest[k : k + 1]) for k in range(6)]
    answer = [high for high, low in best_coefficients(moment, LAMBDA_PARTS)]
    for k in range(1, ny):
        sums[k].wait_send()
    found = answer[0] * vv[0, p] + answer[1] * vv[1, p] + answer[2] * vv[2, p]
    for c in range(3):
        for z in range(EZ + 1):
            inc[c, z, 0:1, :] = found[c : c + 1, z * 16 + 4 : z * 16 + 4 + EYD]


def body(nx, ny, reference_image, deformed_image, route, within, xshift, fractions):
    vmem = pl.BlockSpec(memory_space=pltpu.VMEM)
    half = (NZ, EDGE, NY)
    tile = (8, NY)
    inc, mis = pl.pallas_call(
        lambda *refs: kernel(nx, ny, *refs),
        name="correlate",
        out_shape=(jax.ShapeDtypeStruct((3, EZ + 1, 1, EYD), F32), jax.ShapeDtypeStruct(half, F32)),
        in_specs=[pl.BlockSpec(memory_space=pltpu.HBM)] * 6,
        out_specs=(vmem, vmem),
        scratch_shapes=[
            pltpu.SMEM((1, 1, NEL), jnp.int32),
            pltpu.SMEM((1, 1, NEL), jnp.int32),
            pltpu.SMEM((1, 1, NEL), jnp.int32),
            pltpu.SMEM((1, 3, 1, NEL), jnp.int32),
            pltpu.VMEM(half, BF16),
            pltpu.VMEM(half, BF16),
            pltpu.SemaphoreType.DMA((6,)),
            pltpu.SemaphoreType.REGULAR((5,)),
            pltpu.VMEM((2,) + half, BF16),
            pltpu.VMEM(tile, jnp.int32),
            pltpu.VMEM((4,) + tile, jnp.int32),
            pltpu.VMEM((2, NZ, NY), BF16),
            pltpu.VMEM((2, NZ, NY), BF16),
            pltpu.VMEM((16, NZ * EDGE), BF16),
            pltpu.VMEM((2, 16, NZ * EDGE), BF16),
            pltpu.VMEM((3 * EZ * NY, ROUTES * NY), BF16),
            pltpu.VMEM((EDGE * EDGE, ROUTES * NY), F32),
            pltpu.VMEM((4, EDGE * EDGE, NY), BF16),
            pltpu.VMEM((ROUTES, EDGE * EDGE, NY), BF16),
            pltpu.VMEM((ROUTES * NY, EZ * NY), BF16),
            pltpu.VMEM((3,) + half, BF16),
            pltpu.VMEM((NZ + 2, 32, NY), F32),
            pltpu.VMEM((12 * 24, NY), F32),
            pltpu.VMEM((2, 6) + tile, F32),
            pltpu.VMEM((2, 6) + tile, F32),
            pltpu.VMEM((nx, 3 * HALF) + tile, F32),
            pltpu.VMEM((nx, 9) + tile, F32),
            pltpu.VMEM((nx, 9) + tile, F32),
            pltpu.VMEM((64, NY), F32),
            pltpu.VMEM((3, nx) + tile, F32),
            pltpu.VMEM((4, nx) + tile, F32),
            pltpu.VMEM(tile, F32),
            pltpu.VMEM((ny - 1,) + tile, F32),
            pltpu.SemaphoreType.DMA((A_END,)),
            pltpu.SemaphoreType.DMA((A_END,)),
            pltpu.SemaphoreType.DMA((nx - 1,)),
            pltpu.SemaphoreType.DMA((nx - 1,)),
            pltpu.SemaphoreType.DMA((3 * nx,)),
            pltpu.SemaphoreType.DMA((3 * nx,)),
            pltpu.SemaphoreType.DMA((ny - 1,)),
            pltpu.SemaphoreType.DMA((ny - 1,)),
        ],
        compiler_params=pltpu.CompilerParams(
            collective_id=0, has_side_effects=True, vmem_limit_bytes=48 << 20
        ),
    )(*[
        pltpu.with_memory_space_constraint(array, pltpu.HBM)
        for array in (
            route.reshape(1, 1, NEL), within, xshift, fractions.transpose(0, 3, 1, 2),
            reference_image, deformed_image,
        )
    ])
    return inc, mis


def solution(mesh):
    nx, ny = mesh.shape["gx"], mesh.shape["gy"]
    placed = (
        P(None, "gx", "gy"),
        P(None, "gx", "gy"),
        P("gx", "gy", None, None),
        P("gx", "gy", None),
        P("gx", "gy", None),
        P("gx", "gy", None, None),
    )
    return jax.shard_map(
        lambda *blocks: body(nx, ny, *blocks),
        mesh=mesh,
        in_specs=placed,
        out_specs=(P(None, None, "gx", "gy"), P(None, "gx", "gy")),
        check_vma=False,
    )
```

```python
import jax
import jax.numpy as jnp
import numpy as np
from jax import lax
from jax.experimental import pallas as pl
from jax.experimental.pallas import tpu as pltpu
from jax.sharding import PartitionSpec as P

EDGE = 16
EZ = 4
EYD = 8
SPAN = 2
ROUTES = 2 * SPAN + 1
NEL = 32
CAP = 8
VOL = 4096
NZ = 64
NY = 128
LAMBDA = 0.05
LAMBDA_PARTS = (float(np.float32(LAMBDA)), 0.0)
MESH = pl.DeviceIdType.MESH
F32 = jnp.float32
BF16 = jnp.bfloat16

N_TABLE, N_BLOCK, N_FACE_X, N_FACE_Y, N_PACK, N_EDGE = 4, 2, 2, 2, 4, 2
A_TABLE = 0
A_BLOCK = A_TABLE + N_TABLE
A_FACE_X = A_BLOCK + N_BLOCK
A_FACE_Y = A_FACE_X + N_FACE_X
A_PACK = A_FACE_Y + N_FACE_Y
A_EDGE = A_PACK + N_PACK
A_END = A_EDGE + N_EDGE

OTHER_ROUTES = (0, 4, 1, 3)
ARRIVAL = (2, 1, 3, 0, 4)
STEPS = ((0, 0), (0, 1), (1, -1), (1, 0), (1, 1))
HALF = len(STEPS)
PAIRS = ((0, 0), (1, 1), (2, 2), (0, 1), (0, 2), (1, 2))


def iota(shape, dim):
    return lax.broadcasted_iota(jnp.int32, shape, dim)


def flag(condition):
    return jnp.where(condition, jnp.float32(1.0), jnp.float32(0.0))


def rolled(value, shift, axis):
    size = value.shape[axis]
    shift = shift % size
    return value if shift == 0 else pltpu.roll(value, shift, axis)


def halves(value):
    high = value.astype(BF16)
    return high, (value - high.astype(F32)).astype(BF16)


def near_exact(left, right):
    a, b = halves(left), halves(right)
    total = jnp.dot(a[0], b[1], preferred_element_type=F32) + jnp.dot(a[1], b[0], preferred_element_type=F32)
    return total + jnp.dot(a[0], b[0], preferred_element_type=F32)


def two_sum(a, b):
    total = a + b
    part = total - a
    return total, (a - (total - part)) + (b - part)


def quick_sum(a, b):
    total = a + b
    return total, b - (total - a)


def cut_in_two(a):
    wide = a * 4097.0
    high = wide - (wide - a)
    return high, a - high


def two_product(a, b):
    value = a * b
    (ah, al), (bh, bl) = cut_in_two(a), cut_in_two(b)
    return value, ((ah * bh - value) + ah * bl + al * bh) + al * bl


def plus(a, b):
    high, low = two_sum(a[0], b[0])
    return quick_sum(high, low + a[1] + b[1])


def minus(a, b):
    return plus(a, (-b[0], -b[1]))


def times(a, b):
    high, low = two_product(a[0], b[0])
    return quick_sum(high, low + (a[0] * b[1] + a[1] * b[0]))


def inverse(pivot, scale):
    sound = pivot[0] > scale[0] * 1e-12
    safe = (jnp.where(sound, pivot[0], 1.0), jnp.where(sound, pivot[1], 0.0))
    guess = 1.0 / safe[0]
    zero = jnp.zeros_like(guess)
    left = minus((zero + 1.0, zero), times(safe, (guess, zero)))
    result = quick_sum(guess, guess * left[0])
    return jnp.where(sound, result[0], 0.0), jnp.where(sound, result[1], 0.0)


def best_coefficients(moment, weight):
    count = 3
    level = (jnp.full_like(moment[0][0], weight[0]), jnp.full_like(moment[0][0], weight[1]))
    shifted = [plus(moment[k + 1], times(level, moment[k])) for k in range(2 * count - 1)]
    matrix = [[shifted[i + j] for j in range(count)] for i in range(count)]
    right = moment[:count]
    scale = [matrix[i][i] for i in range(count)]
    pivots = []
    for i in range(count):
        sound = matrix[i][i][0] > scale[i][0] * 1e-12
        pivots.append(jnp.where(sound, 1.0 / jnp.where(sound, matrix[i][i][0], 1.0), 0.0))
        exact = inverse(matrix[i][i], scale[i]) if i + 1 < count else None
        for j in range(i + 1, count):
            ratio = times(matrix[i][j], exact)
            for k in range(j, count):
                matrix[j][k] = minus(matrix[j][k], times(ratio, matrix[i][k]))
            right[j] = minus(right[j], times(ratio, right[i]))
    answer = [None] * count
    for i in reversed(range(count)):
        value = right[i][0]
        for j in range(i + 1, count):
            value = value - matrix[i][j][0] * answer[j]
        answer[i] = value * pivots[i]
    return answer


def hats(position):
    upper = (position.astype(F32) + 0.5) / EDGE
    return 1.0 - upper, upper


def kernel(
    nx, ny, route_hbm, within_hbm, xshift_hbm, fractions_hbm, ref_hbm, dfm_hbm, inc, mis,
    route, within, xshift, fractions, ref, dfm, lsem, gossip,
    xb, tsend, trecv, fxs, fxr, fys, fyr, pmat, pacc, psend, precv, qmat, grad, refp, xrow, es, er, sg,
    kd, k1, rrow, rr, vv, hs, hr, ssem, rsem, gssem, grsem, rssem, rrsem, hssem, hrsem,
):
    p, q = lax.axis_index("gx"), lax.axis_index("gy")

    def at(dp, dq):
        return (lax.rem(p + dp + 2 * nx, nx), lax.rem(q + dq + 2 * ny, ny))

    def copy(src, dst, send_sem, recv_sem, dp, dq):
        c = pltpu.make_async_remote_copy(
            src_ref=src, dst_ref=dst, send_sem=send_sem, recv_sem=recv_sem,
            device_id=at(dp, dq), device_id_type=MESH,
        )
        c.start()
        return c

    started = []

    def send(number, src, dst, dp, dq):
        c = copy(src, dst, ssem.at[number], rsem.at[number], dp, dq)
        started.append(c)
        return c

    near = ((0, 2), (0, -2), (0, 1), (0, -1), (1, 0), (-1, 0))
    barrier = pltpu.get_barrier_semaphore()
    for dp, dq in near:
        pl.semaphore_signal(barrier, inc=1, device_id=at(dp, dq), device_id_type=MESH)
    loads = []
    for k, (src, dst) in enumerate((
        (route_hbm, route), (within_hbm, within), (xshift_hbm, xshift), (fractions_hbm, fractions),
        (ref_hbm, ref), (dfm_hbm, dfm),
    )):
        loads.append(pltpu.make_async_copy(src, dst, lsem.at[k]))
        loads[k].start()

    def tell(number, *places):
        for dp, dq in places:
            pl.semaphore_signal(gossip.at[number], inc=1, device_id=at(dp, dq), device_id_type=MESH)

    def hear(number, count):
        pl.semaphore_wait(gossip.at[number], count)

    lane, sub = iota((8, NY), 1), iota((8, NY), 0)
    block, inner = lane >> 4, lane & 15

    for c in loads[:3]:
        c.wait()
    routes = [route[0, 0, e] for e in range(NEL)]
    wanted = jnp.full((8, NY), -1, jnp.int32)
    count = jnp.zeros((8, NY), jnp.int32)
    for e in range(NEL):
        source = jnp.clip(p + xshift[0, 0, e] - 1, 0, nx - 1) - p + 1
        code = ((source * EZ + e // EYD) * EYD + within[0, 0, e]) * EDGE
        hit = sub == routes[e]
        wanted = jnp.where(hit & (count == block), inner + code, wanted)
        count = count + jnp.where(hit, 1, 0)
    tsend[...] = wanted

    loads[4].wait()
    refp[0] = jnp.zeros((32, NY), F32)
    refp[NZ + 1] = jnp.zeros((32, NY), F32)
    refp[1 : NZ + 1, 8:24, :] = ref[...].astype(F32)
    fxs[0] = refp[1 : NZ + 1, 8, :].astype(BF16)
    fxs[1] = refp[1 : NZ + 1, 23, :].astype(BF16)
    rows16, lanes16 = iota((16, NY), 0), iota((16, NY), 1)
    pick = ((rows16 == 0) & (lanes16 == 0)) | ((rows16 == 1) & (lanes16 == NY - 1))
    fys[...] = lax.dot_general(
        jnp.where(pick, 1.0, 0.0).astype(BF16), ref[...].reshape(NZ * EDGE, NY),
        (((1,), (1,)), ((), ())), preferred_element_type=F32,
    ).astype(BF16)

    pl.semaphore_wait(barrier, len(near))
    faces_y = [
        send(A_FACE_Y, fys, fyr.at[1], 0, -1),
        send(A_FACE_Y + 1, fys, fyr.at[0], 0, 1),
    ]
    tables = [
        send(A_TABLE + k, tsend, trecv.at[k], 0, r - SPAN) for k, r in enumerate(OTHER_ROUTES)
    ]
    faces_x = [
        send(A_FACE_X, fxs.at[0], fxr.at[1], -1, 0),
        send(A_FACE_X + 1, fxs.at[1], fxr.at[0], 1, 0),
    ]
    blocks = [send(A_BLOCK, dfm_hbm, xb.at[1], -1, 0), send(A_BLOCK + 1, dfm_hbm, xb.at[0], 1, 0)]

    loads[3].wait()
    element = sub * EYD + block
    own_route = jnp.zeros((8, NY), jnp.int32)
    parts = [jnp.zeros((8, NY), jnp.int32) for _ in range(3)]
    for e in range(NEL):
        here = element == e
        own_route = jnp.where(here, routes[e], own_route)
        parts = [jnp.where(here, fractions[0, c, 0, e], parts[c]) for c in range(3)]
    slot = jnp.zeros((8, NY), jnp.int32)
    for e in range(NEL):
        slot = slot + jnp.where((element > e) & (own_route == routes[e]), 1, 0)
    turn = jnp.zeros((8, NY), jnp.int32)
    for k, r in enumerate(ARRIVAL):
        turn = jnp.where(own_route == r, k, turn)
    first = (turn * CAP + slot) * EDGE
    portion = [part.astype(F32) / EDGE for part in parts]
    target0 = first + inner
    target1 = first + jnp.minimum(inner + 1, EDGE - 1)

    for z in range(EZ):
        def fill_place(b, _):
            row = b * NY + iota((NY, NY), 0)
            high = portion[2][z : z + 1]
            place = jnp.where(row == target0[z : z + 1], 1.0 - high, 0.0)
            place = place + jnp.where(row == target1[z : z + 1], high, 0.0)
            qmat[pl.ds(pl.multiple_of(b * NY, NY), NY), z * NY : (z + 1) * NY] = place.astype(BF16)
            return 0

        lax.fori_loop(0, ROUTES, fill_place, 0)

    for c in tables:
        c.wait_recv()
    tell(3, (0, 4), (0, -4))
    asked = []
    for r in range(ROUTES):
        if r == SPAN:
            asked.append(wanted[r : r + 1])
        else:
            k = OTHER_ROUTES.index(r)
            asked.append(trecv[k, r : r + 1, :])
    asked = jnp.concatenate(asked, axis=1)

    def fill_pack(b, _):
        row = b * NY + iota((NY, ROUTES * NY), 0)
        pmat[pl.ds(pl.multiple_of(b * NY, NY), NY), :] = jnp.where(row == asked, 1.0, 0.0).astype(BF16)
        return 0

    lax.fori_loop(0, 3 * EZ, fill_pack, 0)

    def brick_rows(source):
        return jnp.concatenate(
            [source[z * EDGE : (z + 1) * EDGE].reshape(EDGE * EDGE, NY) for z in range(EZ)], axis=1
        )

    width = EZ * NY
    loads[5].wait()
    pacc[...] = jnp.dot(brick_rows(dfm), pmat[width : 2 * width, :], preferred_element_type=F32)

    for c in faces_x:
        c.wait_recv()
    tell(0, (1, 0), (-1, 0))
    for c in faces_y:
        c.wait_recv()
    refp[1 : NZ + 1, 7, :] = fxr[0].astype(F32) * flag(p > 0)
    refp[1 : NZ + 1, 24, :] = fxr[1].astype(F32) * flag(p < nx - 1)
    here, there = iota((NY, NY), 1), iota((NY, NY), 0)
    differ = jnp.where(there == here + 1, 0.5, jnp.where(there == here - 1, -0.5, 0.0)).astype(BF16)
    rows32, lanes32 = iota((32, NY), 0), iota((32, NY), 1)
    ends = jnp.where(
        (rows32 == 1) & (lanes32 == 0), flag(q > 0) * -0.5,
        jnp.where((rows32 == 16) & (lanes32 == NY - 1), flag(q < ny - 1) * 0.5, 0.0),
    ).astype(BF16)
    sides = jnp.concatenate([fyr[0], fyr[1]], axis=0)
    along_y = jnp.dot(ref[...].reshape(NZ * EDGE, NY), differ, preferred_element_type=F32)
    along_y = along_y + lax.dot_general(sides, ends, (((0,), (0,)), ((), ())), preferred_element_type=F32)
    grad[2] = along_y.astype(BF16).reshape(NZ, EDGE, NY)

    def slope(b, _):
        base = b * 4
        below, above = refp[pl.ds(base, 4), 8:24, :], refp[pl.ds(base + 2, 4), 8:24, :]
        grad[0, pl.ds(base, 4)] = ((above - below) * 0.5).astype(BF16)
        left, right = refp[pl.ds(base + 1, 4), 7:23, :], refp[pl.ds(base + 1, 4), 9:25, :]
        grad[1, pl.ds(base, 4)] = ((right - left) * 0.5).astype(BF16)
        return 0

    lax.fori_loop(0, NZ // 4, slope, 0)

    rowm, colm = iota((24, 96), 0), iota((24, 96), 1)
    low_x, high_x = hats(colm & 15)
    order = rowm >> 3
    weight_x = jnp.where(order == 0, low_x * low_x, jnp.where(order == 1, low_x * high_x, high_x * high_x))
    weight_x = jnp.where((rowm & 7) == (colm >> 4), weight_x, 0.0)
    weights_x = jnp.concatenate(halves(weight_x), axis=0)

    def moments(z, _):
        total = [[None] * 6 for _ in range(3)]
        for i in range(EDGE):
            g = [grad[c, z * EDGE + i].astype(F32) for c in range(3)]
            high = (i + 0.5) / EDGE
            low = 1.0 - high
            for k, (a, b) in enumerate(PAIRS):
                product = g[a] * g[b]
                for m, weight in enumerate((low * low, low * high, high * high)):
                    term = product * weight
                    total[m][k] = term if i == 0 else total[m][k] + term
        for m in range(3):
            parts = [
                jnp.dot(weights_x, part, preferred_element_type=F32)
                for part in halves(jnp.concatenate(total[m], axis=0))
            ]
            rows = (parts[1][:24] + parts[0][24:]) + parts[0][:24]
            xrow[pl.ds(pl.multiple_of((z * 3 + m) * 24, 24), 24), :] = rows
        return 0

    lax.fori_loop(0, EZ, moments, 0)
    fine, coarse = iota((NY, 3 * NY), 0), iota((NY, 3 * NY), 1)
    low_y, high_y = hats(fine & 15)
    row_y, node_y, step_y = fine >> 4, (coarse & 15) - 4, (coarse >> 7) - 1
    starts, closes = row_y == node_y, row_y + 1 == node_y
    mixed = low_y * high_y
    weight_y = jnp.where(
        step_y == 1, jnp.where(starts, mixed, 0.0),
        jnp.where(
            step_y == -1, jnp.where(closes, mixed, 0.0),
            jnp.where(starts, low_y * low_y, 0.0) + jnp.where(closes, high_y * high_y, 0.0),
        ),
    ) * (1.0 / VOL)
    yrow = near_exact(xrow[...], weight_y)
    on = [block == z for z in range(EZ + 1)]
    mine = [[None] * HALF for _ in range(3)]
    for m in range(3):
        for k, (dz, dy) in enumerate(STEPS):
            def term(z, depth):
                start = (z * 3 + depth) * 24 + m * 8
                return yrow[start : start + 8, (dy + 1) * NY : (dy + 2) * NY]

            total = jnp.zeros((8, NY), F32)
            for z in range(EZ):
                if dz == 1:
                    total = jnp.where(on[z], term(z, 1), total)
                else:
                    total = total + jnp.where(on[z], term(z, 0), 0.0) + jnp.where(on[z + 1], term(z, 2), 0.0)
            mine[m][k] = total
    for m in range(3):
        for part, ks in enumerate(((0, 1, 2), (3, 4))):
            upper, lower = jnp.zeros((8, NY), F32), jnp.zeros((8, NY), F32)
            for k in ks:
                offset = 5 * (k % 3)
                spot = (inner >= offset) & (inner < offset + 5)
                upper = jnp.where(spot, rolled(mine[m][k], offset - 8, 1), upper)
                lower = jnp.where(spot, rolled(mine[m][k], offset - 4, 1), lower)
            es[0, m * 2 + part], es[1, m * 2 + part] = upper, lower
    edges = [send(A_EDGE, es.at[0], er.at[0], 0, 1), send(A_EDGE + 1, es.at[1], er.at[1], 0, -1)]
    hear(0, 2)
    tell(1, (1, 0), (-1, 0))
    blocks[1].wait_recv()
    pacc[...] += jnp.dot(brick_rows(xb[0]), pmat[0:width, :], preferred_element_type=F32)
    blocks[0].wait_recv()
    last = brick_rows(xb[1])

    def packed(r):
        part = jnp.dot(last, pmat[2 * width : 3 * width, r * NY : (r + 1) * NY], preferred_element_type=F32)
        return (pacc[:, r * NY : (r + 1) * NY] + part).astype(BF16)

    packs = []
    for k, r in enumerate(OTHER_ROUTES):
        psend[k] = packed(r)
        packs.append(send(A_PACK + k, psend.at[k], precv.at[r], 0, SPAN - r))
    precv[SPAN] = packed(SPAN)
    hear(1, 2)
    tell(2, (1, 0), (-1, 0))
    hear(3, 2)
    tell(4, (0, 8), (0, -8))

    for c in edges:
        c.wait_recv()
    for m in range(3):
        for k in range(HALF):
            offset, part = 5 * (k % 3), k // 3
            below = jnp.where(inner < 5, rolled(er[0, m * 2 + part], -offset, 1), 0.0) * flag(q > 0)
            above = jnp.where(inner >= 12, rolled(er[1, m * 2 + part], 12 - offset, 1), 0.0) * flag(q < ny - 1)
            sg[p, m * HALF + k] = mine[m][k] + below + above
    spread = []
    for k in sorted(range(1, nx), key=lambda k: (-min(k, nx - k), k)):
        spread.append(copy(sg.at[p], sg.at[p], gssem.at[k - 1], grsem.at[k - 1], k, 0))
    started.extend(spread)

    column = inner - 4
    own = (column >= 0) & (column < EYD) & (block <= EZ) & (sub < 3)
    inside = (q * EYD + column < ny * EYD) & (sub < 3)
    pacc[:, : EZ * NY] = jnp.dot(precv[SPAN], qmat[0:NY, :], preferred_element_type=F32)

    def placed(at, pair):
        for r in pair:
            packs[OTHER_ROUTES.index(r)].wait_recv()
        bricks = jnp.concatenate([precv[r] for r in pair], axis=1)
        return jnp.dot(bricks, qmat[at * NY : (at + 2) * NY, :], preferred_element_type=F32)

    pacc[:, : EZ * NY] += placed(1, ARRIVAL[1:3])
    fetched = pacc[:, : EZ * NY] + placed(3, ARRIVAL[3:5])
    row8, col16 = iota((8, EDGE), 0), iota((8, EDGE), 1)
    low_j, high_j = hats(iota((EDGE, 1), 0))
    for z in range(EZ):
        voxels = fetched[:, z * NY : (z + 1) * NY].reshape(EDGE, EDGE, NY)
        high = portion[1][z : z + 1].reshape(1, 1, NY)
        ahead = jnp.concatenate([voxels[:, 1:], voxels[:, EDGE - 1 :]], axis=1)
        voxels = (1.0 - high) * voxels + high * ahead
        high = portion[0][z : z + 1].reshape(1, 1, NY)
        ahead = jnp.concatenate([voxels[1:], voxels[EDGE - 1 :]], axis=0)
        voxels = (1.0 - high) * voxels + high * ahead
        left = refp[1 + z * EDGE : 1 + (z + 1) * EDGE, 8:24, :] - voxels
        mis[z * EDGE : (z + 1) * EDGE] = left
        sums = [[None] * 3 for _ in range(2)]
        for i in range(EDGE):
            high = (i + 0.5) / EDGE
            for c in range(3):
                value = grad[c, z * EDGE + i].astype(F32) * left[i]
                for m, weight in enumerate((1.0 - high, high)):
                    sums[m][c] = value * weight if i == 0 else sums[m][c] + value * weight
        for m in range(2):
            rows = [jnp.sum(sums[m][c] * w, axis=0, keepdims=True) for w in (low_j, high_j) for c in range(3)]
            blank = jnp.zeros((1, NY), F32)
            start = (z * 2 + m) * 8
            rrow[start : start + 8, :] = jnp.concatenate(rows[:3] + [blank] + rows[3:] + [blank], axis=0)
    fine, coarse = iota((NY, NY), 0), iota((NY, NY), 1)
    low_y, high_y = hats(fine & 15)
    row_y, node_y = fine >> 4, (coarse & 15) - 4
    weight_y = (
        jnp.where(row_y == node_y, low_y, 0.0) + jnp.where(row_y + 1 == node_y, high_y, 0.0)
    ) * (1.0 / VOL)
    weight_y = weight_y.astype(BF16)
    high, low = halves(rrow[...])
    nodes = jnp.dot(low, weight_y, preferred_element_type=F32) + jnp.dot(high, weight_y, preferred_element_type=F32)
    tile = jnp.zeros((8, NY), F32)
    for z in range(EZ):
        for m in range(2):
            start = (z * 2 + m) * 8
            tile = tile + jnp.where(on[z + m], nodes[start : start + 8], 0.0)
    rr[1, p] = tile
    hear(2, 2)
    sent = []
    for k in sorted(range(nx), key=lambda k: (-min(k, nx - k), k)):
        for dq in (1, -1, 0):
            if k or dq:
                number = k * 3 + 1 - dq
                sent.append(copy(rr.at[1, p], rr.at[1 - dq, p], rssem.at[number], rrsem.at[number], k, dq))
    started.extend(sent)

    for c in spread:
        c.wait_recv()
    for x in range(nx):
        for k, (dz, dy) in enumerate(STEPS):
            level, cross = sg[x, k], sg[x, HALF + k]
            if x > 0:
                level = level + sg[x - 1, 2 * HALF + k]
            kd[x, 4 + k], k1[x, 4 + k] = level, cross
            if k:
                shift = dz * 16 + dy
                kd[x, 4 - k], k1[x, 4 - k] = rolled(level, shift, 1), rolled(cross, shift, 1)

    for c in sent:
        c.wait_recv()
    below, above = flag(q > 0), flag(q < ny - 1)
    tiles = []
    for x in range(nx):
        from_below = jnp.where(inner < 8, rolled(rr[0, x], -8, 1), 0.0) * below
        from_above = jnp.where(inner >= 8, rolled(rr[2, x], 8, 1), 0.0) * above
        tiles.append(rr[1, x] + from_below + from_above)
    for x in range(nx):
        whole = tiles[x] + rolled(tiles[x - 1], 4, 0) if x else tiles[x]
        vv[0, x] = jnp.where(inside, whole, 0.0)

    for step in range(3):
        straight = [jnp.zeros((8, NY), F32) for _ in range(nx)]
        crossed = [jnp.zeros((8, NY), F32) for _ in range(nx)]
        for x in range(nx):
            u = [vv[step, x, c : c + 1, :] for c in range(3)]
            second = jnp.where(sub == 0, u[0], jnp.where((sub == 1) | (sub == 3), u[1], u[2]))
            third = jnp.where(sub == 5, u[1], u[0])
            for t in range(9):
                shift = -((t // 3 - 1) * 16 + t % 3 - 1)
                moved, other = rolled(second, shift, 1), rolled(third, shift, 1)
                level, cross = kd[x, t], k1[x, t]
                straight[x] = straight[x] + level * moved
                crossed[x] = crossed[x] + level * other
                if x + 1 < nx:
                    straight[x + 1] = straight[x + 1] + cross * moved
                    crossed[x + 1] = crossed[x + 1] + cross * other
                if x > 0:
                    before = k1[x - 1, t]
                    straight[x - 1] = straight[x - 1] + before * moved
                    crossed[x - 1] = crossed[x - 1] + before * other
        for x in range(nx):
            a, b = straight[x], crossed[x]
            out = [
                a[0:1] + a[3:4] + a[4:5],
                a[1:2] + a[5:6] + b[3:4],
                a[2:3] + b[4:5] + b[5:6],
            ]
            image = jnp.where(sub == 0, out[0], jnp.where(sub == 1, out[1], out[2]))
            vv[step + 1, x] = jnp.where(inside, image, 0.0)

    zero = jnp.zeros((8, NY), F32)
    tile = zero
    for k in range(6):
        high, low = zero, zero
        for x in range(nx):
            value, rest = two_product(vv[k // 2, x], vv[(k + 1) // 2, x])
            high, lost = two_sum(high, value)
            low = low + (lost + rest)
        value, lost = two_sum(high[0:1], high[1:2])
        value, more = two_sum(value, high[2:3])
        rest = (low[0:1] + low[1:2]) + (low[2:3] + (lost + more))
        owned = own[0:1]
        both = jnp.where(owned, value, 0.0) + rolled(jnp.where(owned, rest, 0.0), 8, 1)
        tile = jnp.where(sub == k, both, tile)
    hear(4, 2)
    hs[...] = tile

    sums = {}
    for k in sorted(range(1, ny), key=lambda k: (-min(k, ny - k), k)):
        sums[k] = copy(hs, hr.at[k - 1], hssem.at[k - 1], hrsem.at[k - 1], 0, k)
    for c in started:
        c.wait_send()
    rest = zero
    for k in sorted(range(1, ny), key=lambda k: (min(k, ny - k), k)):
        sums[k].wait_recv()
        tile, lost = two_sum(tile, hr[k - 1])
        rest = rest + lost
    for shift in (64, 32, 16, 8, 4, 2, 1):
        tile, lost = two_sum(tile, rolled(tile, shift, 1))
        rest = (rest + rolled(rest, shift, 1)) + lost
    tile, rest = quick_sum(tile, rest)

    moment = [(tile[k : k + 1], rest[k : k + 1]) for k in range(6)]
    answer = best_coefficients(moment, LAMBDA_PARTS)
    for k in range(1, ny):
        sums[k].wait_send()
    found = answer[0] * vv[0, p] + answer[1] * vv[1, p] + answer[2] * vv[2, p]
    for c in range(3):
        for z in range(EZ + 1):
            inc[c, z, 0:1, :] = found[c : c + 1, z * 16 + 4 : z * 16 + 4 + EYD]


def body(nx, ny, reference_image, deformed_image, route, within, xshift, fractions):
    vmem = pl.BlockSpec(memory_space=pltpu.VMEM)
    half = (NZ, EDGE, NY)
    tile = (8, NY)
    inc, mis = pl.pallas_call(
        lambda *refs: kernel(nx, ny, *refs),
        name="correlate",
        out_shape=(jax.ShapeDtypeStruct((3, EZ + 1, 1, EYD), F32), jax.ShapeDtypeStruct(half, F32)),
        in_specs=[pl.BlockSpec(memory_space=pltpu.HBM)] * 6,
        out_specs=(vmem, vmem),
        scratch_shapes=[
            pltpu.SMEM((1, 1, NEL), jnp.int32),
            pltpu.SMEM((1, 1, NEL), jnp.int32),
            pltpu.SMEM((1, 1, NEL), jnp.int32),
            pltpu.SMEM((1, 3, 1, NEL), jnp.int32),
            pltpu.VMEM(half, BF16),
            pltpu.VMEM(half, BF16),
            pltpu.SemaphoreType.DMA((6,)),
            pltpu.SemaphoreType.REGULAR((5,)),
            pltpu.VMEM((2,) + half, BF16),
            pltpu.VMEM(tile, jnp.int32),
            pltpu.VMEM((4,) + tile, jnp.int32),
            pltpu.VMEM((2, NZ, NY), BF16),
            pltpu.VMEM((2, NZ, NY), BF16),
            pltpu.VMEM((16, NZ * EDGE), BF16),
            pltpu.VMEM((2, 16, NZ * EDGE), BF16),
            pltpu.VMEM((3 * EZ * NY, ROUTES * NY), BF16),
            pltpu.VMEM((EDGE * EDGE, ROUTES * NY), F32),
            pltpu.VMEM((4, EDGE * EDGE, NY), BF16),
            pltpu.VMEM((ROUTES, EDGE * EDGE, NY), BF16),
            pltpu.VMEM((ROUTES * NY, EZ * NY), BF16),
            pltpu.VMEM((3,) + half, BF16),
            pltpu.VMEM((NZ + 2, 32, NY), F32),
            pltpu.VMEM((12 * 24, NY), F32),
            pltpu.VMEM((2, 6) + tile, F32),
            pltpu.VMEM((2, 6) + tile, F32),
            pltpu.VMEM((nx, 3 * HALF) + tile, F32),
            pltpu.VMEM((nx, 9) + tile, F32),
            pltpu.VMEM((nx, 9) + tile, F32),
            pltpu.VMEM((64, NY), F32),
            pltpu.VMEM((3, nx) + tile, F32),
            pltpu.VMEM((4, nx) + tile, F32),
            pltpu.VMEM(tile, F32),
            pltpu.VMEM((ny - 1,) + tile, F32),
            pltpu.SemaphoreType.DMA((A_END,)),
            pltpu.SemaphoreType.DMA((A_END,)),
            pltpu.SemaphoreType.DMA((nx - 1,)),
            pltpu.SemaphoreType.DMA((nx - 1,)),
            pltpu.SemaphoreType.DMA((3 * nx,)),
            pltpu.SemaphoreType.DMA((3 * nx,)),
            pltpu.SemaphoreType.DMA((ny - 1,)),
            pltpu.SemaphoreType.DMA((ny - 1,)),
        ],
        compiler_params=pltpu.CompilerParams(
            collective_id=0, has_side_effects=True, vmem_limit_bytes=48 << 20
        ),
    )(*[
        pltpu.with_memory_space_constraint(array, pltpu.HBM)
        for array in (
            route.reshape(1, 1, NEL), within, xshift, fractions.transpose(0, 3, 1, 2),
            reference_image, deformed_image,
        )
    ])
    return inc, mis


def solution(mesh):
    nx, ny = mesh.shape["gx"], mesh.shape["gy"]
    placed = (
        P(None, "gx", "gy"),
        P(None, "gx", "gy"),
        P("gx", "gy", None, None),
        P("gx", "gy", None),
        P("gx", "gy", None),
        P("gx", "gy", None, None),
    )
    return jax.shard_map(
        lambda *blocks: body(nx, ny, *blocks),
        mesh=mesh,
        in_specs=placed,
        out_specs=(P(None, None, "gx", "gy"), P(None, "gx", "gy")),
        check_vma=False,
    )
```

```python
import jax
import jax.numpy as jnp
import numpy as np
from jax import lax
from jax.experimental import pallas as pl
from jax.experimental.pallas import tpu as pltpu
from jax.sharding import PartitionSpec as P

EDGE = 16
EZ = 4
EYD = 8
SPAN = 2
ROUTES = 2 * SPAN + 1
NEL = 32
CAP = 8
VOL = 4096
NZ = 64
NY = 128
LAMBDA = 0.05
LAMBDA_PARTS = (float(np.float32(LAMBDA)), 0.0)
MESH = pl.DeviceIdType.MESH
F32 = jnp.float32
BF16 = jnp.bfloat16

N_TABLE, N_BLOCK, N_FACE_X, N_FACE_Y, N_PACK, N_EDGE = 4, 2, 2, 2, 4, 2
A_TABLE = 0
A_BLOCK = A_TABLE + N_TABLE
A_FACE_X = A_BLOCK + N_BLOCK
A_FACE_Y = A_FACE_X + N_FACE_X
A_PACK = A_FACE_Y + N_FACE_Y
A_EDGE = A_PACK + N_PACK
A_END = A_EDGE + N_EDGE

OTHER_ROUTES = (0, 4, 1, 3)
ARRIVAL = (2, 1, 3, 0, 4)
STEPS = ((0, 0), (0, 1), (1, -1), (1, 0), (1, 1))
HALF = len(STEPS)
PAIRS = ((0, 0), (1, 1), (2, 2), (0, 1), (0, 2), (1, 2))


def iota(shape, dim):
    return lax.broadcasted_iota(jnp.int32, shape, dim)


def flag(condition):
    return jnp.where(condition, jnp.float32(1.0), jnp.float32(0.0))


def rolled(value, shift, axis):
    size = value.shape[axis]
    shift = shift % size
    return value if shift == 0 else pltpu.roll(value, shift, axis)


def halves(value):
    high = value.astype(BF16)
    return high, (value - high.astype(F32)).astype(BF16)


def near_exact(left, right):
    a, b = halves(left), halves(right)
    total = jnp.dot(a[0], b[1], preferred_element_type=F32) + jnp.dot(a[1], b[0], preferred_element_type=F32)
    return total + jnp.dot(a[0], b[0], preferred_element_type=F32)


def two_sum(a, b):
    total = a + b
    part = total - a
    return total, (a - (total - part)) + (b - part)


def quick_sum(a, b):
    total = a + b
    return total, b - (total - a)


def cut_in_two(a):
    wide = a * 4097.0
    high = wide - (wide - a)
    return high, a - high


def two_product(a, b):
    value = a * b
    (ah, al), (bh, bl) = cut_in_two(a), cut_in_two(b)
    return value, ((ah * bh - value) + ah * bl + al * bh) + al * bl


def plus(a, b):
    high, low = two_sum(a[0], b[0])
    return quick_sum(high, low + a[1] + b[1])


def minus(a, b):
    return plus(a, (-b[0], -b[1]))


def times(a, b):
    high, low = two_product(a[0], b[0])
    return quick_sum(high, low + (a[0] * b[1] + a[1] * b[0]))


def inverse(pivot, scale):
    sound = pivot[0] > scale[0] * 1e-12
    safe = (jnp.where(sound, pivot[0], 1.0), jnp.where(sound, pivot[1], 0.0))
    guess = 1.0 / safe[0]
    zero = jnp.zeros_like(guess)
    left = minus((zero + 1.0, zero), times(safe, (guess, zero)))
    result = quick_sum(guess, guess * left[0])
    return jnp.where(sound, result[0], 0.0), jnp.where(sound, result[1], 0.0)


def best_coefficients(moment, weight):
    count = 3
    level = (jnp.full_like(moment[0][0], weight[0]), jnp.full_like(moment[0][0], weight[1]))
    shifted = [plus(moment[k + 1], times(level, moment[k])) for k in range(2 * count - 1)]
    matrix = [[shifted[i + j] for j in range(count)] for i in range(count)]
    right = moment[:count]
    scale = [matrix[i][i] for i in range(count)]
    pivots = []
    for i in range(count):
        sound = matrix[i][i][0] > scale[i][0] * 1e-12
        pivots.append(jnp.where(sound, 1.0 / jnp.where(sound, matrix[i][i][0], 1.0), 0.0))
        exact = inverse(matrix[i][i], scale[i]) if i + 1 < count else None
        for j in range(i + 1, count):
            ratio = times(matrix[i][j], exact)
            for k in range(j, count):
                matrix[j][k] = minus(matrix[j][k], times(ratio, matrix[i][k]))
            right[j] = minus(right[j], times(ratio, right[i]))
    answer = [None] * count
    for i in reversed(range(count)):
        value = right[i][0]
        for j in range(i + 1, count):
            value = value - matrix[i][j][0] * answer[j]
        answer[i] = value * pivots[i]
    return answer


def hats(position):
    upper = (position.astype(F32) + 0.5) / EDGE
    return 1.0 - upper, upper


def kernel(
    nx, ny, route_hbm, within_hbm, xshift_hbm, fractions_hbm, ref_hbm, dfm_hbm, inc, mis,
    route, within, xshift, fractions, ref, dfm, lsem, gossip,
    xb, tsend, trecv, fxs, fxr, fys, fyr, pmat, pacc, psend, precv, qmat, grad, refp, xrow, es, er, sg,
    kd, k1, rrow, rr, vv, hs, hr, ssem, rsem, gssem, grsem, rssem, rrsem, hssem, hrsem,
):
    p, q = lax.axis_index("gx"), lax.axis_index("gy")

    def at(dp, dq):
        return (lax.rem(p + dp + 2 * nx, nx), lax.rem(q + dq + 2 * ny, ny))

    def copy(src, dst, send_sem, recv_sem, dp, dq):
        c = pltpu.make_async_remote_copy(
            src_ref=src, dst_ref=dst, send_sem=send_sem, recv_sem=recv_sem,
            device_id=at(dp, dq), device_id_type=MESH,
        )
        c.start()
        return c

    started = []

    def send(number, src, dst, dp, dq):
        c = copy(src, dst, ssem.at[number], rsem.at[number], dp, dq)
        started.append(c)
        return c

    near = ((0, 2), (0, -2), (0, 1), (0, -1), (1, 0), (-1, 0))
    barrier = pltpu.get_barrier_semaphore()
    for dp, dq in near:
        pl.semaphore_signal(barrier, inc=1, device_id=at(dp, dq), device_id_type=MESH)
    loads = []
    for k, (src, dst) in enumerate((
        (route_hbm, route), (within_hbm, within), (xshift_hbm, xshift), (fractions_hbm, fractions),
        (ref_hbm, ref), (dfm_hbm, dfm),
    )):
        loads.append(pltpu.make_async_copy(src, dst, lsem.at[k]))
        loads[k].start()

    def tell(number, *places):
        for dp, dq in places:
            pl.semaphore_signal(gossip.at[number], inc=1, device_id=at(dp, dq), device_id_type=MESH)

    def hear(number, count):
        pl.semaphore_wait(gossip.at[number], count)

    lane, sub = iota((8, NY), 1), iota((8, NY), 0)
    block, inner = lane >> 4, lane & 15

    for c in loads[:3]:
        c.wait()
    routes = [route[0, 0, e] for e in range(NEL)]
    wanted = jnp.full((8, NY), -1, jnp.int32)
    count = jnp.zeros((8, NY), jnp.int32)
    for e in range(NEL):
        source = jnp.clip(p + xshift[0, 0, e] - 1, 0, nx - 1) - p + 1
        code = ((source * EZ + e // EYD) * EYD + within[0, 0, e]) * EDGE
        hit = sub == routes[e]
        wanted = jnp.where(hit & (count == block), inner + code, wanted)
        count = count + jnp.where(hit, 1, 0)
    tsend[...] = wanted

    loads[4].wait()
    refp[0] = jnp.zeros((32, NY), F32)
    refp[NZ + 1] = jnp.zeros((32, NY), F32)
    refp[1 : NZ + 1, 8:24, :] = ref[...].astype(F32)
    fxs[0] = refp[1 : NZ + 1, 8, :].astype(BF16)
    fxs[1] = refp[1 : NZ + 1, 23, :].astype(BF16)
    rows16, lanes16 = iota((16, NY), 0), iota((16, NY), 1)
    pick = ((rows16 == 0) & (lanes16 == 0)) | ((rows16 == 1) & (lanes16 == NY - 1))
    fys[...] = lax.dot_general(
        jnp.where(pick, 1.0, 0.0).astype(BF16), ref[...].reshape(NZ * EDGE, NY),
        (((1,), (1,)), ((), ())), preferred_element_type=F32,
    ).astype(BF16)

    pl.semaphore_wait(barrier, len(near))
    faces_y = [
        send(A_FACE_Y, fys, fyr.at[1], 0, -1),
        send(A_FACE_Y + 1, fys, fyr.at[0], 0, 1),
    ]
    tables = [
        send(A_TABLE + k, tsend, trecv.at[k], 0, r - SPAN) for k, r in enumerate(OTHER_ROUTES)
    ]
    faces_x = [
        send(A_FACE_X, fxs.at[0], fxr.at[1], -1, 0),
        send(A_FACE_X + 1, fxs.at[1], fxr.at[0], 1, 0),
    ]
    blocks = [send(A_BLOCK, dfm_hbm, xb.at[1], -1, 0), send(A_BLOCK + 1, dfm_hbm, xb.at[0], 1, 0)]

    loads[3].wait()
    element = sub * EYD + block
    own_route = jnp.zeros((8, NY), jnp.int32)
    parts = [jnp.zeros((8, NY), jnp.int32) for _ in range(3)]
    for e in range(NEL):
        here = element == e
        own_route = jnp.where(here, routes[e], own_route)
        parts = [jnp.where(here, fractions[0, c, 0, e], parts[c]) for c in range(3)]
    slot = jnp.zeros((8, NY), jnp.int32)
    for e in range(NEL):
        slot = slot + jnp.where((element > e) & (own_route == routes[e]), 1, 0)
    turn = jnp.zeros((8, NY), jnp.int32)
    for k, r in enumerate(ARRIVAL):
        turn = jnp.where(own_route == r, k, turn)
    first = (turn * CAP + slot) * EDGE
    portion = [part.astype(F32) / EDGE for part in parts]
    target0 = first + inner
    target1 = first + jnp.minimum(inner + 1, EDGE - 1)

    for z in range(EZ):
        def fill_place(b, _):
            row = b * NY + iota((NY, NY), 0)
            high = portion[2][z : z + 1]
            place = jnp.where(row == target0[z : z + 1], 1.0 - high, 0.0)
            place = place + jnp.where(row == target1[z : z + 1], high, 0.0)
            qmat[pl.ds(pl.multiple_of(b * NY, NY), NY), z * NY : (z + 1) * NY] = place.astype(BF16)
            return 0

        lax.fori_loop(0, ROUTES, fill_place, 0)

    for c in faces_x:
        c.wait_recv()
    tell(0, (1, 0), (-1, 0))
    for c in faces_y:
        c.wait_recv()
    refp[1 : NZ + 1, 7, :] = fxr[0].astype(F32) * flag(p > 0)
    refp[1 : NZ + 1, 24, :] = fxr[1].astype(F32) * flag(p < nx - 1)
    here, there = iota((NY, NY), 1), iota((NY, NY), 0)
    differ = jnp.where(there == here + 1, 0.5, jnp.where(there == here - 1, -0.5, 0.0)).astype(BF16)
    rows32, lanes32 = iota((32, NY), 0), iota((32, NY), 1)
    ends = jnp.where(
        (rows32 == 1) & (lanes32 == 0), flag(q > 0) * -0.5,
        jnp.where((rows32 == 16) & (lanes32 == NY - 1), flag(q < ny - 1) * 0.5, 0.0),
    ).astype(BF16)
    sides = jnp.concatenate([fyr[0], fyr[1]], axis=0)
    along_y = jnp.dot(ref[...].reshape(NZ * EDGE, NY), differ, preferred_element_type=F32)
    along_y = along_y + lax.dot_general(sides, ends, (((0,), (0,)), ((), ())), preferred_element_type=F32)
    grad[2] = along_y.astype(BF16).reshape(NZ, EDGE, NY)

    def slope(b, _):
        base = b * 4
        below, above = refp[pl.ds(base, 4), 8:24, :], refp[pl.ds(base + 2, 4), 8:24, :]
        grad[0, pl.ds(base, 4)] = ((above - below) * 0.5).astype(BF16)
        left, right = refp[pl.ds(base + 1, 4), 7:23, :], refp[pl.ds(base + 1, 4), 9:25, :]
        grad[1, pl.ds(base, 4)] = ((right - left) * 0.5).astype(BF16)
        return 0

    lax.fori_loop(0, NZ // 4, slope, 0)

    rowm, colm = iota((24, 96), 0), iota((24, 96), 1)
    low_x, high_x = hats(colm & 15)
    order = rowm >> 3
    weight_x = jnp.where(order == 0, low_x * low_x, jnp.where(order == 1, low_x * high_x, high_x * high_x))
    weight_x = jnp.where((rowm & 7) == (colm >> 4), weight_x, 0.0)
    weights_x = jnp.concatenate(halves(weight_x), axis=0)

    def moments(z, _):
        total = [[None] * 6 for _ in range(3)]
        for i in range(EDGE):
            g = [grad[c, z * EDGE + i].astype(F32) for c in range(3)]
            high = (i + 0.5) / EDGE
            low = 1.0 - high
            for k, (a, b) in enumerate(PAIRS):
                product = g[a] * g[b]
                for m, weight in enumerate((low * low, low * high, high * high)):
                    term = product * weight
                    total[m][k] = term if i == 0 else total[m][k] + term
        for m in range(3):
            parts = [
                jnp.dot(weights_x, part, preferred_element_type=F32)
                for part in halves(jnp.concatenate(total[m], axis=0))
            ]
            rows = (parts[1][:24] + parts[0][24:]) + parts[0][:24]
            xrow[pl.ds(pl.multiple_of((z * 3 + m) * 24, 24), 24), :] = rows
        return 0

    lax.fori_loop(0, EZ, moments, 0)
    fine, coarse = iota((NY, 3 * NY), 0), iota((NY, 3 * NY), 1)
    low_y, high_y = hats(fine & 15)
    row_y, node_y, step_y = fine >> 4, (coarse & 15) - 4, (coarse >> 7) - 1
    starts, closes = row_y == node_y, row_y + 1 == node_y
    mixed = low_y * high_y
    weight_y = jnp.where(
        step_y == 1, jnp.where(starts, mixed, 0.0),
        jnp.where(
            step_y == -1, jnp.where(closes, mixed, 0.0),
            jnp.where(starts, low_y * low_y, 0.0) + jnp.where(closes, high_y * high_y, 0.0),
        ),
    ) * (1.0 / VOL)
    yrow = near_exact(xrow[...], weight_y)
    on = [block == z for z in range(EZ + 1)]
    mine = [[None] * HALF for _ in range(3)]
    for m in range(3):
        for k, (dz, dy) in enumerate(STEPS):
            def term(z, depth):
                start = (z * 3 + depth) * 24 + m * 8
                return yrow[start : start + 8, (dy + 1) * NY : (dy + 2) * NY]

            total = jnp.zeros((8, NY), F32)
            for z in range(EZ):
                if dz == 1:
                    total = jnp.where(on[z], term(z, 1), total)
                else:
                    total = total + jnp.where(on[z], term(z, 0), 0.0) + jnp.where(on[z + 1], term(z, 2), 0.0)
            mine[m][k] = total
    for m in range(3):
        for part, ks in enumerate(((0, 1, 2), (3, 4))):
            upper, lower = jnp.zeros((8, NY), F32), jnp.zeros((8, NY), F32)
            for k in ks:
                offset = 5 * (k % 3)
                spot = (inner >= offset) & (inner < offset + 5)
                upper = jnp.where(spot, rolled(mine[m][k], offset - 8, 1), upper)
                lower = jnp.where(spot, rolled(mine[m][k], offset - 4, 1), lower)
            es[0, m * 2 + part], es[1, m * 2 + part] = upper, lower
    edges = [send(A_EDGE, es.at[0], er.at[0], 0, 1), send(A_EDGE + 1, es.at[1], er.at[1], 0, -1)]
    for c in tables:
        c.wait_recv()
    tell(3, (0, 4), (0, -4))
    asked = []
    for r in range(ROUTES):
        if r == SPAN:
            asked.append(wanted[r : r + 1])
        else:
            k = OTHER_ROUTES.index(r)
            asked.append(trecv[k, r : r + 1, :])
    asked = jnp.concatenate(asked, axis=1)

    def fill_pack(b, _):
        row = b * NY + iota((NY, ROUTES * NY), 0)
        pmat[pl.ds(pl.multiple_of(b * NY, NY), NY), :] = jnp.where(row == asked, 1.0, 0.0).astype(BF16)
        return 0

    lax.fori_loop(0, 3 * EZ, fill_pack, 0)

    def brick_rows(source):
        return jnp.concatenate(
            [source[z * EDGE : (z + 1) * EDGE].reshape(EDGE * EDGE, NY) for z in range(EZ)], axis=1
        )

    width = EZ * NY
    loads[5].wait()
    pacc[...] = jnp.dot(brick_rows(dfm), pmat[width : 2 * width, :], preferred_element_type=F32)

    hear(0, 2)
    tell(1, (1, 0), (-1, 0))
    blocks[1].wait_recv()
    pacc[...] += jnp.dot(brick_rows(xb[0]), pmat[0:width, :], preferred_element_type=F32)
    blocks[0].wait_recv()
    last = brick_rows(xb[1])

    def packed(r):
        part = jnp.dot(last, pmat[2 * width : 3 * width, r * NY : (r + 1) * NY], preferred_element_type=F32)
        return (pacc[:, r * NY : (r + 1) * NY] + part).astype(BF16)

    packs = []
    for k, r in enumerate(OTHER_ROUTES):
        psend[k] = packed(r)
        packs.append(send(A_PACK + k, psend.at[k], precv.at[r], 0, SPAN - r))
    precv[SPAN] = packed(SPAN)
    hear(1, 2)
    tell(2, (1, 0), (-1, 0))
    hear(3, 2)
    tell(4, (0, 8), (0, -8))

    for c in edges:
        c.wait_recv()
    for m in range(3):
        for k in range(HALF):
            offset, part = 5 * (k % 3), k // 3
            below = jnp.where(inner < 5, rolled(er[0, m * 2 + part], -offset, 1), 0.0) * flag(q > 0)
            above = jnp.where(inner >= 12, rolled(er[1, m * 2 + part], 12 - offset, 1), 0.0) * flag(q < ny - 1)
            sg[p, m * HALF + k] = mine[m][k] + below + above
    spread = []
    for k in sorted(range(1, nx), key=lambda k: (-min(k, nx - k), k)):
        spread.append(copy(sg.at[p], sg.at[p], gssem.at[k - 1], grsem.at[k - 1], k, 0))
    started.extend(spread)

    column = inner - 4
    own = (column >= 0) & (column < EYD) & (block <= EZ) & (sub < 3)
    inside = (q * EYD + column < ny * EYD) & (sub < 3)
    pacc[:, : EZ * NY] = jnp.dot(precv[SPAN], qmat[0:NY, :], preferred_element_type=F32)

    def placed(at, pair):
        for r in pair:
            packs[OTHER_ROUTES.index(r)].wait_recv()
        bricks = jnp.concatenate([precv[r] for r in pair], axis=1)
        return jnp.dot(bricks, qmat[at * NY : (at + 2) * NY, :], preferred_element_type=F32)

    pacc[:, : EZ * NY] += placed(1, ARRIVAL[1:3])
    fetched = pacc[:, : EZ * NY] + placed(3, ARRIVAL[3:5])
    row8, col16 = iota((8, EDGE), 0), iota((8, EDGE), 1)
    low_j, high_j = hats(iota((EDGE, 1), 0))
    for z in range(EZ):
        voxels = fetched[:, z * NY : (z + 1) * NY].reshape(EDGE, EDGE, NY)
        high = portion[1][z : z + 1].reshape(1, 1, NY)
        ahead = jnp.concatenate([voxels[:, 1:], voxels[:, EDGE - 1 :]], axis=1)
        voxels = (1.0 - high) * voxels + high * ahead
        high = portion[0][z : z + 1].reshape(1, 1, NY)
        ahead = jnp.concatenate([voxels[1:], voxels[EDGE - 1 :]], axis=0)
        voxels = (1.0 - high) * voxels + high * ahead
        left = refp[1 + z * EDGE : 1 + (z + 1) * EDGE, 8:24, :] - voxels
        mis[z * EDGE : (z + 1) * EDGE] = left
        sums = [[None] * 3 for _ in range(2)]
        for i in range(EDGE):
            high = (i + 0.5) / EDGE
            for c in range(3):
                value = grad[c, z * EDGE + i].astype(F32) * left[i]
                for m, weight in enumerate((1.0 - high, high)):
                    sums[m][c] = value * weight if i == 0 else sums[m][c] + value * weight
        for m in range(2):
            rows = [jnp.sum(sums[m][c] * w, axis=0, keepdims=True) for w in (low_j, high_j) for c in range(3)]
            blank = jnp.zeros((1, NY), F32)
            start = (z * 2 + m) * 8
            rrow[start : start + 8, :] = jnp.concatenate(rows[:3] + [blank] + rows[3:] + [blank], axis=0)
    fine, coarse = iota((NY, NY), 0), iota((NY, NY), 1)
    low_y, high_y = hats(fine & 15)
    row_y, node_y = fine >> 4, (coarse & 15) - 4
    weight_y = (
        jnp.where(row_y == node_y, low_y, 0.0) + jnp.where(row_y + 1 == node_y, high_y, 0.0)
    ) * (1.0 / VOL)
    weight_y = weight_y.astype(BF16)
    high, low = halves(rrow[...])
    nodes = jnp.dot(low, weight_y, preferred_element_type=F32) + jnp.dot(high, weight_y, preferred_element_type=F32)
    tile = jnp.zeros((8, NY), F32)
    for z in range(EZ):
        for m in range(2):
            start = (z * 2 + m) * 8
            tile = tile + jnp.where(on[z + m], nodes[start : start + 8], 0.0)
    rr[1, p] = tile
    hear(2, 2)
    sent = []
    for k in sorted(range(nx), key=lambda k: (-min(k, nx - k), k)):
        for dq in (1, -1, 0):
            if k or dq:
                number = k * 3 + 1 - dq
                sent.append(copy(rr.at[1, p], rr.at[1 - dq, p], rssem.at[number], rrsem.at[number], k, dq))
    started.extend(sent)

    for c in spread:
        c.wait_recv()
    for x in range(nx):
        for k, (dz, dy) in enumerate(STEPS):
            level, cross = sg[x, k], sg[x, HALF + k]
            if x > 0:
                level = level + sg[x - 1, 2 * HALF + k]
            kd[x, 4 + k], k1[x, 4 + k] = level, cross
            if k:
                shift = dz * 16 + dy
                kd[x, 4 - k], k1[x, 4 - k] = rolled(level, shift, 1), rolled(cross, shift, 1)

    for c in sent:
        c.wait_recv()
    below, above = flag(q > 0), flag(q < ny - 1)
    tiles = []
    for x in range(nx):
        from_below = jnp.where(inner < 8, rolled(rr[0, x], -8, 1), 0.0) * below
        from_above = jnp.where(inner >= 8, rolled(rr[2, x], 8, 1), 0.0) * above
        tiles.append(rr[1, x] + from_below + from_above)
    for x in range(nx):
        whole = tiles[x] + rolled(tiles[x - 1], 4, 0) if x else tiles[x]
        vv[0, x] = jnp.where(inside, whole, 0.0)

    for step in range(3):
        straight = [jnp.zeros((8, NY), F32) for _ in range(nx)]
        crossed = [jnp.zeros((8, NY), F32) for _ in range(nx)]
        for x in range(nx):
            u = [vv[step, x, c : c + 1, :] for c in range(3)]
            second = jnp.where(sub == 0, u[0], jnp.where((sub == 1) | (sub == 3), u[1], u[2]))
            third = jnp.where(sub == 5, u[1], u[0])
            for t in range(9):
                shift = -((t // 3 - 1) * 16 + t % 3 - 1)
                moved, other = rolled(second, shift, 1), rolled(third, shift, 1)
                level, cross = kd[x, t], k1[x, t]
                straight[x] = straight[x] + level * moved
                crossed[x] = crossed[x] + level * other
                if x + 1 < nx:
                    straight[x + 1] = straight[x + 1] + cross * moved
                    crossed[x + 1] = crossed[x + 1] + cross * other
                if x > 0:
                    before = k1[x - 1, t]
                    straight[x - 1] = straight[x - 1] + before * moved
                    crossed[x - 1] = crossed[x - 1] + before * other
        for x in range(nx):
            a, b = straight[x], crossed[x]
            out = [
                a[0:1] + a[3:4] + a[4:5],
                a[1:2] + a[5:6] + b[3:4],
                a[2:3] + b[4:5] + b[5:6],
            ]
            image = jnp.where(sub == 0, out[0], jnp.where(sub == 1, out[1], out[2]))
            vv[step + 1, x] = jnp.where(inside, image, 0.0)

    zero = jnp.zeros((8, NY), F32)
    tile = zero
    for k in range(6):
        high, low = zero, zero
        for x in range(nx):
            value, rest = two_product(vv[k // 2, x], vv[(k + 1) // 2, x])
            high, lost = two_sum(high, value)
            low = low + (lost + rest)
        value, lost = two_sum(high[0:1], high[1:2])
        value, more = two_sum(value, high[2:3])
        rest = (low[0:1] + low[1:2]) + (low[2:3] + (lost + more))
        owned = own[0:1]
        both = jnp.where(owned, value, 0.0) + rolled(jnp.where(owned, rest, 0.0), 8, 1)
        tile = jnp.where(sub == k, both, tile)
    hear(4, 2)
    hs[...] = tile

    sums = {}
    for k in sorted(range(1, ny), key=lambda k: (-min(k, ny - k), k)):
        sums[k] = copy(hs, hr.at[k - 1], hssem.at[k - 1], hrsem.at[k - 1], 0, k)
    for c in started:
        c.wait_send()
    rest = zero
    for k in sorted(range(1, ny), key=lambda k: (min(k, ny - k), k)):
        sums[k].wait_recv()
        tile, lost = two_sum(tile, hr[k - 1])
        rest = rest + lost
    for shift in (64, 32, 16, 8, 4, 2, 1):
        tile, lost = two_sum(tile, rolled(tile, shift, 1))
        rest = (rest + rolled(rest, shift, 1)) + lost
    tile, rest = quick_sum(tile, rest)

    moment = [(tile[k : k + 1], rest[k : k + 1]) for k in range(6)]
    answer = best_coefficients(moment, LAMBDA_PARTS)
    for k in range(1, ny):
        sums[k].wait_send()
    found = answer[0] * vv[0, p] + answer[1] * vv[1, p] + answer[2] * vv[2, p]
    for c in range(3):
        for z in range(EZ + 1):
            inc[c, z, 0:1, :] = found[c : c + 1, z * 16 + 4 : z * 16 + 4 + EYD]


def body(nx, ny, reference_image, deformed_image, route, within, xshift, fractions):
    vmem = pl.BlockSpec(memory_space=pltpu.VMEM)
    half = (NZ, EDGE, NY)
    tile = (8, NY)
    inc, mis = pl.pallas_call(
        lambda *refs: kernel(nx, ny, *refs),
        name="correlate",
        out_shape=(jax.ShapeDtypeStruct((3, EZ + 1, 1, EYD), F32), jax.ShapeDtypeStruct(half, F32)),
        in_specs=[pl.BlockSpec(memory_space=pltpu.HBM)] * 6,
        out_specs=(vmem, vmem),
        scratch_shapes=[
            pltpu.SMEM((1, 1, NEL), jnp.int32),
            pltpu.SMEM((1, 1, NEL), jnp.int32),
            pltpu.SMEM((1, 1, NEL), jnp.int32),
            pltpu.SMEM((1, 3, 1, NEL), jnp.int32),
            pltpu.VMEM(half, BF16),
            pltpu.VMEM(half, BF16),
            pltpu.SemaphoreType.DMA((6,)),
            pltpu.SemaphoreType.REGULAR((5,)),
            pltpu.VMEM((2,) + half, BF16),
            pltpu.VMEM(tile, jnp.int32),
            pltpu.VMEM((4,) + tile, jnp.int32),
            pltpu.VMEM((2, NZ, NY), BF16),
            pltpu.VMEM((2, NZ, NY), BF16),
            pltpu.VMEM((16, NZ * EDGE), BF16),
            pltpu.VMEM((2, 16, NZ * EDGE), BF16),
            pltpu.VMEM((3 * EZ * NY, ROUTES * NY), BF16),
            pltpu.VMEM((EDGE * EDGE, ROUTES * NY), F32),
            pltpu.VMEM((4, EDGE * EDGE, NY), BF16),
            pltpu.VMEM((ROUTES, EDGE * EDGE, NY), BF16),
            pltpu.VMEM((ROUTES * NY, EZ * NY), BF16),
            pltpu.VMEM((3,) + half, BF16),
            pltpu.VMEM((NZ + 2, 32, NY), F32),
            pltpu.VMEM((12 * 24, NY), F32),
            pltpu.VMEM((2, 6) + tile, F32),
            pltpu.VMEM((2, 6) + tile, F32),
            pltpu.VMEM((nx, 3 * HALF) + tile, F32),
            pltpu.VMEM((nx, 9) + tile, F32),
            pltpu.VMEM((nx, 9) + tile, F32),
            pltpu.VMEM((64, NY), F32),
            pltpu.VMEM((3, nx) + tile, F32),
            pltpu.VMEM((4, nx) + tile, F32),
            pltpu.VMEM(tile, F32),
            pltpu.VMEM((ny - 1,) + tile, F32),
            pltpu.SemaphoreType.DMA((A_END,)),
            pltpu.SemaphoreType.DMA((A_END,)),
            pltpu.SemaphoreType.DMA((nx - 1,)),
            pltpu.SemaphoreType.DMA((nx - 1,)),
            pltpu.SemaphoreType.DMA((3 * nx,)),
            pltpu.SemaphoreType.DMA((3 * nx,)),
            pltpu.SemaphoreType.DMA((ny - 1,)),
            pltpu.SemaphoreType.DMA((ny - 1,)),
        ],
        compiler_params=pltpu.CompilerParams(
            collective_id=0, has_side_effects=True, vmem_limit_bytes=48 << 20
        ),
    )(*[
        pltpu.with_memory_space_constraint(array, pltpu.HBM)
        for array in (
            route.reshape(1, 1, NEL), within, xshift, fractions.transpose(0, 3, 1, 2),
            reference_image, deformed_image,
        )
    ])
    return inc, mis


def solution(mesh):
    nx, ny = mesh.shape["gx"], mesh.shape["gy"]
    placed = (
        P(None, "gx", "gy"),
        P(None, "gx", "gy"),
        P("gx", "gy", None, None),
        P("gx", "gy", None),
        P("gx", "gy", None),
        P("gx", "gy", None, None),
    )
    return jax.shard_map(
        lambda *blocks: body(nx, ny, *blocks),
        mesh=mesh,
        in_specs=placed,
        out_specs=(P(None, None, "gx", "gy"), P(None, "gx", "gy")),
        check_vma=False,
    )
```

```python
import jax
import jax.numpy as jnp
import numpy as np
from jax import lax
from jax.experimental import pallas as pl
from jax.experimental.pallas import tpu as pltpu
from jax.sharding import PartitionSpec as P

EDGE = 16
EZ = 4
EYD = 8
SPAN = 2
ROUTES = 2 * SPAN + 1
NEL = 32
CAP = 8
VOL = 4096
NZ = 64
NY = 128
LAMBDA = 0.05
LAMBDA_PARTS = (float(np.float32(LAMBDA)), 0.0)
MESH = pl.DeviceIdType.MESH
F32 = jnp.float32
BF16 = jnp.bfloat16

N_TABLE, N_BLOCK, N_FACE_X, N_FACE_Y, N_PACK, N_EDGE = 4, 2, 2, 2, 4, 2
A_TABLE = 0
A_BLOCK = A_TABLE + N_TABLE
A_FACE_X = A_BLOCK + N_BLOCK
A_FACE_Y = A_FACE_X + N_FACE_X
A_PACK = A_FACE_Y + N_FACE_Y
A_EDGE = A_PACK + N_PACK
A_END = A_EDGE + N_EDGE

OTHER_ROUTES = (0, 4, 1, 3)
ARRIVAL = (2, 1, 3, 0, 4)
STEPS = ((0, 0), (0, 1), (1, -1), (1, 0), (1, 1))
HALF = len(STEPS)
PAIRS = ((0, 0), (1, 1), (2, 2), (0, 1), (0, 2), (1, 2))


def iota(shape, dim):
    return lax.broadcasted_iota(jnp.int32, shape, dim)


def flag(condition):
    return jnp.where(condition, jnp.float32(1.0), jnp.float32(0.0))


def rolled(value, shift, axis):
    size = value.shape[axis]
    shift = shift % size
    return value if shift == 0 else pltpu.roll(value, shift, axis)


def halves(value):
    high = value.astype(BF16)
    return high, (value - high.astype(F32)).astype(BF16)


def near_exact(left, right):
    a, b = halves(left), halves(right)
    total = jnp.dot(a[0], b[1], preferred_element_type=F32) + jnp.dot(a[1], b[0], preferred_element_type=F32)
    return total + jnp.dot(a[0], b[0], preferred_element_type=F32)


def two_sum(a, b):
    total = a + b
    part = total - a
    return total, (a - (total - part)) + (b - part)


def quick_sum(a, b):
    total = a + b
    return total, b - (total - a)


def cut_in_two(a):
    wide = a * 4097.0
    high = wide - (wide - a)
    return high, a - high


def two_product(a, b):
    value = a * b
    (ah, al), (bh, bl) = cut_in_two(a), cut_in_two(b)
    return value, ((ah * bh - value) + ah * bl + al * bh) + al * bl


def plus(a, b):
    high, low = two_sum(a[0], b[0])
    return quick_sum(high, low + a[1] + b[1])


def minus(a, b):
    return plus(a, (-b[0], -b[1]))


def times(a, b):
    high, low = two_product(a[0], b[0])
    return quick_sum(high, low + (a[0] * b[1] + a[1] * b[0]))


def inverse(pivot, scale):
    sound = pivot[0] > scale[0] * 1e-12
    safe = (jnp.where(sound, pivot[0], 1.0), jnp.where(sound, pivot[1], 0.0))
    guess = 1.0 / safe[0]
    zero = jnp.zeros_like(guess)
    left = minus((zero + 1.0, zero), times(safe, (guess, zero)))
    result = quick_sum(guess, guess * left[0])
    return jnp.where(sound, result[0], 0.0), jnp.where(sound, result[1], 0.0)


def best_coefficients(moment, weight):
    count = 3
    level = (jnp.full_like(moment[0][0], weight[0]), jnp.full_like(moment[0][0], weight[1]))
    shifted = [plus(moment[k + 1], times(level, moment[k])) for k in range(2 * count - 1)]
    matrix = [[shifted[i + j] for j in range(count)] for i in range(count)]
    right = moment[:count]
    scale = [matrix[i][i] for i in range(count)]
    pivots = []
    for i in range(count):
        sound = matrix[i][i][0] > scale[i][0] * 1e-12
        pivots.append(jnp.where(sound, 1.0 / jnp.where(sound, matrix[i][i][0], 1.0), 0.0))
        exact = inverse(matrix[i][i], scale[i]) if i + 1 < count else None
        for j in range(i + 1, count):
            ratio = times(matrix[i][j], exact)
            for k in range(j, count):
                matrix[j][k] = minus(matrix[j][k], times(ratio, matrix[i][k]))
            right[j] = minus(right[j], times(ratio, right[i]))
    answer = [None] * count
    for i in reversed(range(count)):
        value = right[i][0]
        for j in range(i + 1, count):
            value = value - matrix[i][j][0] * answer[j]
        answer[i] = value * pivots[i]
    return answer


def hats(position):
    upper = (position.astype(F32) + 0.5) / EDGE
    return 1.0 - upper, upper


def kernel(
    nx, ny, route_hbm, within_hbm, xshift_hbm, fractions_hbm, ref_hbm, dfm_hbm, inc, mis,
    route, within, xshift, fractions, ref, dfm, lsem, gossip,
    xb, tsend, trecv, fxs, fxr, fys, fyr, pmat, pacc, psend, precv, qmat, grad, refp, xrow, es, er, sg,
    kd, k1, rrow, rr, vv, hs, hr, ssem, rsem, gssem, grsem, rssem, rrsem, hssem, hrsem,
):
    p, q = lax.axis_index("gx"), lax.axis_index("gy")

    def at(dp, dq):
        return (lax.rem(p + dp + 2 * nx, nx), lax.rem(q + dq + 2 * ny, ny))

    def copy(src, dst, send_sem, recv_sem, dp, dq):
        c = pltpu.make_async_remote_copy(
            src_ref=src, dst_ref=dst, send_sem=send_sem, recv_sem=recv_sem,
            device_id=at(dp, dq), device_id_type=MESH,
        )
        c.start()
        return c

    started = []

    def send(number, src, dst, dp, dq):
        c = copy(src, dst, ssem.at[number], rsem.at[number], dp, dq)
        started.append(c)
        return c

    near = ((0, 2), (0, -2), (0, 1), (0, -1), (1, 0), (-1, 0))
    barrier = pltpu.get_barrier_semaphore()
    for dp, dq in near:
        pl.semaphore_signal(barrier, inc=1, device_id=at(dp, dq), device_id_type=MESH)
    loads = []
    for k, (src, dst) in enumerate((
        (route_hbm, route), (within_hbm, within), (xshift_hbm, xshift), (fractions_hbm, fractions),
        (ref_hbm, ref), (dfm_hbm, dfm),
    )):
        loads.append(pltpu.make_async_copy(src, dst, lsem.at[k]))
        loads[k].start()

    def tell(number, *places):
        for dp, dq in places:
            pl.semaphore_signal(gossip.at[number], inc=1, device_id=at(dp, dq), device_id_type=MESH)

    def hear(number, count):
        pl.semaphore_wait(gossip.at[number], count)

    lane, sub = iota((8, NY), 1), iota((8, NY), 0)
    block, inner = lane >> 4, lane & 15

    for c in loads[:3]:
        c.wait()
    routes = [route[0, 0, e] for e in range(NEL)]
    wanted = jnp.full((8, NY), -1, jnp.int32)
    count = jnp.zeros((8, NY), jnp.int32)
    for e in range(NEL):
        source = jnp.clip(p + xshift[0, 0, e] - 1, 0, nx - 1) - p + 1
        code = ((source * EZ + e // EYD) * EYD + within[0, 0, e]) * EDGE
        hit = sub == routes[e]
        wanted = jnp.where(hit & (count == block), inner + code, wanted)
        count = count + jnp.where(hit, 1, 0)
    tsend[...] = wanted

    loads[4].wait()
    refp[0] = jnp.zeros((32, NY), F32)
    refp[NZ + 1] = jnp.zeros((32, NY), F32)
    refp[1 : NZ + 1, 8:24, :] = ref[...].astype(F32)
    fxs[0] = refp[1 : NZ + 1, 8, :].astype(BF16)
    fxs[1] = refp[1 : NZ + 1, 23, :].astype(BF16)
    rows16, lanes16 = iota((16, NY), 0), iota((16, NY), 1)
    pick = ((rows16 == 0) & (lanes16 == 0)) | ((rows16 == 1) & (lanes16 == NY - 1))
    fys[...] = lax.dot_general(
        jnp.where(pick, 1.0, 0.0).astype(BF16), ref[...].reshape(NZ * EDGE, NY),
        (((1,), (1,)), ((), ())), preferred_element_type=F32,
    ).astype(BF16)

    pl.semaphore_wait(barrier, len(near))
    faces_y = [
        send(A_FACE_Y, fys, fyr.at[1], 0, -1),
        send(A_FACE_Y + 1, fys, fyr.at[0], 0, 1),
    ]
    tables = [
        send(A_TABLE + k, tsend, trecv.at[k], 0, r - SPAN) for k, r in enumerate(OTHER_ROUTES)
    ]
    faces_x = [
        send(A_FACE_X, fxs.at[0], fxr.at[1], -1, 0),
        send(A_FACE_X + 1, fxs.at[1], fxr.at[0], 1, 0),
    ]
    blocks = [send(A_BLOCK, dfm_hbm, xb.at[1], -1, 0), send(A_BLOCK + 1, dfm_hbm, xb.at[0], 1, 0)]

    loads[3].wait()
    element = sub * EYD + block
    own_route = jnp.zeros((8, NY), jnp.int32)
    parts = [jnp.zeros((8, NY), jnp.int32) for _ in range(3)]
    for e in range(NEL):
        here = element == e
        own_route = jnp.where(here, routes[e], own_route)
        parts = [jnp.where(here, fractions[0, c, 0, e], parts[c]) for c in range(3)]
    slot = jnp.zeros((8, NY), jnp.int32)
    for e in range(NEL):
        slot = slot + jnp.where((element > e) & (own_route == routes[e]), 1, 0)
    turn = jnp.zeros((8, NY), jnp.int32)
    for k, r in enumerate(ARRIVAL):
        turn = jnp.where(own_route == r, k, turn)
    first = (turn * CAP + slot) * EDGE
    portion = [part.astype(F32) / EDGE for part in parts]
    target0 = first + inner
    target1 = first + jnp.minimum(inner + 1, EDGE - 1)

    for z in range(EZ):
        def fill_place(b, _):
            row = b * NY + iota((NY, NY), 0)
            high = portion[2][z : z + 1]
            place = jnp.where(row == target0[z : z + 1], 1.0 - high, 0.0)
            place = place + jnp.where(row == target1[z : z + 1], high, 0.0)
            qmat[pl.ds(pl.multiple_of(b * NY, NY), NY), z * NY : (z + 1) * NY] = place.astype(BF16)
            return 0

        lax.fori_loop(0, ROUTES, fill_place, 0)

    for c in faces_x:
        c.wait_recv()
    tell(0, (1, 0), (-1, 0))
    for c in faces_y:
        c.wait_recv()
    refp[1 : NZ + 1, 7, :] = fxr[0].astype(F32) * flag(p > 0)
    refp[1 : NZ + 1, 24, :] = fxr[1].astype(F32) * flag(p < nx - 1)
    here, there = iota((NY, NY), 1), iota((NY, NY), 0)
    differ = jnp.where(there == here + 1, 0.5, jnp.where(there == here - 1, -0.5, 0.0)).astype(BF16)
    rows32, lanes32 = iota((32, NY), 0), iota((32, NY), 1)
    ends = jnp.where(
        (rows32 == 1) & (lanes32 == 0), flag(q > 0) * -0.5,
        jnp.where((rows32 == 16) & (lanes32 == NY - 1), flag(q < ny - 1) * 0.5, 0.0),
    ).astype(BF16)
    sides = jnp.concatenate([fyr[0], fyr[1]], axis=0)
    along_y = jnp.dot(ref[...].reshape(NZ * EDGE, NY), differ, preferred_element_type=F32)
    along_y = along_y + lax.dot_general(sides, ends, (((0,), (0,)), ((), ())), preferred_element_type=F32)
    grad[2] = along_y.astype(BF16).reshape(NZ, EDGE, NY)

    def slope(b, _):
        base = b * 4
        below, above = refp[pl.ds(base, 4), 8:24, :], refp[pl.ds(base + 2, 4), 8:24, :]
        grad[0, pl.ds(base, 4)] = ((above - below) * 0.5).astype(BF16)
        left, right = refp[pl.ds(base + 1, 4), 7:23, :], refp[pl.ds(base + 1, 4), 9:25, :]
        grad[1, pl.ds(base, 4)] = ((right - left) * 0.5).astype(BF16)
        return 0

    lax.fori_loop(0, NZ // 4, slope, 0)

    rowm, colm = iota((24, 96), 0), iota((24, 96), 1)
    low_x, high_x = hats(colm & 15)
    order = rowm >> 3
    weight_x = jnp.where(order == 0, low_x * low_x, jnp.where(order == 1, low_x * high_x, high_x * high_x))
    weight_x = jnp.where((rowm & 7) == (colm >> 4), weight_x, 0.0)
    weights_x = jnp.concatenate(halves(weight_x), axis=0)

    def moments(z, _):
        total = [[None] * 6 for _ in range(3)]
        for i in range(EDGE):
            g = [grad[c, z * EDGE + i].astype(F32) for c in range(3)]
            high = (i + 0.5) / EDGE
            low = 1.0 - high
            for k, (a, b) in enumerate(PAIRS):
                product = g[a] * g[b]
                for m, weight in enumerate((low * low, low * high, high * high)):
                    term = product * weight
                    total[m][k] = term if i == 0 else total[m][k] + term
        for m in range(3):
            parts = [
                jnp.dot(weights_x, part, preferred_element_type=F32)
                for part in halves(jnp.concatenate(total[m], axis=0))
            ]
            rows = (parts[1][:24] + parts[0][24:]) + parts[0][:24]
            xrow[pl.ds(pl.multiple_of((z * 3 + m) * 24, 24), 24), :] = rows
        return 0

    lax.fori_loop(0, EZ, moments, 0)
    fine, coarse = iota((NY, 3 * NY), 0), iota((NY, 3 * NY), 1)
    low_y, high_y = hats(fine & 15)
    row_y, node_y, step_y = fine >> 4, (coarse & 15) - 4, (coarse >> 7) - 1
    starts, closes = row_y == node_y, row_y + 1 == node_y
    mixed = low_y * high_y
    weight_y = jnp.where(
        step_y == 1, jnp.where(starts, mixed, 0.0),
        jnp.where(
            step_y == -1, jnp.where(closes, mixed, 0.0),
            jnp.where(starts, low_y * low_y, 0.0) + jnp.where(closes, high_y * high_y, 0.0),
        ),
    ) * (1.0 / VOL)
    yrow = near_exact(xrow[...], weight_y)
    on = [block == z for z in range(EZ + 1)]
    mine = [[None] * HALF for _ in range(3)]
    for m in range(3):
        for k, (dz, dy) in enumerate(STEPS):
            def term(z, depth):
                start = (z * 3 + depth) * 24 + m * 8
                return yrow[start : start + 8, (dy + 1) * NY : (dy + 2) * NY]

            total = jnp.zeros((8, NY), F32)
            for z in range(EZ):
                if dz == 1:
                    total = jnp.where(on[z], term(z, 1), total)
                else:
                    total = total + jnp.where(on[z], term(z, 0), 0.0) + jnp.where(on[z + 1], term(z, 2), 0.0)
            mine[m][k] = total
    for m in range(3):
        for part, ks in enumerate(((0, 1, 2), (3, 4))):
            upper, lower = jnp.zeros((8, NY), F32), jnp.zeros((8, NY), F32)
            for k in ks:
                offset = 5 * (k % 3)
                spot = (inner >= offset) & (inner < offset + 5)
                upper = jnp.where(spot, rolled(mine[m][k], offset - 8, 1), upper)
                lower = jnp.where(spot, rolled(mine[m][k], offset - 4, 1), lower)
            es[0, m * 2 + part], es[1, m * 2 + part] = upper, lower
    edges = [send(A_EDGE, es.at[0], er.at[0], 0, 1), send(A_EDGE + 1, es.at[1], er.at[1], 0, -1)]
    for c in tables:
        c.wait_recv()
    tell(3, (0, 4), (0, -4))
    asked = []
    for r in range(ROUTES):
        if r == SPAN:
            asked.append(wanted[r : r + 1])
        else:
            k = OTHER_ROUTES.index(r)
            asked.append(trecv[k, r : r + 1, :])
    asked = jnp.concatenate(asked, axis=1)

    def fill_pack(b, _):
        row = b * NY + iota((NY, ROUTES * NY), 0)
        pmat[pl.ds(pl.multiple_of(b * NY, NY), NY), :] = jnp.where(row == asked, 1.0, 0.0).astype(BF16)
        return 0

    lax.fori_loop(0, 3 * EZ, fill_pack, 0)

    def brick_rows(source):
        return jnp.concatenate(
            [source[z * EDGE : (z + 1) * EDGE].reshape(EDGE * EDGE, NY) for z in range(EZ)], axis=1
        )

    width = EZ * NY
    loads[5].wait()
    pacc[...] = jnp.dot(brick_rows(dfm), pmat[width : 2 * width, :], preferred_element_type=F32)

    hear(0, 2)
    tell(1, (1, 0), (-1, 0))
    blocks[1].wait_recv()
    pacc[...] += jnp.dot(brick_rows(xb[0]), pmat[0:width, :], preferred_element_type=F32)
    blocks[0].wait_recv()
    last = brick_rows(xb[1])

    def packed(r):
        part = jnp.dot(last, pmat[2 * width : 3 * width, r * NY : (r + 1) * NY], preferred_element_type=F32)
        return (pacc[:, r * NY : (r + 1) * NY] + part).astype(BF16)

    packs = []
    for k, r in enumerate(OTHER_ROUTES):
        psend[k] = packed(r)
        packs.append(send(A_PACK + k, psend.at[k], precv.at[r], 0, SPAN - r))
    precv[SPAN] = packed(SPAN)
    hear(1, 2)
    tell(2, (1, 0), (-1, 0))

    for c in edges:
        c.wait_recv()
    for m in range(3):
        for k in range(HALF):
            offset, part = 5 * (k % 3), k // 3
            below = jnp.where(inner < 5, rolled(er[0, m * 2 + part], -offset, 1), 0.0) * flag(q > 0)
            above = jnp.where(inner >= 12, rolled(er[1, m * 2 + part], 12 - offset, 1), 0.0) * flag(q < ny - 1)
            sg[p, m * HALF + k] = mine[m][k] + below + above
    spread = []
    for k in sorted(range(1, nx), key=lambda k: (-min(k, nx - k), k)):
        spread.append(copy(sg.at[p], sg.at[p], gssem.at[k - 1], grsem.at[k - 1], k, 0))
    started.extend(spread)

    hear(3, 2)
    tell(4, (0, 8), (0, -8))

    column = inner - 4
    own = (column >= 0) & (column < EYD) & (block <= EZ) & (sub < 3)
    inside = (q * EYD + column < ny * EYD) & (sub < 3)
    pacc[:, : EZ * NY] = jnp.dot(precv[SPAN], qmat[0:NY, :], preferred_element_type=F32)

    def placed(at, pair):
        for r in pair:
            packs[OTHER_ROUTES.index(r)].wait_recv()
        bricks = jnp.concatenate([precv[r] for r in pair], axis=1)
        return jnp.dot(bricks, qmat[at * NY : (at + 2) * NY, :], preferred_element_type=F32)

    pacc[:, : EZ * NY] += placed(1, ARRIVAL[1:3])
    fetched = pacc[:, : EZ * NY] + placed(3, ARRIVAL[3:5])
    row8, col16 = iota((8, EDGE), 0), iota((8, EDGE), 1)
    low_j, high_j = hats(iota((EDGE, 1), 0))
    for z in range(EZ):
        voxels = fetched[:, z * NY : (z + 1) * NY].reshape(EDGE, EDGE, NY)
        high = portion[1][z : z + 1].reshape(1, 1, NY)
        ahead = jnp.concatenate([voxels[:, 1:], voxels[:, EDGE - 1 :]], axis=1)
        voxels = (1.0 - high) * voxels + high * ahead
        high = portion[0][z : z + 1].reshape(1, 1, NY)
        ahead = jnp.concatenate([voxels[1:], voxels[EDGE - 1 :]], axis=0)
        voxels = (1.0 - high) * voxels + high * ahead
        left = refp[1 + z * EDGE : 1 + (z + 1) * EDGE, 8:24, :] - voxels
        mis[z * EDGE : (z + 1) * EDGE] = left
        sums = [[None] * 3 for _ in range(2)]
        for i in range(EDGE):
            high = (i + 0.5) / EDGE
            for c in range(3):
                value = grad[c, z * EDGE + i].astype(F32) * left[i]
                for m, weight in enumerate((1.0 - high, high)):
                    sums[m][c] = value * weight if i == 0 else sums[m][c] + value * weight
        for m in range(2):
            rows = [jnp.sum(sums[m][c] * w, axis=0, keepdims=True) for w in (low_j, high_j) for c in range(3)]
            blank = jnp.zeros((1, NY), F32)
            start = (z * 2 + m) * 8
            rrow[start : start + 8, :] = jnp.concatenate(rows[:3] + [blank] + rows[3:] + [blank], axis=0)
    fine, coarse = iota((NY, NY), 0), iota((NY, NY), 1)
    low_y, high_y = hats(fine & 15)
    row_y, node_y = fine >> 4, (coarse & 15) - 4
    weight_y = (
        jnp.where(row_y == node_y, low_y, 0.0) + jnp.where(row_y + 1 == node_y, high_y, 0.0)
    ) * (1.0 / VOL)
    weight_y = weight_y.astype(BF16)
    high, low = halves(rrow[...])
    nodes = jnp.dot(low, weight_y, preferred_element_type=F32) + jnp.dot(high, weight_y, preferred_element_type=F32)
    tile = jnp.zeros((8, NY), F32)
    for z in range(EZ):
        for m in range(2):
            start = (z * 2 + m) * 8
            tile = tile + jnp.where(on[z + m], nodes[start : start + 8], 0.0)
    rr[1, p] = tile
    hear(2, 2)
    sent = []
    for k in sorted(range(nx), key=lambda k: (-min(k, nx - k), k)):
        for dq in (1, -1, 0):
            if k or dq:
                number = k * 3 + 1 - dq
                sent.append(copy(rr.at[1, p], rr.at[1 - dq, p], rssem.at[number], rrsem.at[number], k, dq))
    started.extend(sent)

    for c in spread:
        c.wait_recv()
    for x in range(nx):
        for k, (dz, dy) in enumerate(STEPS):
            level, cross = sg[x, k], sg[x, HALF + k]
            if x > 0:
                level = level + sg[x - 1, 2 * HALF + k]
            kd[x, 4 + k], k1[x, 4 + k] = level, cross
            if k:
                shift = dz * 16 + dy
                kd[x, 4 - k], k1[x, 4 - k] = rolled(level, shift, 1), rolled(cross, shift, 1)

    for c in sent:
        c.wait_recv()
    below, above = flag(q > 0), flag(q < ny - 1)
    tiles = []
    for x in range(nx):
        from_below = jnp.where(inner < 8, rolled(rr[0, x], -8, 1), 0.0) * below
        from_above = jnp.where(inner >= 8, rolled(rr[2, x], 8, 1), 0.0) * above
        tiles.append(rr[1, x] + from_below + from_above)
    for x in range(nx):
        whole = tiles[x] + rolled(tiles[x - 1], 4, 0) if x else tiles[x]
        vv[0, x] = jnp.where(inside, whole, 0.0)

    for step in range(3):
        straight = [jnp.zeros((8, NY), F32) for _ in range(nx)]
        crossed = [jnp.zeros((8, NY), F32) for _ in range(nx)]
        for x in range(nx):
            u = [vv[step, x, c : c + 1, :] for c in range(3)]
            second = jnp.where(sub == 0, u[0], jnp.where((sub == 1) | (sub == 3), u[1], u[2]))
            third = jnp.where(sub == 5, u[1], u[0])
            for t in range(9):
                shift = -((t // 3 - 1) * 16 + t % 3 - 1)
                moved, other = rolled(second, shift, 1), rolled(third, shift, 1)
                level, cross = kd[x, t], k1[x, t]
                straight[x] = straight[x] + level * moved
                crossed[x] = crossed[x] + level * other
                if x + 1 < nx:
                    straight[x + 1] = straight[x + 1] + cross * moved
                    crossed[x + 1] = crossed[x + 1] + cross * other
                if x > 0:
                    before = k1[x - 1, t]
                    straight[x - 1] = straight[x - 1] + before * moved
                    crossed[x - 1] = crossed[x - 1] + before * other
        for x in range(nx):
            a, b = straight[x], crossed[x]
            out = [
                a[0:1] + a[3:4] + a[4:5],
                a[1:2] + a[5:6] + b[3:4],
                a[2:3] + b[4:5] + b[5:6],
            ]
            image = jnp.where(sub == 0, out[0], jnp.where(sub == 1, out[1], out[2]))
            vv[step + 1, x] = jnp.where(inside, image, 0.0)

    zero = jnp.zeros((8, NY), F32)
    tile = zero
    for k in range(6):
        high, low = zero, zero
        for x in range(nx):
            value, rest = two_product(vv[k // 2, x], vv[(k + 1) // 2, x])
            high, lost = two_sum(high, value)
            low = low + (lost + rest)
        value, lost = two_sum(high[0:1], high[1:2])
        value, more = two_sum(value, high[2:3])
        rest = (low[0:1] + low[1:2]) + (low[2:3] + (lost + more))
        owned = own[0:1]
        both = jnp.where(owned, value, 0.0) + rolled(jnp.where(owned, rest, 0.0), 8, 1)
        tile = jnp.where(sub == k, both, tile)
    hear(4, 2)
    hs[...] = tile

    sums = {}
    for k in sorted(range(1, ny), key=lambda k: (-min(k, ny - k), k)):
        sums[k] = copy(hs, hr.at[k - 1], hssem.at[k - 1], hrsem.at[k - 1], 0, k)
    for c in started:
        c.wait_send()
    rest = zero
    for k in sorted(range(1, ny), key=lambda k: (min(k, ny - k), k)):
        sums[k].wait_recv()
        tile, lost = two_sum(tile, hr[k - 1])
        rest = rest + lost
    for shift in (64, 32, 16, 8, 4, 2, 1):
        tile, lost = two_sum(tile, rolled(tile, shift, 1))
        rest = (rest + rolled(rest, shift, 1)) + lost
    tile, rest = quick_sum(tile, rest)

    moment = [(tile[k : k + 1], rest[k : k + 1]) for k in range(6)]
    answer = best_coefficients(moment, LAMBDA_PARTS)
    for k in range(1, ny):
        sums[k].wait_send()
    found = answer[0] * vv[0, p] + answer[1] * vv[1, p] + answer[2] * vv[2, p]
    for c in range(3):
        for z in range(EZ + 1):
            inc[c, z, 0:1, :] = found[c : c + 1, z * 16 + 4 : z * 16 + 4 + EYD]


def body(nx, ny, reference_image, deformed_image, route, within, xshift, fractions):
    vmem = pl.BlockSpec(memory_space=pltpu.VMEM)
    half = (NZ, EDGE, NY)
    tile = (8, NY)
    inc, mis = pl.pallas_call(
        lambda *refs: kernel(nx, ny, *refs),
        name="correlate",
        out_shape=(jax.ShapeDtypeStruct((3, EZ + 1, 1, EYD), F32), jax.ShapeDtypeStruct(half, F32)),
        in_specs=[pl.BlockSpec(memory_space=pltpu.HBM)] * 6,
        out_specs=(vmem, vmem),
        scratch_shapes=[
            pltpu.SMEM((1, 1, NEL), jnp.int32),
            pltpu.SMEM((1, 1, NEL), jnp.int32),
            pltpu.SMEM((1, 1, NEL), jnp.int32),
            pltpu.SMEM((1, 3, 1, NEL), jnp.int32),
            pltpu.VMEM(half, BF16),
            pltpu.VMEM(half, BF16),
            pltpu.SemaphoreType.DMA((6,)),
            pltpu.SemaphoreType.REGULAR((5,)),
            pltpu.VMEM((2,) + half, BF16),
            pltpu.VMEM(tile, jnp.int32),
            pltpu.VMEM((4,) + tile, jnp.int32),
            pltpu.VMEM((2, NZ, NY), BF16),
            pltpu.VMEM((2, NZ, NY), BF16),
            pltpu.VMEM((16, NZ * EDGE), BF16),
            pltpu.VMEM((2, 16, NZ * EDGE), BF16),
            pltpu.VMEM((3 * EZ * NY, ROUTES * NY), BF16),
            pltpu.VMEM((EDGE * EDGE, ROUTES * NY), F32),
            pltpu.VMEM((4, EDGE * EDGE, NY), BF16),
            pltpu.VMEM((ROUTES, EDGE * EDGE, NY), BF16),
            pltpu.VMEM((ROUTES * NY, EZ * NY), BF16),
            pltpu.VMEM((3,) + half, BF16),
            pltpu.VMEM((NZ + 2, 32, NY), F32),
            pltpu.VMEM((12 * 24, NY), F32),
            pltpu.VMEM((2, 6) + tile, F32),
            pltpu.VMEM((2, 6) + tile, F32),
            pltpu.VMEM((nx, 3 * HALF) + tile, F32),
            pltpu.VMEM((nx, 9) + tile, F32),
            pltpu.VMEM((nx, 9) + tile, F32),
            pltpu.VMEM((64, NY), F32),
            pltpu.VMEM((3, nx) + tile, F32),
            pltpu.VMEM((4, nx) + tile, F32),
            pltpu.VMEM(tile, F32),
            pltpu.VMEM((ny - 1,) + tile, F32),
            pltpu.SemaphoreType.DMA((A_END,)),
            pltpu.SemaphoreType.DMA((A_END,)),
            pltpu.SemaphoreType.DMA((nx - 1,)),
            pltpu.SemaphoreType.DMA((nx - 1,)),
            pltpu.SemaphoreType.DMA((3 * nx,)),
            pltpu.SemaphoreType.DMA((3 * nx,)),
            pltpu.SemaphoreType.DMA((ny - 1,)),
            pltpu.SemaphoreType.DMA((ny - 1,)),
        ],
        compiler_params=pltpu.CompilerParams(
            collective_id=0, has_side_effects=True, vmem_limit_bytes=48 << 20
        ),
    )(*[
        pltpu.with_memory_space_constraint(array, pltpu.HBM)
        for array in (
            route.reshape(1, 1, NEL), within, xshift, fractions.transpose(0, 3, 1, 2),
            reference_image, deformed_image,
        )
    ])
    return inc, mis


def solution(mesh):
    nx, ny = mesh.shape["gx"], mesh.shape["gy"]
    placed = (
        P(None, "gx", "gy"),
        P(None, "gx", "gy"),
        P("gx", "gy", None, None),
        P("gx", "gy", None),
        P("gx", "gy", None),
        P("gx", "gy", None, None),
    )
    return jax.shard_map(
        lambda *blocks: body(nx, ny, *blocks),
        mesh=mesh,
        in_specs=placed,
        out_specs=(P(None, None, "gx", "gy"), P(None, "gx", "gy")),
        check_vma=False,
    )
```
